32 devices in a mesh: seq: 16 (over z, y, x), feat: 2 (over core).
Axes of the slice: x: 2, y: 2, z: 4, core: 2. Of those that a mesh axis runs over, the one named last changes fastest.
Arguments:
- layer_input: bfloat16 [16384, 768], P(('seq', 'feat')), may hold values from -6 to 6
- ln1_gain: bfloat16 [768], replicated, may hold values from 0.25 to 1.75
- ln1_bias: bfloat16 [768], replicated, may hold values from -1.75 to 1.75
- w_qkv: bfloat16 [768, 2304], replicated, may hold values from -0.21875 to 0.21875
- b_qkv: bfloat16 [2304], replicated, may hold values from -1.75 to 1.75
- w_out: bfloat16 [768, 768], replicated, may hold values from -0.875 to 0.875
- b_out: bfloat16 [768], replicated, may hold values from -1.75 to 1.75
- ln2_gain: bfloat16 [768], replicated, may hold values from 0.25 to 1.75
- ln2_bias: bfloat16 [768], replicated, may hold values from -1.75 to 1.75
- w_up: bfloat16 [768, 3072], P(None, 'feat'), may hold values from -0.21875 to 0.21875
- b_up: bfloat16 [3072], P('feat'), may hold values from -1.75 to 1.75
- w_down: bfloat16 [3072, 768], P('feat'), may hold values from -0.109375 to 0.109375
- b_down: bfloat16 [768], replicated, may hold values from -1.75 to 1.75
- feature_signs: int32 [12, 64, 256], P(None, None, 'feat'), may hold values from 0 to 1
- match_blocks: int32 [16, 12, 16, 4], P('seq'), may hold values from 0 to 15, as said below
- match_count: int32 [16, 12, 16], P('seq'), may hold values from 1 to 4, as said below
- out_grad: bfloat16 [16384, 768], P(('seq', 'feat')), may hold values from -12 to 12
Outputs:
- layer_output: bfloat16 [16384, 768], P(('seq', 'feat'))
- d_input: float32 [16384, 768], P(('seq', 'feat'))
- d_ln1_gain: float32 [768], P(('seq', 'feat'))
- d_ln1_bias: float32 [768], P(('seq', 'feat'))
- d_w_qkv: float32 [768, 2304], P(('seq', 'feat'))
- d_b_qkv: float32 [2304], P(('seq', 'feat'))
- d_w_out: float32 [768, 768], P(('seq', 'feat'))
- d_b_out: float32 [768], P(('seq', 'feat'))
- d_ln2_gain: float32 [768], P(('seq', 'feat'))
- d_ln2_bias: float32 [768], P(('seq', 'feat'))
- d_w_up: float32 [768, 3072], P('seq', 'feat')
- d_b_up: float32 [3072], P(('feat', 'seq'))
- d_w_down: float32 [3072, 768], P('feat', 'seq')
- d_b_down: float32 [768], P(('seq', 'feat'))
The draws below stay inside these ranges and needn't reach their ends.
Inputs may be any that keep to these rules, and one draw needn't show every extreme that they name: `match_blocks`: each list names distinct key blocks of the query block's own sequence; entries from match_count on are not used. `match_count`: some list holds 4 used entries in every draw.
All inputs are finite; a program needn't handle non-finite values.
Results may differ from the reference program's by a relative error of at most 0.025.
Values may be sent and summed in bfloat16 or wider, within the bound.
A program may use at most 192 MiB of HBM per device.

```python
import jax
import jax.numpy as jnp
from jax import lax

D = 768
HEADS = 12
HEAD_DIM = 64
FF = 3072
FEATS = 256
BLOCK = 64
MATCH = 4
SEQLEN = 1024
NB = 16
SEQS = 16
TOKENS = 16384


def draw_match_blocks(key, part):
    list_key = jax.random.fold_in(key, 11)
    scores = jax.random.randint(list_key, (SEQS, HEADS, NB, NB), 0, 1 << 20)
    scores = scores * NB + jnp.arange(NB, dtype=jnp.int32)
    order = jnp.argsort(scores, axis=-1)
    return order[..., :MATCH].astype(jnp.int32)


def draw_match_count(key, part):
    hot_key = jax.random.fold_in(key, 21)
    heavy_key = jax.random.fold_in(key, 22)
    light_key = jax.random.fold_in(key, 23)
    hot_block = jax.random.randint(hot_key, (SEQS, 1, NB), 0, 4) == 0
    heavy = MATCH - jax.random.randint(heavy_key, (SEQS, HEADS, NB), 0, 2)
    light = jnp.minimum(jax.random.randint(light_key, (SEQS, HEADS, NB), 1, 3), MATCH)
    counts = jnp.where(hot_block, heavy, light)
    counts = counts.at[0, 0, 0].set(MATCH)
    return counts.astype(jnp.int32)


def plant(values, rng, least, high):
    shape = values.shape
    index_at = [jax.random.randint(jax.random.fold_in(rng, axis), (), 0, shape[axis]) for axis in range(len(shape))]
    values = values.at[tuple(index_at)].set(least)
    longest = shape.index(max(shape))
    index_at[longest] = (index_at[longest] + 1) % shape[longest]
    return values.at[tuple(index_at)].set(high)


def raised(values, stream_key, source, target, parts, factor):
    def block_of(dim):
        return (jnp.arange(values.shape[dim]) // (values.shape[dim] // parts)).reshape((-1,) + (1,) * (values.ndim - 1 - dim))

    first = jax.random.permutation(stream_key, parts)[block_of(target)]
    other_side = (block_of(target) + parts // 2) % parts
    return jnp.where((block_of(source) == first) | (block_of(source) == other_side), factor * values, values)


def shard_levels(own_key, dims, cuts, low, high):
    def one(dim, blocks):
        steps = jax.random.uniform(jax.random.fold_in(jax.random.fold_in(own_key, 6), dim), (blocks,), jnp.float32, low / len(cuts), high / len(cuts))
        return jnp.repeat(jnp.exp(steps), dims[dim] // blocks).reshape((-1,) + (1,) * (len(dims) - dim - 1))

    level = one(*cuts[0])
    for cut in cuts[1:]:
        level = level * one(*cut)
    return level


def centred(own_key, extent, deviation, reach, cuts=(), kind=jnp.bfloat16):
    array = jax.random.normal(own_key, extent, jnp.float32) * deviation
    if len(cuts) > 0:
        array = shard_levels(own_key, extent, cuts, -0.22, 0.18) * array
    return jnp.clip(array, min=-reach, max=reach).astype(kind)


def gaussian_with(stream_key, dims, deviation, limit, cuts, heavy, kind=jnp.bfloat16):
    values = deviation * jax.random.normal(stream_key, dims, jnp.float32)
    if cuts:
        values = values * shard_levels(stream_key, dims, cuts, -0.22, 0.18)
    return jnp.clip(raised(values, jax.random.fold_in(stream_key, 3), *heavy), -limit, limit).astype(kind)


def setup_inputs(seed: int = 0) -> dict:
    seeds = jax.random.split(jax.random.key(seed), 18)
    return {
        "layer_input": centred(seeds[0], (TOKENS, D), 1.0, 6.0, ((0, 32),)),
        "ln1_gain": jnp.clip(1.0 + 0.15 * jax.random.normal(seeds[1], (D,), jnp.float32), 0.25, 1.75).astype(jnp.bfloat16),
        "ln1_bias": centred(seeds[2], (D,), 0.3, 1.75),
        "w_qkv": centred(seeds[3], (D, 3 * D), D ** -0.5, 0.21875),
        "b_qkv": centred(seeds[4], (3 * D,), 0.3, 1.75),
        "w_out": centred(seeds[5], (D, D), (D // 16) ** -0.5, 0.875),
        "b_out": centred(seeds[6], (D,), 0.3, 1.75),
        "ln2_gain": jnp.clip(1.0 + 0.15 * jax.random.normal(seeds[7], (D,), jnp.float32), 0.25, 1.75).astype(jnp.bfloat16),
        "ln2_bias": centred(seeds[8], (D,), 0.3, 1.75),
        "w_up": centred(seeds[9], (D, FF), D ** -0.5, 0.21875, ((1, 2),)),
        "b_up": centred(seeds[10], (FF,), 0.3, 1.75, ((0, 2),)),
        "w_down": centred(seeds[11], (FF, D), FF ** -0.5, 0.109375, ((0, 2),)),
        "b_down": centred(seeds[12], (D,), 0.3, 1.75),
        "feature_signs": plant(jax.random.randint(seeds[13], (HEADS, HEAD_DIM, FEATS), 0, 2), jax.random.fold_in(seeds[13], 1), 0, 1).astype(jnp.int32),
        "match_blocks": draw_match_blocks(jax.random.fold_in(seeds[17], 71), 0),
        "match_count": draw_match_count(jax.random.fold_in(seeds[17], 71), 0),
        "out_grad": gaussian_with(seeds[16], (TOKENS, D), 1.0, 12.0, ((0, 32),), (0, 1, 32, 2.75)),
    }


@jax.custom_vjp
def low(v):
    return lax.optimization_barrier(v.astype(jnp.bfloat16)).astype(jnp.float32)

@jax.custom_vjp
def low_back(v):
    return v

def low_keep(v):
    return (low(v), None)

def low_pass(kept, grad):
    return (grad,)

def back_keep(v):
    return (v, None)

def back_low(kept, grad):
    return (low(grad),)
low.defvjp(low_keep, low_pass)
low_back.defvjp(back_keep, back_low)
exact_mode = lax.Precision.HIGHEST
norm_epsilon = 1e-05

def matmul_exact(left, right):
    return jnp.dot(left, right, precision=exact_mode, preferred_element_type=jnp.float32)

def layer_norm(values, gain, shift):
    center = values - lax.optimization_barrier(jnp.mean(values, axis=-1, keepdims=True))
    spread = lax.optimization_barrier(jnp.mean(center * center, axis=-1, keepdims=True))
    return center * lax.rsqrt(spread + norm_epsilon) * gain + shift

def features(tokens, sign_table):
    lifted = low_back(jnp.einsum('slhd,hdf->slhf', tokens, sign_table, precision=exact_mode) * HEAD_DIM ** (-0.25))
    square = lax.optimization_barrier(jnp.sum(tokens * tokens, axis=-1, keepdims=True)) * (0.5 * HEAD_DIM ** (-0.5))
    return low(jnp.exp(lifted - square) * FEATS ** (-0.5))

def attend(queries, key_rows, value_rows, sign_table, match_lists, match_counts):
    seq_count = queries.shape[0]
    nblocks = SEQLEN // BLOCK
    split = (seq_count, nblocks, BLOCK, HEADS)
    q_blocks = features(queries, sign_table).reshape(split + (FEATS,))
    k_feats = features(key_rows, sign_table).reshape(split + (FEATS,))
    v_blocks = value_rows.reshape(split + (HEAD_DIM,))
    key_state = low_back(jnp.einsum('snkhf,snkhd->snhfd', k_feats, v_blocks, precision=exact_mode))
    key_sum = lax.optimization_barrier(jnp.sum(k_feats, axis=2))
    in_use = (jnp.arange(MATCH, dtype=jnp.int32) < match_counts[..., None]).astype(jnp.float32)
    matched = lax.optimization_barrier(jnp.sum(in_use[..., None] * (match_lists[..., None] == jnp.arange(nblocks, dtype=jnp.int32)).astype(jnp.float32), axis=3))
    unmatched = 1.0 - matched
    low_state = low(jnp.einsum('shbm,smhfd->sbhfd', unmatched, key_state, precision=exact_mode))
    low_sum = low(jnp.einsum('shbm,smhf->sbhf', unmatched, key_sum, precision=exact_mode))
    numerator = jnp.einsum('sbqhf,sbhfd->sbqhd', q_blocks, low_state, precision=exact_mode)
    denominator = jnp.einsum('sbqhf,sbhf->sbqh', q_blocks, low_sum, precision=exact_mode)
    key_table = key_rows.reshape(split + (HEAD_DIM,)).transpose(0, 3, 1, 2, 4).reshape(seq_count * HEADS * nblocks, BLOCK, HEAD_DIM)
    value_table = value_rows.reshape(split + (HEAD_DIM,)).transpose(0, 3, 1, 2, 4).reshape(seq_count * HEADS * nblocks, BLOCK, HEAD_DIM)
    seq_iota = jnp.arange(seq_count, dtype=jnp.int32)[:, None, None, None]
    head_iota = jnp.arange(HEADS, dtype=jnp.int32)[None, :, None, None]
    flat_index = ((seq_iota * HEADS + head_iota) * nblocks + match_lists).astype(jnp.int32)
    key_pick = key_table[flat_index]
    value_pick = value_table[flat_index]
    query_blocks = queries.reshape(split + (HEAD_DIM,)).transpose(0, 3, 1, 2, 4)
    scores = low_back(jnp.einsum('shbqd,shbjkd->shbjqk', query_blocks, key_pick, precision=exact_mode) * HEAD_DIM ** (-0.5))
    exact_probs = low(jnp.exp(scores)) * in_use[..., None, None]
    exact_num = jnp.einsum('shbjqk,shbjkd->shbqd', exact_probs, value_pick, precision=exact_mode)
    exact_den = lax.optimization_barrier(jnp.sum(exact_probs, axis=(3, 5)))
    numerator = low_back(numerator + exact_num.transpose(0, 2, 3, 1, 4))
    denominator = low_back(denominator + exact_den.transpose(0, 2, 3, 1))
    return (numerator / denominator[..., None]).reshape(seq_count * SEQLEN, HEADS * HEAD_DIM)

def layer_group(inputs, match_lists, match_counts, gain_one, bias_one, w_qkv, b_qkv, w_out, b_out, gain_two, bias_two, w_up, b_up, w_down, b_down, sign_table):
    h_one = low(layer_norm(inputs, gain_one, bias_one))
    qkv = low(low_back(matmul_exact(h_one, w_qkv) + b_qkv))
    seq_count = match_lists.shape[0]
    head_shape = (seq_count, SEQLEN, HEADS, HEAD_DIM)
    queries = qkv[:, :D].reshape(head_shape)
    key_rows = qkv[:, D:2 * D].reshape(head_shape)
    value_rows = qkv[:, 2 * D:].reshape(head_shape)
    attended = low(attend(queries, key_rows, value_rows, sign_table, match_lists, match_counts))
    mixed = inputs + low_back(matmul_exact(attended, w_out) + b_out)
    h_two = low(layer_norm(mixed, gain_two, bias_two))
    pre_act = low_back(matmul_exact(h_two, w_up) + b_up)
    activation = low(jax.nn.gelu(pre_act, approximate=True))
    return mixed + matmul_exact(activation, w_down) + b_down

def reference(layer_input, ln1_gain, ln1_bias, w_qkv, b_qkv, w_out, b_out, ln2_gain, ln2_bias, w_up, b_up, w_down, b_down, feature_signs, match_blocks, match_count, out_grad):
    sign_table = (2 * feature_signs - 1).astype(jnp.float32)
    nblocks = SEQLEN // BLOCK
    group_seqs = 1
    for candidate in range(1, SEQS + 1):
        if SEQS % candidate == 0 and candidate * SEQLEN <= 4096:
            group_seqs = candidate
    group_count = SEQS // group_seqs
    lists_grouped = match_blocks.reshape(group_count, group_seqs, HEADS, nblocks, MATCH)
    counts_grouped = match_count.reshape(group_count, group_seqs, HEADS, nblocks)
    params = (layer_input, ln1_gain, ln1_bias, w_qkv, b_qkv, w_out, b_out, ln2_gain, ln2_bias, w_up, b_up, w_down, b_down)
    params = tuple((item.astype(jnp.float32) for item in params))
    checked = jax.checkpoint(layer_group)

    def forward(inputs, gain_one, bias_one, wqkv, bqkv, wout, bout, gain_two, bias_two, wup, bup, wdown, bdown):
        stacked = inputs.reshape(group_count, group_seqs * SEQLEN, D)

        def one_group(packed):
            return checked(packed[0], packed[1], packed[2], gain_one, bias_one, wqkv, bqkv, wout, bout, gain_two, bias_two, wup, bup, wdown, bdown, sign_table)
        outputs = lax.map(one_group, (stacked, lists_grouped, counts_grouped))
        return outputs.reshape(TOKENS, D)
    result, pullback = jax.vjp(forward, *params)
    grads = pullback(out_grad.astype(jnp.float32))
    return (result.astype(jnp.bfloat16), grads[0], grads[1], grads[2], grads[3], grads[4], grads[5], grads[6], grads[7], grads[8], grads[9], grads[10], grads[11], grads[12])
```

```python
import functools
import math

import jax
import jax.numpy as jnp
from jax import lax
from jax.experimental import pallas as pl
from jax.experimental.pallas import tpu as pltpu
from jax.sharding import PartitionSpec as P

HEADS = 12
HEAD_DIM = 64
BLOCK = 64
NB = 16
SEQLEN = NB * BLOCK
BF = jnp.bfloat16
F32 = jnp.float32
EPS = 1e-05
TILE = 256
GELU_A = math.sqrt(2.0 / math.pi)
GELU_B = 0.044715
VMEM = pl.BlockSpec(memory_space=pltpu.VMEM)
ANY = pl.BlockSpec(memory_space=pl.ANY)


def nn(a, b):
    return lax.dot_general(a, b, (((1,), (0,)), ((), ())), preferred_element_type=F32)


def nt(a, b):
    return lax.dot_general(a, b, (((1,), (1,)), ((), ())), preferred_element_type=F32)


def tn(a, b):
    return lax.dot_general(a, b, (((0,), (0,)), ((), ())), preferred_element_type=F32)


def ds(i, n):
    return pl.ds(i * n if isinstance(i, int) else pl.multiple_of(i * n, n), n)


def norm(x):
    c = x - jnp.mean(x, axis=-1, keepdims=True)
    inv = lax.rsqrt(jnp.mean(c * c, axis=-1, keepdims=True) + EPS)
    return c * inv, inv


def norm_back(g, normed, inv, gain):
    a = g * gain
    return inv * (
        a
        - jnp.mean(a, axis=-1, keepdims=True)
        - normed * jnp.mean(a * normed, axis=-1, keepdims=True)
    )


def call(body, outs, ins, specs=None, scratch=(), name=None):
    return pl.pallas_call(
        body,
        out_shape=[jax.ShapeDtypeStruct(s, d) for s, d in outs],
        in_specs=specs or [VMEM] * len(ins),
        out_specs=[VMEM] * len(outs),
        scratch_shapes=list(scratch),
        compiler_params=pltpu.CompilerParams(vmem_limit_bytes=64000 * 1024),
        name=name,
    )(*ins)


def qkv_body(x_ref, g_ref, s_ref, w_ref, b_ref, h_ref, qkv_ref):
    gain = g_ref[...].astype(F32)
    shift = s_ref[...].astype(F32)
    bias = b_ref[...].astype(F32)

    def step(i, _):
        rows = ds(i, TILE)
        normed, _inv = norm(x_ref[rows, :].astype(F32))
        h = (normed * gain + shift).astype(BF)
        h_ref[rows, :] = h
        qkv_ref[rows, :] = (nn(h, w_ref[...]) + bias).astype(BF)
        return 0

    lax.fori_loop(0, x_ref.shape[0] // TILE, step, 0)


def head_parts(qkv_ref, h):
    own = qkv_ref.shape[1] // 3
    p, e = h // 2, h % 2
    lane = lax.broadcasted_iota(jnp.int32, (1, 128), 1)
    mine = (lane // HEAD_DIM) == e

    def cols(part):
        return pl.ds(pl.multiple_of(part * own + p * 128, 128), 128)

    return p, e, lane, mine, cols


def lift_all(qkv_ref, s_ref, h, pq_ref, pk_ref):
    p, e, lane, mine, cols = head_parts(qkv_ref, h)
    feats = pq_ref.shape[1]
    signs = s_ref[p, :, ds(e, feats)]

    def step(i, _):
        rows = ds(i, TILE)
        for part, out in ((0, pq_ref), (1, pk_ref)):
            t = qkv_ref[rows, cols(part)]
            w = jnp.where(mine, t.astype(F32), 0.0)
            sq = jnp.sum(w * w, axis=-1, keepdims=True) * (0.5 * HEAD_DIM ** (-0.5))
            lifted = nn(t, signs) * HEAD_DIM ** (-0.25)
            out[rows, :] = (jnp.exp(lifted - sq) * feats ** (-0.5)).astype(BF)
        return 0

    lax.fori_loop(0, qkv_ref.shape[0] // TILE, step, 0)


def att_body(qkv_ref, s_ref, m_ref, att_ref, den_ref, pq_ref, pk_ref):
    def head(h, _):
        p, e, lane, mine, cols = head_parts(qkv_ref, h)
        lift_all(qkv_ref, s_ref, h, pq_ref, pk_ref)
        zero = jnp.zeros((), BF)
        v_one = jnp.where(mine, qkv_ref[:, cols(2)], jnp.ones((), BF))

        def step(i, _):
            rows = ds(i, TILE)
            q = jnp.where(mine, qkv_ref[rows, cols(0)] * BF(HEAD_DIM ** (-0.5)), zero)
            ex = jnp.exp(nt(q, qkv_ref[:, cols(1)]))
            low = nt(pq_ref[rows, :], pk_ref[...])
            per = TILE // BLOCK
            marks = m_ref[h, i]
            probs = jnp.concatenate(
                [
                    jnp.where(
                        marks[j : j + 1, :] > 0.5,
                        ex[j * BLOCK : (j + 1) * BLOCK],
                        low[j * BLOCK : (j + 1) * BLOCK],
                    )
                    for j in range(per)
                ],
                axis=0,
            ).astype(BF)
            both = nn(probs, v_one)
            den = pltpu.roll(both, HEAD_DIM, 1)
            out_cols = ds(p, 128)
            att = (both / den).astype(BF)
            att_ref[rows, out_cols] = jnp.where(mine, att, att_ref[rows, out_cols])
            den_ref[rows, out_cols] = jnp.where(mine, den, den_ref[rows, out_cols])
            return 0

        lax.fori_loop(0, qkv_ref.shape[0] // TILE, step, 0)
        return 0

    lax.fori_loop(0, qkv_ref.shape[1] // (3 * HEAD_DIM), head, 0)


def mix_body(x_ref, mine_ref, other_ref, w_ref, b_ref, g_ref, s_ref, mixed_ref, h_ref):
    f = lax.axis_index("feat")
    half = mine_ref.shape[1]

    def step(i, _):
        rows = ds(i, TILE)
        mixed = (
            x_ref[rows, :].astype(F32)
            + nn(mine_ref[rows, :], w_ref[ds(f, half), :])
            + nn(other_ref[rows, :], w_ref[ds(1 - f, half), :])
            + b_ref[...].astype(F32)
        )
        mixed_ref[rows, :] = mixed
        normed, _inv = norm(mixed)
        h_ref[rows, :] = (normed * g_ref[...].astype(F32) + s_ref[...].astype(F32)).astype(BF)
        return 0

    lax.fori_loop(0, x_ref.shape[0] // TILE, step, 0)


def ff_body(h_ref, og_ref, up_ref, down_ref, b_ref, act_ref, gp_ref, hid_ref, gh_ref, db_ref):
    db_ref[...] = jnp.zeros_like(db_ref)

    def step(i, _):
        rows = ds(i, TILE)
        v = nn(h_ref[rows, :], up_ref[...]) + b_ref[...].astype(F32)
        vv = v * v
        th = jnp.tanh(GELU_A * v * (1.0 + GELU_B * vv))
        half = 0.5 + 0.5 * th
        act = (v * half).astype(BF)
        slope = half + (0.5 * GELU_A) * v * (1.0 - th * th) * (1.0 + (3.0 * GELU_B) * vv)
        act_ref[rows, :] = act
        hid_ref[rows, :] = nn(act, down_ref[...]).astype(BF)
        gp = nt(og_ref[rows, :], down_ref[...]) * slope
        gpl = gp.astype(BF)
        gp_ref[rows, :] = gpl
        db_ref[...] += jnp.sum(gpl.astype(F32), axis=0, keepdims=True)
        gh_ref[rows, :] = nt(gpl, up_ref[...]).astype(BF)
        return 0

    lax.fori_loop(0, h_ref.shape[0] // TILE, step, 0)


def ffw_body(h_ref, og_ref, act_ref, gp_ref, up_ref, down_ref):
    def step(i, _):
        rows = ds(i, TILE)
        up_ref[rows, :] = tn(h_ref[:, rows], gp_ref[...]).astype(BF)
        down_ref[rows, :] = tn(og_ref[:, rows], act_ref[...]).astype(BF)
        return 0

    lax.fori_loop(0, h_ref.shape[1] // TILE, step, 0)


def outb_body(
    gh_ref, gho_ref, mixed_ref, og_ref, hid_ref, hido_ref, bd_ref, g_ref, w_ref, mine_ref, other_ref,
    gm_ref, gatt_ref, dw_ref, y_ref, vec_ref, gb_ref,
):
    f = lax.axis_index("feat")
    half = mine_ref.shape[1]
    tiles = mixed_ref.shape[0] // TILE
    own = tiles // 2
    gain = g_ref[...].astype(F32)
    vec_ref[...] = jnp.zeros_like(vec_ref)

    def step(i, _):
        rows = ds(i, TILE)
        mixed = mixed_ref[rows, :]
        og = og_ref[rows, :].astype(F32)
        normed, inv = norm(mixed)
        g = gh_ref[rows, :].astype(F32) + gho_ref[rows, :].astype(F32)
        gm = og + norm_back(g, normed, inv, gain)
        gm_ref[rows, :] = gm
        gb = gm.astype(BF)
        gb_ref[rows, :] = gb
        gatt_ref[rows, :] = nt(gb, w_ref[ds(f, half), :])

        @pl.when(i < own)
        def _():
            y_ref[rows, :] = (
                mixed + hid_ref[rows, :].astype(F32) + hido_ref[rows, :].astype(F32) + bd_ref[...].astype(F32)
            ).astype(BF)
            for j, term in enumerate((g * normed, g, gb.astype(F32), og)):
                vec_ref[j : j + 1, :] += jnp.sum(term, axis=0, keepdims=True)

        return 0

    lax.fori_loop(0, tiles, step, 0)
    gb_own = gb_ref[:, ds(f, half)]
    dw_ref[ds(f, half), :] = tn(mine_ref[...], gb_own).astype(BF)
    dw_ref[ds(1 - f, half), :] = tn(other_ref[...], gb_own).astype(BF)


def attb_body(
    qkv_ref, s_ref, m_ref, att_ref, den_ref, gatt_ref,
    gqkv_ref, pq_ref, pk_ref, gn_ref, gq_ref, gpq_ref,
):
    rows_all = qkv_ref.shape[0]
    scale = HEAD_DIM ** (-0.5)

    def head(h, _):
        p, e, lane, mine, cols = head_parts(qkv_ref, h)
        feats = pq_ref.shape[1]
        zero = jnp.zeros((), BF)
        lift_all(qkv_ref, s_ref, h, pq_ref, pk_ref)
        first_other = (1 - e) * HEAD_DIM

        def prep(i, _):
            rows = ds(i, TILE)
            inv = 1.0 / den_ref[rows, ds(p, 128)]
            ga = jnp.where(mine, gatt_ref[rows, ds(p, 128)] * inv, 0.0)
            gd = -jnp.sum(ga * att_ref[rows, ds(p, 128)].astype(F32), axis=-1, keepdims=True)
            gn_ref[rows, :] = jnp.where(lane == first_other, gd, ga).astype(BF)
            return 0

        lax.fori_loop(0, rows_all // TILE, prep, 0)
        gq_ref[...] = jnp.zeros_like(gq_ref)
        gpq_ref[...] = jnp.zeros_like(gpq_ref)
        signs = s_ref[p, :, ds(e, feats)]

        def lift_back(t, raw, g_phi):
            gl = g_phi * raw.astype(F32)
            gt = nt(gl.astype(BF), signs) * HEAD_DIM ** (-0.25)
            return gt - jnp.sum(gl, axis=-1, keepdims=True) * (scale * t.astype(F32))

        def put(part, rows, value):
            gqkv_ref[rows, cols(part)] = jnp.where(mine, value.astype(BF), gqkv_ref[rows, cols(part)])

        def step(i, _):
            rows = ds(i, TILE)
            k = jnp.where(mine, qkv_ref[rows, cols(1)] * BF(scale), zero)
            v_one = jnp.where(mine, qkv_ref[rows, cols(2)], jnp.ones((), BF))
            q_all = qkv_ref[:, cols(0)]
            pk = pk_ref[rows, :]
            ex = jnp.exp(nt(k, q_all))
            low = nt(pk, pq_ref[...])
            da = nt(v_one, gn_ref[...])
            per = TILE // BLOCK
            marks = m_ref[h, i]
            probs, dl, gs = [], [], []
            for j in range(per):
                part = slice(j * BLOCK, (j + 1) * BLOCK)
                on = marks[j : j + 1, :] > 0.5
                exj, daj = ex[part], da[part]
                probs.append(jnp.where(on, exj, low[part]))
                dl.append(jnp.where(on, 0.0, daj))
                gs.append(jnp.where(on, daj * exj, 0.0))
            probs = jnp.concatenate(probs, axis=0).astype(BF)
            dl = jnp.concatenate(dl, axis=0).astype(BF)
            gs = jnp.concatenate(gs, axis=0).astype(BF)
            put(2, rows, nn(probs, gn_ref[...]))
            g_phi_k = nn(dl, pq_ref[...])
            gk = nn(gs, q_all) * scale + lift_back(qkv_ref[rows, cols(1)], pk, g_phi_k)
            put(1, rows, gk)
            gpq_ref[...] += tn(dl, pk)
            gq_ref[...] += tn(gs, k)
            return 0

        lax.fori_loop(0, rows_all // TILE, step, 0)

        def last(i, _):
            rows = ds(i, TILE)
            gq = gq_ref[rows, :] + lift_back(qkv_ref[rows, cols(0)], pq_ref[rows, :], gpq_ref[rows, :])
            put(0, rows, gq)
            return 0

        lax.fori_loop(0, rows_all // TILE, last, 0)
        return 0

    lax.fori_loop(0, qkv_ref.shape[1] // (3 * HEAD_DIM), head, 0)


def qkvb_body(gqkv_ref, h_ref, w_ref, gh_ref, dw_ref, db_ref):
    db_ref[...] = jnp.zeros_like(db_ref)

    def step(i, _):
        rows = ds(i, TILE)
        g = gqkv_ref[rows, :]
        db_ref[...] += jnp.sum(g.astype(F32), axis=0, keepdims=True)
        gh_ref[rows, :] = nt(g, w_ref[...]).astype(BF)
        return 0

    lax.fori_loop(0, gqkv_ref.shape[0] // TILE, step, 0)

    def weight(i, _):
        rows = ds(i, TILE)
        dw_ref[rows, :] = tn(h_ref[:, rows], gqkv_ref[...]).astype(BF)
        return 0

    lax.fori_loop(0, h_ref.shape[1] // TILE, weight, 0)


def ln1b_body(gh_ref, gho_ref, x_ref, g_ref, gm_ref, dx_ref, vec_ref):
    gain = g_ref[...].astype(F32)
    vec_ref[...] = jnp.zeros_like(vec_ref)

    def step(i, _):
        rows = ds(i, TILE)
        normed, inv = norm(x_ref[rows, :].astype(F32))
        g = gh_ref[rows, :].astype(F32) + gho_ref[rows, :].astype(F32)
        dx_ref[rows, :] = gm_ref[rows, :] + norm_back(g, normed, inv, gain)
        vec_ref[0:1, :] += jnp.sum(g * normed, axis=0, keepdims=True)
        vec_ref[1:2, :] += jnp.sum(g, axis=0, keepdims=True)
        return 0

    lax.fori_loop(0, dx_ref.shape[0] // TILE, step, 0)


def body(
    layer_input, ln1_gain, ln1_bias, w_qkv, b_qkv, w_out, b_out, ln2_gain, ln2_bias,
    w_up, b_up, w_down, b_down, feature_signs, match_blocks, match_count, out_grad,
):
    rows, width = layer_input.shape
    half_width = width // 2
    half_heads = HEADS // 2
    hidden = w_up.shape[1]
    f = lax.axis_index("feat")
    tokens = 2 * rows
    assert lax.axis_size("feat") == 2 and match_blocks.shape[0] == 1 and tokens == SEQLEN

    def swap(a):
        return lax.ppermute(a, "feat", [(0, 1), (1, 0)])

    def row(a):
        return a.reshape(1, -1)

    x = jnp.concatenate([layer_input, swap(layer_input)], axis=0)
    og = jnp.concatenate([out_grad, swap(out_grad)], axis=0)
    signs = (2 * feature_signs - 1).astype(BF)
    own_signs = lax.dynamic_slice_in_dim(signs, f * half_heads, half_heads, 0)
    far_signs = swap(lax.dynamic_slice_in_dim(signs, (1 - f) * half_heads, half_heads, 0))
    signs = jnp.concatenate([own_signs, far_signs], axis=2)
    feats = signs.shape[2]
    pairs = signs.reshape(half_heads // 2, 2, HEAD_DIM, feats)
    table = jnp.concatenate(
        [
            jnp.pad(pairs[:, 0], ((0, 0), (0, HEAD_DIM), (0, 0))),
            jnp.pad(pairs[:, 1], ((0, 0), (HEAD_DIM, 0), (0, 0))),
        ],
        axis=2,
    )
    lists = lax.dynamic_slice_in_dim(match_blocks[0], f * half_heads, half_heads, 0)
    counts = lax.dynamic_slice_in_dim(match_count[0], f * half_heads, half_heads, 0)
    used = jnp.arange(lists.shape[2], dtype=jnp.int32) < counts[..., None]
    shift = f * (NB // 2)
    block = (jnp.arange(NB, dtype=jnp.int32) + shift) % NB
    matched = jnp.any(used[..., None] & (lists[..., None] == block), axis=2)
    matched = jnp.where(f == 0, matched, jnp.roll(matched, NB // 2, axis=1)).astype(F32)
    tiled = (half_heads, tokens // TILE, TILE // BLOCK, tokens)
    marks = jnp.repeat(matched, BLOCK, axis=2).reshape(tiled)
    marks_t = jnp.repeat(matched.transpose(0, 2, 1), BLOCK, axis=2).reshape(tiled)

    def own_cols(a):
        return jnp.concatenate(
            [lax.dynamic_slice_in_dim(a, i * width + f * half_width, half_width, 1) for i in range(3)], axis=1
        )

    w_own, b_own = own_cols(w_qkv), own_cols(row(b_qkv))
    h1, qkv = call(
        qkv_body, [((tokens, width), BF), ((tokens, 3 * half_width), BF)],
        [x, row(ln1_gain), row(ln1_bias), w_own, b_own], name="qkv",
    )
    phi = pltpu.VMEM((tokens, feats), BF)
    att, den = call(
        att_body, [((tokens, half_width), BF), ((tokens, half_width), F32)], [qkv, table, marks],
        scratch=[phi, phi], name="att",
    )
    far = swap(att)
    att_far = jnp.concatenate([far[rows:], far[:rows]], axis=0)
    mixed, h2 = call(
        mix_body, [((tokens, width), F32), ((tokens, width), BF)],
        [x, att, att_far, w_out, row(b_out), row(ln2_gain), row(ln2_bias)], name="mix",
    )
    act, gp, hid, gh2, d_bup = call(
        ff_body,
        [((tokens, hidden), BF), ((tokens, hidden), BF), ((tokens, width), BF), ((tokens, width), BF), ((1, hidden), F32)],
        [h2, og, w_up, w_down, row(b_up)], name="ff",
    )
    gh_far = swap(gh2)
    gh_far = jnp.concatenate([gh_far[rows:], gh_far[:rows]], axis=0)
    hid_far = swap(hid[rows:])
    d_up, d_down = call(
        ffw_body, [((width, hidden), BF), ((width, hidden), BF)], [h2, og, act, gp], name="ffw"
    )
    gm, gatt, d_out, y, vec2 = call(
        outb_body,
        [
            ((tokens, width), F32), ((tokens, half_width), F32), ((width, half_width), BF),
            ((rows, width), BF), ((8, width), F32),
        ],
        [gh2, gh_far, mixed, og, hid, hid_far, row(b_down), row(ln2_gain), w_out, att, att_far],
        scratch=[pltpu.VMEM((tokens, width), BF)], name="outb",
    )
    gqkv, = call(
        attb_body, [((tokens, 3 * half_width), BF)], [qkv, table, marks_t, att, den, gatt],
        scratch=[phi, phi, pltpu.VMEM((tokens, 128), BF), pltpu.VMEM((tokens, 128), F32), pltpu.VMEM((tokens, feats), F32)],
        name="attb",
    )
    gh1, d_qkv, d_bqkv = call(
        qkvb_body, [((tokens, width), BF), ((width, 3 * half_width), BF), ((1, 3 * half_width), F32)],
        [gqkv, h1, w_own], name="qkvb",
    )
    gh1_far = swap(gh1[rows:])
    dx, vec1 = call(
        ln1b_body, [((rows, width), F32), ((8, width), F32)],
        [gh1, gh1_far, layer_input, row(ln1_gain), gm], name="ln1b",
    )

    def over_seq(a):
        return lax.psum_scatter(a, "seq", scatter_dimension=0, tiled=True).astype(F32)

    up = over_seq(d_up)
    down = over_seq(d_down).T
    both = over_seq(jnp.concatenate([d_qkv, d_out], axis=1))
    keep = both.shape[0] // 2
    mine = lax.dynamic_slice_in_dim(both, f * keep, keep, 0)
    theirs = swap(lax.dynamic_slice_in_dim(both, (1 - f) * keep, keep, 0))
    low = jnp.where(f == 0, mine, theirs).reshape(keep, 4, 1, half_width)
    high = jnp.where(f == 0, theirs, mine).reshape(keep, 4, 1, half_width)
    full = jnp.concatenate([low, high], axis=2).reshape(keep, 4 * width)

    def scatter(v):
        return lax.psum_scatter(v.reshape(-1), ("seq", "feat"), scatter_dimension=0, tiled=True)

    d_b = jnp.zeros((1, 3 * width), F32)
    for i in range(3):
        d_b = lax.dynamic_update_slice(
            d_b, d_bqkv[:, i * half_width : (i + 1) * half_width], (0, i * width + f * half_width)
        )
    return (
        y, dx, scatter(vec1[0]), scatter(vec1[1]), full[:, : 3 * width], scatter(d_b), full[:, 3 * width :],
        scatter(vec2[2]), scatter(vec2[0]), scatter(vec2[1]), up, over_seq(d_bup.reshape(-1)), down, scatter(vec2[3]),
    )


def solution(mesh):
    both = ("seq", "feat")
    return jax.shard_map(
        body,
        mesh=mesh,
        in_specs=(
            P(both, None), P(), P(), P(), P(), P(), P(), P(), P(), P(None, "feat"), P("feat"), P("feat", None), P(),
            P(None, None, "feat"), P("seq", None, None, None), P("seq", None, None), P(both, None),
        ),
        out_specs=(
            P(both, None), P(both, None), P(both), P(both), P(both, None), P(both), P(both, None), P(both), P(both),
            P(both), P("seq", "feat"), P(("feat", "seq")), P("feat", "seq"), P(both),
        ),
        check_vma=False,
    )
```

```python
import functools
import math

import jax
import jax.numpy as jnp
from jax import lax
from jax.experimental import pallas as pl
from jax.experimental.pallas import tpu as pltpu
from jax.sharding import PartitionSpec as P

HEADS = 12
HEAD_DIM = 64
BLOCK = 64
NB = 16
SEQLEN = NB * BLOCK
BF = jnp.bfloat16
F32 = jnp.float32
EPS = 1e-05
TILE = 256
GELU_A = math.sqrt(2.0 / math.pi)
GELU_B = 0.044715
MESH = pl.DeviceIdType.MESH
VMEM = pl.BlockSpec(memory_space=pltpu.VMEM)
ANY = pl.BlockSpec(memory_space=pl.ANY)


def nn(a, b):
    return lax.dot_general(a, b, (((1,), (0,)), ((), ())), preferred_element_type=F32)


def nt(a, b):
    return lax.dot_general(a, b, (((1,), (1,)), ((), ())), preferred_element_type=F32)


def tn(a, b):
    return lax.dot_general(a, b, (((0,), (0,)), ((), ())), preferred_element_type=F32)


def ds(i, n):
    return pl.ds(i * n if isinstance(i, int) else pl.multiple_of(i * n, n), n)


def norm(x):
    c = x - jnp.mean(x, axis=-1, keepdims=True)
    inv = lax.rsqrt(jnp.mean(c * c, axis=-1, keepdims=True) + EPS)
    return c * inv, inv


def norm_back(g, normed, inv, gain):
    a = g * gain
    return inv * (
        a
        - jnp.mean(a, axis=-1, keepdims=True)
        - normed * jnp.mean(a * normed, axis=-1, keepdims=True)
    )


def split(n):
    p = 1
    while 2 * (2 * p) ** 3 <= n:
        p *= 2
    assert n % (p * p) == 0
    return p, n // (p * p)


class Net:
    def __init__(self, n):
        p, self.nz = split(n)
        self.p = p
        self.s, self.f = lax.axis_index("seq"), lax.axis_index("feat")
        x, y = lax.rem(self.s, p), lax.rem(self.s // p, p)
        f = self.f
        self.sizes = (p, p, self.nz)
        self.at = (x + f * (y - x), y + f * (x - y), self.s // (p * p))
        self.strides = (1 + f * (p - 1), p + f * (1 - p), p * p)

    def place(self, dest):
        p = self.p
        x, y, z = lax.rem(dest, p), lax.rem(dest // p, p), dest // (p * p)
        f = self.f
        return ((x + f * (y - x)) * p + y + f * (x - y)) * self.nz + z

    def peer(self, phase, d):
        j = lax.rem(self.at[phase] + d, self.sizes[phase])
        return j, self.s + (j - self.at[phase]) * self.strides[phase]

    def barrier(self):
        sem = pltpu.get_barrier_semaphore()
        count = 1
        for phase in range(3):
            for d in range(1, self.sizes[phase]):
                pl.semaphore_signal(sem, inc=1, device_id={"seq": self.peer(phase, d)[1]}, device_id_type=MESH)
                count += 1
        pl.semaphore_signal(sem, inc=1, device_id={"feat": 1 - self.f}, device_id_type=MESH)
        pl.semaphore_wait(sem, count)

    def slot(self, phase, d):
        return sum(size - 1 for size in self.sizes[:phase]) + d - 1

    def slots(self):
        return self.slot(3, 1) + 1


def scatter_bufs(n, rows, cols):
    p, nz = split(n)
    return [
        pltpu.VMEM((p - 1, p * nz, rows, cols), BF),
        pltpu.VMEM((p * nz, rows, cols), BF),
        pltpu.VMEM((p - 1, nz, rows, cols), BF),
        pltpu.VMEM((nz, rows, cols), BF),
        pltpu.VMEM((nz - 1, 1, rows, cols), BF),
    ]


class Scatter:
    def __init__(self, net, src, bufs, send, recv):
        self.net, self.send, self.recv = net, send, recv
        self.hold = (src, bufs[1], bufs[3])
        self.got = (bufs[0], bufs[2], bufs[4])

    def block(self, phase, j):
        size = self.got[phase].shape[1]
        return pl.ds(j * size, size)

    def copies(self, phase):
        net, out = self.net, []
        for d in range(1, net.sizes[phase]):
            j, device = net.peer(phase, d)
            k = net.slot(phase, d)
            out.append(
                pltpu.make_async_remote_copy(
                    src_ref=self.hold[phase].at[self.block(phase, j)],
                    dst_ref=self.got[phase].at[d - 1],
                    send_sem=self.send.at[k],
                    recv_sem=self.recv.at[k],
                    device_id={"seq": device},
                    device_id_type=MESH,
                )
            )
        return out

    def start(self, phase):
        for copy in self.copies(phase):
            copy.start()

    def finish(self, phase, put=None):
        for copy in self.copies(phase):
            copy.wait()
        got, own = self.got[phase], self.hold[phase]
        size = got.shape[1]
        base = self.net.at[phase] * size

        def add(i, _):
            total = own[base + i].astype(F32)
            for d in range(got.shape[0]):
                total = total + got[d, i].astype(F32)
            if put is None:
                self.hold[phase + 1][i] = total.astype(BF)
            else:
                put(total)
            return 0

        lax.fori_loop(0, size, add, 0)


class Vector:
    def __init__(self, net, bufs, send, recv, both):
        self.net, self.bufs, self.send, self.recv, self.both = net, bufs, send, recv, both

    def copies(self, phase):
        net, out = self.net, []
        peers = [({"feat": 1 - net.f}, net.slots() - 1)]
        if phase < 3:
            peers = [({"seq": net.peer(phase, d)[1]}, net.slot(phase, d)) for d in range(1, net.sizes[phase])]
        for device, k in peers:
            out.append(
                pltpu.make_async_remote_copy(
                    src_ref=self.bufs.at[phase],
                    dst_ref=self.bufs.at[4 + k],
                    send_sem=self.send.at[k],
                    recv_sem=self.recv.at[k],
                    device_id=device,
                    device_id_type=MESH,
                )
            )
        return out

    def start(self, phase):
        for copy in self.copies(phase):
            copy.start()

    def finish(self, phase):
        for copy in self.copies(phase):
            copy.wait()
        first, count = (self.net.slots() - 1, 1) if phase == 3 else (self.net.slot(phase, 1), self.net.sizes[phase] - 1)
        total = self.bufs[phase]
        for k in range(count):
            total = total + self.bufs[4 + first + k]
        if phase < 3:
            self.bufs[phase + 1] = total
        return total


def grads_body(
    n, up_ref, down_ref, out_ref, qkv_ref, rows_ref, bqkv_ref, bup_ref,
    oup_ref, odown_ref, oout_ref, oqkv_ref, orows_ref, obqkv_ref, obup_ref, *scratch,
):
    net = Net(n)
    bufs, tail = scratch[:20], scratch[20:]
    sout, sqkv, gout, gqkv, vrows, vbqkv, vbup, send, recv = tail
    parts = []
    for i, src in enumerate((down_ref, up_ref, out_ref, qkv_ref)):
        parts.append(Scatter(net, src, bufs[5 * i : 5 * i + 5], send.at[i], recv.at[i]))
    vectors = [Vector(net, ref, send.at[4 + i], recv.at[4 + i], i < 2) for i, ref in enumerate((vrows, vbqkv, vbup))]
    vrows[0], vbqkv[0], vbup[0] = rows_ref[...], bqkv_ref[...], bup_ref[...]
    half = sout.shape[1]

    def whole(ref):
        def put(total):
            ref[...] = total

        return put

    def halves(ref):
        def put(total):
            ref[0], ref[1] = total[:half], total[half:]

        return put

    net.barrier()
    for part in parts:
        part.start(0)
    for v in vectors:
        v.start(0)
    for phase in (0, 1):
        for part in parts:
            part.finish(phase)
            part.start(phase + 1)
        for v in vectors:
            v.finish(phase)
            v.start(phase + 1)
    for part, put in zip(parts, (whole(odown_ref), whole(oup_ref), halves(sout), halves(sqkv))):
        part.finish(2, put)
    last = net.slots() - 1
    swaps = []
    for i, (src, dst) in enumerate(((sout, gout), (sqkv, gqkv))):
        swaps.append(
            pltpu.make_async_remote_copy(
                src_ref=src.at[1 - net.f], dst_ref=dst, send_sem=send.at[2 + i, last], recv_sem=recv.at[2 + i, last],
                device_id={"feat": 1 - net.f}, device_id_type=MESH,
            )
        )
    for swap in swaps:
        swap.start()
    rows = vectors[0].finish(2)
    bqkv = vectors[1].finish(2)
    bup = vectors[2].finish(2)
    vectors[0].start(3)
    vectors[1].start(3)
    width = rows.shape[1]
    lanes = orows_ref.shape[1]
    where = 2 * net.s + net.f

    def cut(value, per, index, size):
        shift = lax.rem(size - index * per, size)
        return pltpu.roll(value, shift, 1)[:, :lanes]

    obup_ref[...] = cut(bup, bup.shape[1] // n, net.s, bup.shape[1])
    rows = vectors[0].finish(3)
    bqkv = vectors[1].finish(3)
    orows_ref[...] = cut(rows, width // (2 * n), where, width)
    obqkv_ref[...] = cut(bqkv, bqkv.shape[1] // (2 * n), where, bqkv.shape[1])
    for swap in swaps:
        swap.wait()
    own = sout.shape[2]
    f = net.f
    oout_ref[:, ds(f, own)] = sout[f]
    oout_ref[:, ds(1 - f, own)] = gout[...]
    for i in range(3):
        part = slice(i * own, (i + 1) * own)
        oqkv_ref[:, ds(2 * i + f, own)] = sqkv[f, :, part]
        oqkv_ref[:, ds(2 * i + 1 - f, own)] = gqkv[:, part]


def call(body, outs, ins, specs=None, scratch=(), name=None, net=None):
    return pl.pallas_call(
        body,
        out_shape=[jax.ShapeDtypeStruct(s, d) for s, d in outs],
        in_specs=specs or [VMEM] * len(ins),
        out_specs=[VMEM] * len(outs),
        scratch_shapes=list(scratch),
        compiler_params=pltpu.CompilerParams(
            vmem_limit_bytes=64000 * 1024, collective_id=net, has_side_effects=net is not None
        ),
        name=name,
    )(*ins)


def qkv_body(x_ref, g_ref, s_ref, w_ref, b_ref, h_ref, qkv_ref):
    gain = g_ref[...].astype(F32)
    shift = s_ref[...].astype(F32)
    bias = b_ref[...].astype(F32)

    def step(i, _):
        rows = ds(i, TILE)
        normed, _inv = norm(x_ref[rows, :].astype(F32))
        h = (normed * gain + shift).astype(BF)
        h_ref[rows, :] = h
        qkv_ref[rows, :] = (nn(h, w_ref[...]) + bias).astype(BF)
        return 0

    lax.fori_loop(0, x_ref.shape[0] // TILE, step, 0)


def head_parts(qkv_ref, h):
    own = qkv_ref.shape[1] // 3
    p, e = h // 2, h % 2
    lane = lax.broadcasted_iota(jnp.int32, (1, 128), 1)
    mine = (lane // HEAD_DIM) == e

    def cols(part):
        return pl.ds(pl.multiple_of(part * own + p * 128, 128), 128)

    return p, e, lane, mine, cols


def lift_all(qkv_ref, s_ref, h, pq_ref, pk_ref):
    p, e, lane, mine, cols = head_parts(qkv_ref, h)
    feats = pq_ref.shape[1]
    signs = s_ref[p, :, ds(e, feats)]

    def step(i, _):
        rows = ds(i, TILE)
        for part, out in ((0, pq_ref), (1, pk_ref)):
            t = qkv_ref[rows, cols(part)]
            w = jnp.where(mine, t.astype(F32), 0.0)
            sq = jnp.sum(w * w, axis=-1, keepdims=True) * (0.5 * HEAD_DIM ** (-0.5))
            lifted = nn(t, signs) * HEAD_DIM ** (-0.25)
            out[rows, :] = (jnp.exp(lifted - sq) * feats ** (-0.5)).astype(BF)
        return 0

    lax.fori_loop(0, qkv_ref.shape[0] // TILE, step, 0)


def att_body(qkv_ref, s_ref, m_ref, att_ref, den_ref, pq_ref, pk_ref):
    def head(h, _):
        p, e, lane, mine, cols = head_parts(qkv_ref, h)
        lift_all(qkv_ref, s_ref, h, pq_ref, pk_ref)
        zero = jnp.zeros((), BF)
        v_one = jnp.where(mine, qkv_ref[:, cols(2)], jnp.ones((), BF))

        def step(i, _):
            rows = ds(i, TILE)
            q = jnp.where(mine, qkv_ref[rows, cols(0)] * BF(HEAD_DIM ** (-0.5)), zero)
            ex = jnp.exp(nt(q, qkv_ref[:, cols(1)]))
            low = nt(pq_ref[rows, :], pk_ref[...])
            per = TILE // BLOCK
            marks = m_ref[h, i]
            probs = jnp.concatenate(
                [
                    jnp.where(
                        marks[j : j + 1, :] > 0.5,
                        ex[j * BLOCK : (j + 1) * BLOCK],
                        low[j * BLOCK : (j + 1) * BLOCK],
                    )
                    for j in range(per)
                ],
                axis=0,
            ).astype(BF)
            both = nn(probs, v_one)
            den = pltpu.roll(both, HEAD_DIM, 1)
            out_cols = ds(p, 128)
            att = (both / den).astype(BF)
            att_ref[rows, out_cols] = jnp.where(mine, att, att_ref[rows, out_cols])
            den_ref[rows, out_cols] = jnp.where(mine, den, den_ref[rows, out_cols])
            return 0

        lax.fori_loop(0, qkv_ref.shape[0] // TILE, step, 0)
        return 0

    lax.fori_loop(0, qkv_ref.shape[1] // (3 * HEAD_DIM), head, 0)


def mix_body(x_ref, mine_ref, other_ref, w_ref, b_ref, g_ref, s_ref, mixed_ref, h_ref):
    f = lax.axis_index("feat")
    half = mine_ref.shape[1]

    def step(i, _):
        rows = ds(i, TILE)
        mixed = (
            x_ref[rows, :].astype(F32)
            + nn(mine_ref[rows, :], w_ref[ds(f, half), :])
            + nn(other_ref[rows, :], w_ref[ds(1 - f, half), :])
            + b_ref[...].astype(F32)
        )
        mixed_ref[rows, :] = mixed
        normed, _inv = norm(mixed)
        h_ref[rows, :] = (normed * g_ref[...].astype(F32) + s_ref[...].astype(F32)).astype(BF)
        return 0

    lax.fori_loop(0, x_ref.shape[0] // TILE, step, 0)


def ff_body(h_ref, og_ref, up_ref, down_ref, b_ref, act_ref, gp_ref, hid_ref, gh_ref, db_ref):
    db_ref[...] = jnp.zeros_like(db_ref)

    def step(i, _):
        rows = ds(i, TILE)
        v = nn(h_ref[rows, :], up_ref[...]) + b_ref[...].astype(F32)
        vv = v * v
        th = jnp.tanh(GELU_A * v * (1.0 + GELU_B * vv))
        half = 0.5 + 0.5 * th
        act = (v * half).astype(BF)
        slope = half + (0.5 * GELU_A) * v * (1.0 - th * th) * (1.0 + (3.0 * GELU_B) * vv)
        act_ref[rows, :] = act
        hid_ref[rows, :] = nn(act, down_ref[...]).astype(BF)
        gp = nt(og_ref[rows, :], down_ref[...]) * slope
        gpl = gp.astype(BF)
        gp_ref[rows, :] = gpl
        db_ref[...] += jnp.sum(gpl.astype(F32), axis=0, keepdims=True)
        gh_ref[rows, :] = nt(gpl, up_ref[...]).astype(BF)
        return 0

    lax.fori_loop(0, h_ref.shape[0] // TILE, step, 0)


def put_chunks(out_ref, first, value, net):
    rows = out_ref.shape[1]
    for i in range(value.shape[0] // rows):
        out_ref[net.place(first + i)] = value[i * rows : (i + 1) * rows].astype(BF)


def ffw_body(n, h_ref, og_ref, act_ref, gp_ref, up_ref, down_ref):
    net = Net(n)
    wide = h_ref.shape[1] // 2
    per = wide // up_ref.shape[1]

    def step(i, _):
        rows = ds(i, wide)
        put_chunks(up_ref, i * per, tn(h_ref[:, rows], gp_ref[...]), net)
        put_chunks(down_ref, i * per, tn(og_ref[:, rows], act_ref[...]), net)
        return 0

    lax.fori_loop(0, 2, step, 0)


def outb_body(
    n, gh_ref, gho_ref, mixed_ref, og_ref, hid_ref, hido_ref, bd_ref, g_ref, w_ref, mine_ref, other_ref,
    gm_ref, gatt_ref, dw_ref, y_ref, vec_ref, gb_ref,
):
    f = lax.axis_index("feat")
    half = mine_ref.shape[1]
    tiles = mixed_ref.shape[0] // TILE
    own = tiles // 2
    gain = g_ref[...].astype(F32)
    vec_ref[...] = jnp.zeros_like(vec_ref)

    def step(i, _):
        rows = ds(i, TILE)
        mixed = mixed_ref[rows, :]
        og = og_ref[rows, :].astype(F32)
        normed, inv = norm(mixed)
        g = gh_ref[rows, :].astype(F32) + gho_ref[rows, :].astype(F32)
        gm = og + norm_back(g, normed, inv, gain)
        gm_ref[rows, :] = gm
        gb = gm.astype(BF)
        gb_ref[rows, :] = gb
        gatt_ref[rows, :] = nt(gb, w_ref[ds(f, half), :])

        @pl.when(i < own)
        def _():
            y_ref[rows, :] = (
                mixed + hid_ref[rows, :].astype(F32) + hido_ref[rows, :].astype(F32) + bd_ref[...].astype(F32)
            ).astype(BF)
            for j, term in enumerate((g * normed, g, gb.astype(F32), og)):
                vec_ref[j : j + 1, :] += jnp.sum(term, axis=0, keepdims=True)

        return 0

    lax.fori_loop(0, tiles, step, 0)
    gb_own = gb_ref[:, ds(f, half)]
    net = Net(n)
    per = half // dw_ref.shape[1]
    put_chunks(dw_ref, f * per, tn(mine_ref[...], gb_own), net)
    put_chunks(dw_ref, (1 - f) * per, tn(other_ref[...], gb_own), net)


def attb_body(
    qkv_ref, s_ref, m_ref, att_ref, den_ref, gatt_ref,
    gqkv_ref, pq_ref, pk_ref, gn_ref, gq_ref, gpq_ref,
):
    rows_all = qkv_ref.shape[0]
    scale = HEAD_DIM ** (-0.5)

    def head(h, _):
        p, e, lane, mine, cols = head_parts(qkv_ref, h)
        feats = pq_ref.shape[1]
        zero = jnp.zeros((), BF)
        lift_all(qkv_ref, s_ref, h, pq_ref, pk_ref)
        first_other = (1 - e) * HEAD_DIM

        def prep(i, _):
            rows = ds(i, TILE)
            inv = 1.0 / den_ref[rows, ds(p, 128)]
            ga = jnp.where(mine, gatt_ref[rows, ds(p, 128)] * inv, 0.0)
            gd = -jnp.sum(ga * att_ref[rows, ds(p, 128)].astype(F32), axis=-1, keepdims=True)
            gn_ref[rows, :] = jnp.where(lane == first_other, gd, ga).astype(BF)
            return 0

        lax.fori_loop(0, rows_all // TILE, prep, 0)
        gq_ref[...] = jnp.zeros_like(gq_ref)
        gpq_ref[...] = jnp.zeros_like(gpq_ref)
        signs = s_ref[p, :, ds(e, feats)]

        def lift_back(t, raw, g_phi):
            gl = g_phi * raw.astype(F32)
            gt = nt(gl.astype(BF), signs) * HEAD_DIM ** (-0.25)
            return gt - jnp.sum(gl, axis=-1, keepdims=True) * (scale * t.astype(F32))

        def put(part, rows, value):
            gqkv_ref[rows, cols(part)] = jnp.where(mine, value.astype(BF), gqkv_ref[rows, cols(part)])

        def step(i, _):
            rows = ds(i, TILE)
            k = jnp.where(mine, qkv_ref[rows, cols(1)] * BF(scale), zero)
            v_one = jnp.where(mine, qkv_ref[rows, cols(2)], jnp.ones((), BF))
            q_all = qkv_ref[:, cols(0)]
            pk = pk_ref[rows, :]
            ex = jnp.exp(nt(k, q_all))
            low = nt(pk, pq_ref[...])
            da = nt(v_one, gn_ref[...])
            per = TILE // BLOCK
            marks = m_ref[h, i]
            probs, dl, gs = [], [], []
            for j in range(per):
                part = slice(j * BLOCK, (j + 1) * BLOCK)
                on = marks[j : j + 1, :] > 0.5
                exj, daj = ex[part], da[part]
                probs.append(jnp.where(on, exj, low[part]))
                dl.append(jnp.where(on, 0.0, daj))
                gs.append(jnp.where(on, daj * exj, 0.0))
            probs = jnp.concatenate(probs, axis=0).astype(BF)
            dl = jnp.concatenate(dl, axis=0).astype(BF)
            gs = jnp.concatenate(gs, axis=0).astype(BF)
            put(2, rows, nn(probs, gn_ref[...]))
            g_phi_k = nn(dl, pq_ref[...])
            gk = nn(gs, q_all) * scale + lift_back(qkv_ref[rows, cols(1)], pk, g_phi_k)
            put(1, rows, gk)
            gpq_ref[...] += tn(dl, pk)
            gq_ref[...] += tn(gs, k)
            return 0

        lax.fori_loop(0, rows_all // TILE, step, 0)

        def last(i, _):
            rows = ds(i, TILE)
            gq = gq_ref[rows, :] + lift_back(qkv_ref[rows, cols(0)], pq_ref[rows, :], gpq_ref[rows, :])
            put(0, rows, gq)
            return 0

        lax.fori_loop(0, rows_all // TILE, last, 0)
        return 0

    lax.fori_loop(0, qkv_ref.shape[1] // (3 * HEAD_DIM), head, 0)


def qkvb_body(n, gqkv_ref, h_ref, w_ref, gh_ref, dw_ref, db_ref):
    db_ref[...] = jnp.zeros_like(db_ref)

    def step(i, _):
        rows = ds(i, TILE)
        g = gqkv_ref[rows, :]
        db_ref[...] += jnp.sum(g.astype(F32), axis=0, keepdims=True)
        gh_ref[rows, :] = nt(g, w_ref[...]).astype(BF)
        return 0

    lax.fori_loop(0, gqkv_ref.shape[0] // TILE, step, 0)

    net = Net(n)
    wide = h_ref.shape[1] // 2
    per = wide // dw_ref.shape[1]

    def weight(i, _):
        rows = ds(i, wide)
        put_chunks(dw_ref, i * per, tn(h_ref[:, rows], gqkv_ref[...]), net)
        return 0

    lax.fori_loop(0, 2, weight, 0)


def ln1b_body(gh_ref, gho_ref, x_ref, g_ref, gm_ref, dx_ref, vec_ref):
    gain = g_ref[...].astype(F32)
    vec_ref[...] = jnp.zeros_like(vec_ref)

    def step(i, _):
        rows = ds(i, TILE)
        normed, inv = norm(x_ref[rows, :].astype(F32))
        g = gh_ref[rows, :].astype(F32) + gho_ref[rows, :].astype(F32)
        dx_ref[rows, :] = gm_ref[rows, :] + norm_back(g, normed, inv, gain)
        vec_ref[0:1, :] += jnp.sum(g * normed, axis=0, keepdims=True)
        vec_ref[1:2, :] += jnp.sum(g, axis=0, keepdims=True)
        return 0

    lax.fori_loop(0, dx_ref.shape[0] // TILE, step, 0)


def body(
    layer_input, ln1_gain, ln1_bias, w_qkv, b_qkv, w_out, b_out, ln2_gain, ln2_bias,
    w_up, b_up, w_down, b_down, feature_signs, match_blocks, match_count, out_grad,
):
    rows, width = layer_input.shape
    half_width = width // 2
    half_heads = HEADS // 2
    hidden = w_up.shape[1]
    f = lax.axis_index("feat")
    tokens = 2 * rows
    n = lax.axis_size("seq")
    chunk = width // n
    assert lax.axis_size("feat") == 2 and match_blocks.shape[0] == 1 and tokens == SEQLEN

    def swap(a):
        return lax.ppermute(a, "feat", [(0, 1), (1, 0)])

    def row(a):
        return a.reshape(1, -1)

    x = jnp.concatenate([layer_input, swap(layer_input)], axis=0)
    og = jnp.concatenate([out_grad, swap(out_grad)], axis=0)
    signs = (2 * feature_signs - 1).astype(BF)
    own_signs = lax.dynamic_slice_in_dim(signs, f * half_heads, half_heads, 0)
    far_signs = swap(lax.dynamic_slice_in_dim(signs, (1 - f) * half_heads, half_heads, 0))
    signs = jnp.concatenate([own_signs, far_signs], axis=2)
    feats = signs.shape[2]
    pairs = signs.reshape(half_heads // 2, 2, HEAD_DIM, feats)
    table = jnp.concatenate(
        [
            jnp.pad(pairs[:, 0], ((0, 0), (0, HEAD_DIM), (0, 0))),
            jnp.pad(pairs[:, 1], ((0, 0), (HEAD_DIM, 0), (0, 0))),
        ],
        axis=2,
    )
    lists = lax.dynamic_slice_in_dim(match_blocks[0], f * half_heads, half_heads, 0)
    counts = lax.dynamic_slice_in_dim(match_count[0], f * half_heads, half_heads, 0)
    used = jnp.arange(lists.shape[2], dtype=jnp.int32) < counts[..., None]
    shift = f * (NB // 2)
    block = (jnp.arange(NB, dtype=jnp.int32) + shift) % NB
    matched = jnp.any(used[..., None] & (lists[..., None] == block), axis=2)
    matched = jnp.where(f == 0, matched, jnp.roll(matched, NB // 2, axis=1)).astype(F32)
    tiled = (half_heads, tokens // TILE, TILE // BLOCK, tokens)
    marks = jnp.repeat(matched, BLOCK, axis=2).reshape(tiled)
    marks_t = jnp.repeat(matched.transpose(0, 2, 1), BLOCK, axis=2).reshape(tiled)

    def own_cols(a):
        return jnp.concatenate(
            [lax.dynamic_slice_in_dim(a, i * width + f * half_width, half_width, 1) for i in range(3)], axis=1
        )

    w_own, b_own = own_cols(w_qkv), own_cols(row(b_qkv))
    h1, qkv = call(
        qkv_body, [((tokens, width), BF), ((tokens, 3 * half_width), BF)],
        [x, row(ln1_gain), row(ln1_bias), w_own, b_own], name="qkv",
    )
    phi = pltpu.VMEM((tokens, feats), BF)
    att, den = call(
        att_body, [((tokens, half_width), BF), ((tokens, half_width), F32)], [qkv, table, marks],
        scratch=[phi, phi], name="att",
    )
    far = swap(att)
    att_far = jnp.concatenate([far[rows:], far[:rows]], axis=0)
    mixed, h2 = call(
        mix_body, [((tokens, width), F32), ((tokens, width), BF)],
        [x, att, att_far, w_out, row(b_out), row(ln2_gain), row(ln2_bias)], name="mix",
    )
    act, gp, hid, gh2, d_bup = call(
        ff_body,
        [((tokens, hidden), BF), ((tokens, hidden), BF), ((tokens, width), BF), ((tokens, width), BF), ((1, hidden), F32)],
        [h2, og, w_up, w_down, row(b_up)], name="ff",
    )
    gh_far = swap(gh2)
    gh_far = jnp.concatenate([gh_far[rows:], gh_far[:rows]], axis=0)
    hid_far = swap(hid[rows:])
    d_up, d_down = call(
        functools.partial(ffw_body, n), [((n, chunk, hidden), BF), ((n, chunk, hidden), BF)], [h2, og, act, gp],
        name="ffw",
    )
    gm, gatt, d_out, y, vec2 = call(
        functools.partial(outb_body, n),
        [
            ((tokens, width), F32), ((tokens, half_width), F32), ((n, chunk, half_width), BF),
            ((rows, width), BF), ((8, width), F32),
        ],
        [gh2, gh_far, mixed, og, hid, hid_far, row(b_down), row(ln2_gain), w_out, att, att_far],
        scratch=[pltpu.VMEM((tokens, width), BF)], name="outb",
    )
    gqkv, = call(
        attb_body, [((tokens, 3 * half_width), BF)], [qkv, table, marks_t, att, den, gatt],
        scratch=[phi, phi, pltpu.VMEM((tokens, 128), BF), pltpu.VMEM((tokens, 128), F32), pltpu.VMEM((tokens, feats), F32)],
        name="attb",
    )
    gh1, d_qkv, d_bqkv = call(
        functools.partial(qkvb_body, n),
        [((tokens, width), BF), ((n, chunk, 3 * half_width), BF), ((1, 3 * half_width), F32)],
        [gqkv, h1, w_own], name="qkvb",
    )
    gh1_far = swap(gh1[rows:])
    dx, vec1 = call(
        ln1b_body, [((rows, width), F32), ((8, width), F32)],
        [gh1, gh1_far, layer_input, row(ln1_gain), gm], name="ln1b",
    )

    d_b = jnp.zeros((1, 3 * width), F32)
    for i in range(3):
        d_b = lax.dynamic_update_slice(
            d_b, d_bqkv[:, i * half_width : (i + 1) * half_width], (0, i * width + f * half_width)
        )
    vecs = jnp.concatenate([vec1[:2], vec2[:4], jnp.zeros((2, width), F32)], axis=0)
    slots = sum(split(n)) + split(n)[0] - 3 + 1
    bufs = []
    for cols in (hidden, hidden, half_width, 3 * half_width):
        bufs += scatter_bufs(n, chunk, cols)
    half_chunk = chunk // 2
    sems = pltpu.SemaphoreType.DMA((7, slots))
    up, down, out, full, vecs, d_b, d_bup = call(
        functools.partial(grads_body, n),
        [
            ((chunk, hidden), F32), ((chunk, hidden), F32), ((half_chunk, width), F32), ((half_chunk, 3 * width), F32),
            ((8, 128), F32), ((1, 128), F32), ((1, 128), F32),
        ],
        [d_up, d_down, d_out, d_qkv, vecs, d_b, d_bup],
        scratch=bufs + [
            pltpu.VMEM((2, half_chunk, half_width), F32), pltpu.VMEM((2, half_chunk, 3 * half_width), F32),
            pltpu.VMEM((half_chunk, half_width), F32), pltpu.VMEM((half_chunk, 3 * half_width), F32),
            pltpu.VMEM((4 + slots, 8, width), F32), pltpu.VMEM((4 + slots, 1, 3 * width), F32),
            pltpu.VMEM((4 + slots, 1, hidden), F32), sems, sems,
        ],
        name="grads", net=1,
    )
    own = width // (2 * n)

    def vec(i):
        return vecs[i, :own]

    return (
        y, dx, vec(0), vec(1), full, d_b[0, : 3 * own], out, vec(4), vec(2), vec(3), up, d_bup[0, : hidden // n],
        down.T, vec(5),
    )


def solution(mesh):
    both = ("seq", "feat")
    return jax.shard_map(
        body,
        mesh=mesh,
        in_specs=(
            P(both, None), P(), P(), P(), P(), P(), P(), P(), P(), P(None, "feat"), P("feat"), P("feat", None), P(),
            P(None, None, "feat"), P("seq", None, None, None), P("seq", None, None), P(both, None),
        ),
        out_specs=(
            P(both, None), P(both, None), P(both), P(both), P(both, None), P(both), P(both, None), P(both), P(both),
            P(both), P("seq", "feat"), P(("feat", "seq")), P("feat", "seq"), P(both),
        ),
        check_vma=False,
    )
```

```python
import functools
import math

import jax
import jax.numpy as jnp
from jax import lax
from jax.experimental import pallas as pl
from jax.experimental.pallas import tpu as pltpu
from jax.sharding import PartitionSpec as P

HEADS = 12
HEAD_DIM = 64
BLOCK = 64
NB = 16
SEQLEN = NB * BLOCK
BF = jnp.bfloat16
F32 = jnp.float32
EPS = 1e-05
TILE = 256
GELU_A = math.sqrt(2.0 / math.pi)
GELU_B = 0.044715
MESH = pl.DeviceIdType.MESH
VMEM = pl.BlockSpec(memory_space=pltpu.VMEM)
ANY = pl.BlockSpec(memory_space=pl.ANY)


def nn(a, b):
    return lax.dot_general(a, b, (((1,), (0,)), ((), ())), preferred_element_type=F32)


def nt(a, b):
    return lax.dot_general(a, b, (((1,), (1,)), ((), ())), preferred_element_type=F32)


def tn(a, b):
    return lax.dot_general(a, b, (((0,), (0,)), ((), ())), preferred_element_type=F32)


def ds(i, n):
    return pl.ds(i * n if isinstance(i, int) else pl.multiple_of(i * n, n), n)


def norm(x):
    c = x - jnp.mean(x, axis=-1, keepdims=True)
    inv = lax.rsqrt(jnp.mean(c * c, axis=-1, keepdims=True) + EPS)
    return c * inv, inv


def norm_back(g, normed, inv, gain):
    a = g * gain
    return inv * (
        a
        - jnp.mean(a, axis=-1, keepdims=True)
        - normed * jnp.mean(a * normed, axis=-1, keepdims=True)
    )


def split(n):
    p = 1
    while 2 * (2 * p) ** 3 <= n:
        p *= 2
    assert n % (p * p) == 0
    return p, n // (p * p)


class Net:
    def __init__(self, n):
        p, self.nz = split(n)
        self.p = p
        self.s, self.f = lax.axis_index("seq"), lax.axis_index("feat")
        x, y = lax.rem(self.s, p), lax.rem(self.s // p, p)
        f = self.f
        self.sizes = (p, p, self.nz)
        self.at = (x + f * (y - x), y + f * (x - y), self.s // (p * p))
        self.strides = (1 + f * (p - 1), p + f * (1 - p), p * p)

    def place(self, dest):
        p = self.p
        x, y, z = lax.rem(dest, p), lax.rem(dest // p, p), dest // (p * p)
        f = self.f
        return ((x + f * (y - x)) * p + y + f * (x - y)) * self.nz + z

    def peer(self, phase, d):
        j = lax.rem(self.at[phase] + d, self.sizes[phase])
        return j, self.s + (j - self.at[phase]) * self.strides[phase]

    def barrier(self):
        sem = pltpu.get_barrier_semaphore()
        count = 1
        for phase in range(3):
            for d in range(1, self.sizes[phase]):
                pl.semaphore_signal(sem, inc=1, device_id={"seq": self.peer(phase, d)[1]}, device_id_type=MESH)
                count += 1
        pl.semaphore_signal(sem, inc=1, device_id={"feat": 1 - self.f}, device_id_type=MESH)
        pl.semaphore_wait(sem, count)

    def slot(self, phase, d):
        return sum(size - 1 for size in self.sizes[:phase]) + d - 1

    def slots(self):
        return self.slot(3, 1) + 1


def scatter_bufs(n, rows, cols):
    p, nz = split(n)
    return [
        pltpu.VMEM((p - 1, p * nz, rows, cols), BF),
        pltpu.VMEM((p * nz, rows, cols), BF),
        pltpu.VMEM((p - 1, nz, rows, cols), BF),
        pltpu.VMEM((nz, rows, cols), BF),
        pltpu.VMEM((nz - 1, 1, rows, cols), BF),
    ]


class Scatter:
    def __init__(self, net, src, bufs, send, recv):
        self.net, self.send, self.recv = net, send, recv
        self.hold = (src, bufs[1], bufs[3])
        self.got = (bufs[0], bufs[2], bufs[4])

    def block(self, phase, j):
        size = self.got[phase].shape[1]
        return pl.ds(j * size, size)

    def copies(self, phase):
        net, out = self.net, []
        for d in range(1, net.sizes[phase]):
            j, device = net.peer(phase, d)
            k = net.slot(phase, d)
            out.append(
                pltpu.make_async_remote_copy(
                    src_ref=self.hold[phase].at[self.block(phase, j)],
                    dst_ref=self.got[phase].at[d - 1],
                    send_sem=self.send.at[k],
                    recv_sem=self.recv.at[k],
                    device_id={"seq": device},
                    device_id_type=MESH,
                )
            )
        return out

    def start(self, phase):
        for copy in self.copies(phase):
            copy.start()

    def finish(self, phase, put=None):
        for copy in self.copies(phase):
            copy.wait()
        got, own = self.got[phase], self.hold[phase]
        size = got.shape[1]
        base = self.net.at[phase] * size

        def add(i, _):
            total = own[base + i].astype(F32)
            for d in range(got.shape[0]):
                total = total + got[d, i].astype(F32)
            if put is None:
                self.hold[phase + 1][i] = total.astype(BF)
            else:
                put(total)
            return 0

        lax.fori_loop(0, size, add, 0)


class Vector:
    def __init__(self, net, bufs, send, recv):
        self.net, self.bufs, self.send, self.recv = net, bufs, send, recv

    def copies(self, phase):
        net, out = self.net, []
        peers = [({"feat": 1 - net.f}, net.slots() - 1)]
        if phase < 3:
            peers = [({"seq": net.peer(phase, d)[1]}, net.slot(phase, d)) for d in range(1, net.sizes[phase])]
        for device, k in peers:
            out.append(
                pltpu.make_async_remote_copy(
                    src_ref=self.bufs.at[phase],
                    dst_ref=self.bufs.at[4 + k],
                    send_sem=self.send.at[k],
                    recv_sem=self.recv.at[k],
                    device_id=device,
                    device_id_type=MESH,
                )
            )
        return out

    def start(self, phase):
        for copy in self.copies(phase):
            copy.start()

    def finish(self, phase):
        for copy in self.copies(phase):
            copy.wait()
        first, count = (self.net.slots() - 1, 1) if phase == 3 else (self.net.slot(phase, 1), self.net.sizes[phase] - 1)
        total = self.bufs[phase]
        for k in range(count):
            total = total + self.bufs[4 + first + k]
        if phase < 3:
            self.bufs[phase + 1] = total
        return total


def call(body, outs, ins, specs=None, scratch=(), name=None, net=None):
    return pl.pallas_call(
        body,
        out_shape=[jax.ShapeDtypeStruct(s, d) for s, d in outs],
        in_specs=specs or [VMEM] * len(ins),
        out_specs=[VMEM] * len(outs),
        scratch_shapes=list(scratch),
        compiler_params=pltpu.CompilerParams(
            vmem_limit_bytes=64000 * 1024, collective_id=net, has_side_effects=net is not None
        ),
        name=name,
    )(*ins)


def qkv_body(x_ref, g_ref, s_ref, w_ref, b_ref, h_ref, qkv_ref):
    gain = g_ref[...].astype(F32)
    shift = s_ref[...].astype(F32)
    bias = b_ref[...].astype(F32)

    def step(i, _):
        rows = ds(i, TILE)
        normed, _inv = norm(x_ref[rows, :].astype(F32))
        h = (normed * gain + shift).astype(BF)
        h_ref[rows, :] = h
        qkv_ref[rows, :] = (nn(h, w_ref[...]) + bias).astype(BF)
        return 0

    lax.fori_loop(0, x_ref.shape[0] // TILE, step, 0)


def head_parts(qkv_ref, h):
    own = qkv_ref.shape[1] // 3
    p, e = h // 2, h % 2
    lane = lax.broadcasted_iota(jnp.int32, (1, 128), 1)
    mine = (lane // HEAD_DIM) == e

    def cols(part):
        return pl.ds(pl.multiple_of(part * own + p * 128, 128), 128)

    return p, e, lane, mine, cols


def lift_all(qkv_ref, s_ref, h, pq_ref, pk_ref):
    p, e, lane, mine, cols = head_parts(qkv_ref, h)
    feats = pq_ref.shape[1]
    signs = s_ref[p, :, ds(e, feats)]

    def step(i, _):
        rows = ds(i, TILE)
        for part, out in ((0, pq_ref), (1, pk_ref)):
            t = qkv_ref[rows, cols(part)]
            w = jnp.where(mine, t.astype(F32), 0.0)
            sq = jnp.sum(w * w, axis=-1, keepdims=True) * (0.5 * HEAD_DIM ** (-0.5))
            lifted = nn(t, signs) * HEAD_DIM ** (-0.25)
            out[rows, :] = (jnp.exp(lifted - sq) * feats ** (-0.5)).astype(BF)
        return 0

    lax.fori_loop(0, qkv_ref.shape[0] // TILE, step, 0)


def att_body(qkv_ref, s_ref, m_ref, att_ref, den_ref, pq_ref, pk_ref):
    def head(h, _):
        p, e, lane, mine, cols = head_parts(qkv_ref, h)
        lift_all(qkv_ref, s_ref, h, pq_ref, pk_ref)
        zero = jnp.zeros((), BF)
        v_one = jnp.where(mine, qkv_ref[:, cols(2)], jnp.ones((), BF))

        def step(i, _):
            rows = ds(i, TILE)
            q = jnp.where(mine, qkv_ref[rows, cols(0)] * BF(HEAD_DIM ** (-0.5)), zero)
            ex = jnp.exp(nt(q, qkv_ref[:, cols(1)]))
            low = nt(pq_ref[rows, :], pk_ref[...])
            per = TILE // BLOCK
            marks = m_ref[h, i]
            probs = jnp.concatenate(
                [
                    jnp.where(
                        marks[j : j + 1, :] > 0.5,
                        ex[j * BLOCK : (j + 1) * BLOCK],
                        low[j * BLOCK : (j + 1) * BLOCK],
                    )
                    for j in range(per)
                ],
                axis=0,
            ).astype(BF)
            both = nn(probs, v_one)
            den = pltpu.roll(both, HEAD_DIM, 1)
            out_cols = ds(p, 128)
            att = (both / den).astype(BF)
            att_ref[rows, out_cols] = jnp.where(mine, att, att_ref[rows, out_cols])
            den_ref[rows, out_cols] = jnp.where(mine, den, den_ref[rows, out_cols])
            return 0

        lax.fori_loop(0, qkv_ref.shape[0] // TILE, step, 0)
        return 0

    lax.fori_loop(0, qkv_ref.shape[1] // (3 * HEAD_DIM), head, 0)


def mix_body(x_ref, mine_ref, other_ref, w_ref, b_ref, g_ref, s_ref, mixed_ref, h_ref):
    f = lax.axis_index("feat")
    half = mine_ref.shape[1]

    def step(i, _):
        rows = ds(i, TILE)
        mixed = (
            x_ref[rows, :].astype(F32)
            + nn(mine_ref[rows, :], w_ref[ds(f, half), :])
            + nn(other_ref[rows, :], w_ref[ds(1 - f, half), :])
            + b_ref[...].astype(F32)
        )
        mixed_ref[rows, :] = mixed
        normed, _inv = norm(mixed)
        h_ref[rows, :] = (normed * g_ref[...].astype(F32) + s_ref[...].astype(F32)).astype(BF)
        return 0

    lax.fori_loop(0, x_ref.shape[0] // TILE, step, 0)


def ff_body(h_ref, og_ref, up_ref, down_ref, b_ref, act_ref, gp_ref, hid_ref, gh_ref, db_ref):
    db_ref[...] = jnp.zeros_like(db_ref)

    def step(i, _):
        rows = ds(i, TILE)
        v = nn(h_ref[rows, :], up_ref[...]) + b_ref[...].astype(F32)
        vv = v * v
        th = jnp.tanh(GELU_A * v * (1.0 + GELU_B * vv))
        half = 0.5 + 0.5 * th
        act = (v * half).astype(BF)
        slope = half + (0.5 * GELU_A) * v * (1.0 - th * th) * (1.0 + (3.0 * GELU_B) * vv)
        act_ref[rows, :] = act
        hid_ref[rows, :] = nn(act, down_ref[...]).astype(BF)
        gp = nt(og_ref[rows, :], down_ref[...]) * slope
        gpl = gp.astype(BF)
        gp_ref[rows, :] = gpl
        db_ref[...] += jnp.sum(gpl.astype(F32), axis=0, keepdims=True)
        gh_ref[rows, :] = nt(gpl, up_ref[...]).astype(BF)
        return 0

    lax.fori_loop(0, h_ref.shape[0] // TILE, step, 0)


def put_chunks(out_ref, first, value, net):
    rows = out_ref.shape[1]
    for i in range(value.shape[0] // rows):
        out_ref[net.place(first + i)] = value[i * rows : (i + 1) * rows].astype(BF)


def ffw_body(n, h_ref, og_ref, act_ref, gp_ref, up_ref, down_ref):
    net = Net(n)
    wide = h_ref.shape[1] // 2
    per = wide // up_ref.shape[1]

    def step(i, _):
        rows = ds(i, wide)
        put_chunks(up_ref, i * per, tn(h_ref[:, rows], gp_ref[...]), net)
        put_chunks(down_ref, i * per, tn(og_ref[:, rows], act_ref[...]), net)
        return 0

    lax.fori_loop(0, 2, step, 0)


def outb_body(
    n, gh_ref, gho_ref, mixed_ref, og_ref, hid_ref, hido_ref, bd_ref, g_ref, w_ref, mine_ref, other_ref,
    gm_ref, gatt_ref, dw_ref, y_ref, vec_ref, gb_ref,
):
    f = lax.axis_index("feat")
    half = mine_ref.shape[1]
    tiles = mixed_ref.shape[0] // TILE
    own = tiles // 2
    gain = g_ref[...].astype(F32)
    vec_ref[...] = jnp.zeros_like(vec_ref)

    def step(i, _):
        rows = ds(i, TILE)
        mixed = mixed_ref[rows, :]
        og = og_ref[rows, :].astype(F32)
        normed, inv = norm(mixed)
        g = gh_ref[rows, :].astype(F32) + gho_ref[rows, :].astype(F32)
        gm = og + norm_back(g, normed, inv, gain)
        gb = gm.astype(BF)
        gb_ref[rows, :] = gb
        gatt_ref[rows, :] = nt(gb, w_ref[ds(f, half), :])

        @pl.when(i < own)
        def _():
            gm_ref[rows, :] = gm
            y_ref[rows, :] = (
                mixed + hid_ref[rows, :].astype(F32) + hido_ref[rows, :].astype(F32) + bd_ref[...].astype(F32)
            ).astype(BF)
            for j, term in enumerate((g * normed, g, gb.astype(F32), og)):
                vec_ref[j + 2 : j + 3, :] += jnp.sum(term, axis=0, keepdims=True)

        return 0

    lax.fori_loop(0, tiles, step, 0)
    gb_own = gb_ref[:, ds(f, half)]
    net = Net(n)
    per = half // dw_ref.shape[1]
    put_chunks(dw_ref, f * per, tn(mine_ref[...], gb_own), net)
    put_chunks(dw_ref, (1 - f) * per, tn(other_ref[...], gb_own), net)


def heads_back(
    qkv_ref, s_ref, m_ref, att_ref, den_ref, gatt_ref, gqkv_ref, pq_ref, pk_ref, gn_ref, gq_ref, gpq_ref, after
):
    rows_all = qkv_ref.shape[0]
    scale = HEAD_DIM ** (-0.5)

    def head(h, _):
        p, e, lane, mine, cols = head_parts(qkv_ref, h)
        feats = pq_ref.shape[1]
        zero = jnp.zeros((), BF)
        lift_all(qkv_ref, s_ref, h, pq_ref, pk_ref)
        first_other = (1 - e) * HEAD_DIM

        def prep(i, _):
            rows = ds(i, TILE)
            inv = 1.0 / den_ref[rows, ds(p, 128)]
            ga = jnp.where(mine, gatt_ref[rows, ds(p, 128)] * inv, 0.0)
            gd = -jnp.sum(ga * att_ref[rows, ds(p, 128)].astype(F32), axis=-1, keepdims=True)
            gn_ref[rows, :] = jnp.where(lane == first_other, gd, ga).astype(BF)
            return 0

        lax.fori_loop(0, rows_all // TILE, prep, 0)
        gq_ref[...] = jnp.zeros_like(gq_ref)
        gpq_ref[...] = jnp.zeros_like(gpq_ref)
        signs = s_ref[p, :, ds(e, feats)]

        def lift_back(t, raw, g_phi):
            gl = g_phi * raw.astype(F32)
            gt = nt(gl.astype(BF), signs) * HEAD_DIM ** (-0.25)
            return gt - jnp.sum(gl, axis=-1, keepdims=True) * (scale * t.astype(F32))

        def put(part, rows, value):
            gqkv_ref[rows, cols(part)] = jnp.where(mine, value.astype(BF), gqkv_ref[rows, cols(part)])

        def step(i, _):
            rows = ds(i, TILE)
            k = jnp.where(mine, qkv_ref[rows, cols(1)] * BF(scale), zero)
            v_one = jnp.where(mine, qkv_ref[rows, cols(2)], jnp.ones((), BF))
            q_all = qkv_ref[:, cols(0)]
            pk = pk_ref[rows, :]
            ex = jnp.exp(nt(k, q_all))
            low = nt(pk, pq_ref[...])
            da = nt(v_one, gn_ref[...])
            per = TILE // BLOCK
            marks = m_ref[h, i]
            probs, dl, gs = [], [], []
            for j in range(per):
                part = slice(j * BLOCK, (j + 1) * BLOCK)
                on = marks[j : j + 1, :] > 0.5
                exj, daj = ex[part], da[part]
                probs.append(jnp.where(on, exj, low[part]))
                dl.append(jnp.where(on, 0.0, daj))
                gs.append(jnp.where(on, daj * exj, 0.0))
            probs = jnp.concatenate(probs, axis=0).astype(BF)
            dl = jnp.concatenate(dl, axis=0).astype(BF)
            gs = jnp.concatenate(gs, axis=0).astype(BF)
            put(2, rows, nn(probs, gn_ref[...]))
            g_phi_k = nn(dl, pq_ref[...])
            gk = nn(gs, q_all) * scale + lift_back(qkv_ref[rows, cols(1)], pk, g_phi_k)
            put(1, rows, gk)
            gpq_ref[...] += tn(dl, pk)
            gq_ref[...] += tn(gs, k)
            return 0

        lax.fori_loop(0, rows_all // TILE, step, 0)

        def last(i, _):
            rows = ds(i, TILE)
            gq = gq_ref[rows, :] + lift_back(qkv_ref[rows, cols(0)], pq_ref[rows, :], gpq_ref[rows, :])
            put(0, rows, gq)
            return 0

        lax.fori_loop(0, rows_all // TILE, last, 0)
        for k, then in after.items():
            pl.when(h == k)(then)
        return 0

    lax.fori_loop(0, qkv_ref.shape[1] // (3 * HEAD_DIM), head, 0)


def back_body(
    n, qkv_ref, s_ref, m_ref, att_ref, den_ref, gatt_ref, h_ref, w_ref, x_ref, g_ref, gm_ref, up_ref, down_ref, out_ref,
    vec_ref, bup_ref, dx_ref, oup_ref, odown_ref, oout_ref, oqkv_ref, orows_ref, obqkv_ref, obup_ref, *scratch,
):
    net = Net(n)
    bufs, tail = scratch[:30], scratch[30:]
    pq, pk, gn, gq, gpq, gqkv, gw, gh_send, gh_got, sout, rout, sqkv, rqkv, vrows, vbqkv, vbup, send, recv = tail
    f = net.f
    other = {"feat": 1 - f}
    parts = [
        Scatter(net, src, bufs[5 * i : 5 * i + 5], send.at[i], recv.at[i])
        for i, src in enumerate((down_ref, up_ref, out_ref, gw.at[0], gw.at[1], gw.at[2]))
    ]
    down, up, out = parts[:3]
    pairs = parts[3:]
    vectors = [Vector(net, ref, send.at[6 + i], recv.at[6 + i]) for i, ref in enumerate((vrows, vbqkv, vbup))]
    last = net.slots() - 1
    half = sout.shape[1]
    rows = x_ref.shape[0]
    width = x_ref.shape[1]
    own = width // 2
    lanes = orows_ref.shape[1]

    def whole(ref):
        def put(total):
            ref[...] = total

        return put

    def halves(ref):
        def put(total):
            ref[0], ref[1] = total[:half], total[half:]

        return put

    def swap(i, src, dst):
        return pltpu.make_async_remote_copy(
            src_ref=src, dst_ref=dst, send_sem=send.at[i, last], recv_sem=recv.at[i, last],
            device_id=other, device_id_type=MESH,
        )

    def move(part, phase):
        part.finish(phase)
        part.start(phase + 1)

    def weight(p):
        g = jnp.concatenate([gqkv[:, i * own + p * 128 : i * own + (p + 1) * 128] for i in range(3)], axis=1)
        per = own // gw.shape[2]
        for i in range(2):
            put_chunks(gw.at[p], i * per, tn(h_ref[:, i * own : (i + 1) * own], g), net)
        pairs[p].start(0)

    net.barrier()
    for part in (down, up, out):
        part.start(0)

    def after1():
        move(down, 0)
        weight(0)

    def after2():
        move(up, 0)
        move(out, 0)

    def after3():
        move(down, 1)
        move(pairs[0], 0)
        weight(1)

    def after4():
        move(up, 1)
        move(out, 1)
        move(pairs[0], 1)

    heads_back(
        qkv_ref, s_ref, m_ref, att_ref, den_ref, gatt_ref, gqkv, pq, pk, gn, gq, gpq,
        {1: after1, 2: after2, 3: after3, 4: after4},
    )
    weight(2)
    tiles = rows // TILE

    def far(i, total):
        g = gqkv[ds(tiles + i, TILE), :]
        gh_send[ds(i, TILE), :] = nt(g, w_ref[...]).astype(BF)
        return total + jnp.sum(g.astype(F32), axis=0, keepdims=True)

    total = lax.fori_loop(0, tiles, far, jnp.zeros((1, 3 * own), F32))
    gh_swap = swap(9, gh_send, gh_got)
    gh_swap.start()
    move(pairs[1], 0)

    def sums(i, total):
        return total + jnp.sum(gqkv[ds(i, TILE), :].astype(F32), axis=0, keepdims=True)

    total = lax.fori_loop(0, tiles, sums, total)
    vbqkv[0] = jnp.zeros_like(vbqkv[0])
    for i in range(3):
        vbqkv[0, :, ds(2 * i + f, own)] = total[:, i * own : (i + 1) * own]
    vbup[0] = bup_ref[...]
    down.finish(2, whole(odown_ref))
    out.finish(2, halves(sout))
    out_swap = swap(2, sout.at[1 - f], rout)
    out_swap.start()
    up.finish(2, whole(oup_ref))
    move(pairs[1], 1)
    move(pairs[2], 0)
    gh_swap.wait()
    gain = g_ref[...].astype(F32)
    vrows[0] = vec_ref[...]

    def norm1(i, _):
        r = ds(i, TILE)
        normed, inv = norm(x_ref[r, :].astype(F32))
        g = nt(gqkv[r, :], w_ref[...]) + gh_got[r, :].astype(F32)
        dx_ref[r, :] = gm_ref[r, :] + norm_back(g, normed, inv, gain)
        vrows[0, 0:1, :] += jnp.sum(g * normed, axis=0, keepdims=True)
        vrows[0, 1:2, :] += jnp.sum(g, axis=0, keepdims=True)
        return 0

    lax.fori_loop(0, tiles, norm1, 0)
    for v in vectors:
        v.start(0)
    move(pairs[2], 1)
    for p in (0, 1):
        pairs[p].finish(2, halves(sqkv.at[p]))
    for v in vectors:
        v.finish(0)
        v.start(1)
    swaps = [swap(3 + p, sqkv.at[p, 1 - f], rqkv.at[p]) for p in range(3)]
    swaps[0].start()
    swaps[1].start()
    for v in vectors:
        v.finish(1)
        v.start(2)
    pairs[2].finish(2, halves(sqkv.at[2]))
    swaps[2].start()
    vecs, bqkv, bup = [v.finish(2) for v in vectors]
    vectors[0].start(3)
    vectors[1].start(3)
    where = 2 * net.s + f

    def cut(value, per, index, size):
        return pltpu.roll(value, lax.rem(size - index * per, size), 1)[:, :lanes]

    obup_ref[...] = cut(bup, bup.shape[1] // n, net.s, bup.shape[1])
    out_swap.wait()
    oout_ref[:, ds(f, own)] = sout[f]
    oout_ref[:, ds(1 - f, own)] = rout[...]

    def cols(i, p, side):
        return pl.ds(pl.multiple_of(i * width + side * own + p * 128, 128), 128)

    for p in range(3):
        swaps[p].wait()
        for i in range(3):
            part = slice(i * 128, (i + 1) * 128)
            oqkv_ref[:, cols(i, p, f)] = sqkv[p, f, :, part]
            oqkv_ref[:, cols(i, p, 1 - f)] = rqkv[p, :, part]
    vecs = vectors[0].finish(3)
    bqkv = vectors[1].finish(3)
    orows_ref[...] = cut(vecs, width // (2 * n), where, width)
    obqkv_ref[...] = cut(bqkv, bqkv.shape[1] // (2 * n), where, bqkv.shape[1])


def emit_body(dx_ref, up_ref, down_ref, out_ref, qkv_ref, rows_ref, bqkv_ref, bup_ref, *outs):
    odx, oup, odown, oout, oqkv, obqkv, obup = outs[:7]
    odx[...], oup[...], oout[...], oqkv[...] = dx_ref[...], up_ref[...], out_ref[...], qkv_ref[...]
    down = down_ref[...]
    odown[...] = down if odown.shape == down.shape else down.T
    obqkv[...] = bqkv_ref[:, : obqkv.shape[1]]
    obup[...] = bup_ref[:, : obup.shape[1]]
    for i, ref in enumerate(outs[7:]):
        ref[...] = rows_ref[i : i + 1, : ref.shape[1]]


def body(
    layer_input, ln1_gain, ln1_bias, w_qkv, b_qkv, w_out, b_out, ln2_gain, ln2_bias,
    w_up, b_up, w_down, b_down, feature_signs, match_blocks, match_count, out_grad,
):
    rows, width = layer_input.shape
    half_width = width // 2
    half_heads = HEADS // 2
    hidden = w_up.shape[1]
    f = lax.axis_index("feat")
    tokens = 2 * rows
    n = lax.axis_size("seq")
    chunk = width // n
    assert lax.axis_size("feat") == 2 and match_blocks.shape[0] == 1 and tokens == SEQLEN

    def swap(a):
        return lax.ppermute(a, "feat", [(0, 1), (1, 0)])

    def row(a):
        return a.reshape(1, -1)

    x = jnp.concatenate([layer_input, swap(layer_input)], axis=0)
    og = jnp.concatenate([out_grad, swap(out_grad)], axis=0)
    signs = (2 * feature_signs - 1).astype(BF)
    own_signs = lax.dynamic_slice_in_dim(signs, f * half_heads, half_heads, 0)
    far_signs = swap(lax.dynamic_slice_in_dim(signs, (1 - f) * half_heads, half_heads, 0))
    signs = jnp.concatenate([own_signs, far_signs], axis=2)
    feats = signs.shape[2]
    pairs = signs.reshape(half_heads // 2, 2, HEAD_DIM, feats)
    table = jnp.concatenate(
        [
            jnp.pad(pairs[:, 0], ((0, 0), (0, HEAD_DIM), (0, 0))),
            jnp.pad(pairs[:, 1], ((0, 0), (HEAD_DIM, 0), (0, 0))),
        ],
        axis=2,
    )
    lists = lax.dynamic_slice_in_dim(match_blocks[0], f * half_heads, half_heads, 0)
    counts = lax.dynamic_slice_in_dim(match_count[0], f * half_heads, half_heads, 0)
    used = jnp.arange(lists.shape[2], dtype=jnp.int32) < counts[..., None]
    shift = f * (NB // 2)
    block = (jnp.arange(NB, dtype=jnp.int32) + shift) % NB
    matched = jnp.any(used[..., None] & (lists[..., None] == block), axis=2)
    matched = jnp.where(f == 0, matched, jnp.roll(matched, NB // 2, axis=1)).astype(F32)
    tiled = (half_heads, tokens // TILE, TILE // BLOCK, tokens)
    marks = jnp.repeat(matched, BLOCK, axis=2).reshape(tiled)
    marks_t = jnp.repeat(matched.transpose(0, 2, 1), BLOCK, axis=2).reshape(tiled)

    def own_cols(a):
        return jnp.concatenate(
            [lax.dynamic_slice_in_dim(a, i * width + f * half_width, half_width, 1) for i in range(3)], axis=1
        )

    w_own, b_own = own_cols(w_qkv), own_cols(row(b_qkv))
    h1, qkv = call(
        qkv_body, [((tokens, width), BF), ((tokens, 3 * half_width), BF)],
        [x, row(ln1_gain), row(ln1_bias), w_own, b_own], name="qkv",
    )
    phi = pltpu.VMEM((tokens, feats), BF)
    att, den = call(
        att_body, [((tokens, half_width), BF), ((tokens, half_width), F32)], [qkv, table, marks],
        scratch=[phi, phi], name="att",
    )
    far = swap(att)
    att_far = jnp.concatenate([far[rows:], far[:rows]], axis=0)
    mixed, h2 = call(
        mix_body, [((tokens, width), F32), ((tokens, width), BF)],
        [x, att, att_far, w_out, row(b_out), row(ln2_gain), row(ln2_bias)], name="mix",
    )
    act, gp, hid, gh2, d_bup = call(
        ff_body,
        [((tokens, hidden), BF), ((tokens, hidden), BF), ((tokens, width), BF), ((tokens, width), BF), ((1, hidden), F32)],
        [h2, og, w_up, w_down, row(b_up)], name="ff",
    )
    gh_far = swap(gh2)
    gh_far = jnp.concatenate([gh_far[rows:], gh_far[:rows]], axis=0)
    hid_far = swap(hid[rows:])
    d_up, d_down = call(
        functools.partial(ffw_body, n), [((n, chunk, hidden), BF), ((n, chunk, hidden), BF)], [h2, og, act, gp],
        name="ffw",
    )
    gm, gatt, d_out, y, vec2 = call(
        functools.partial(outb_body, n),
        [
            ((rows, width), F32), ((tokens, half_width), F32), ((n, chunk, half_width), BF),
            ((rows, width), BF), ((8, width), F32),
        ],
        [gh2, gh_far, mixed, og, hid, hid_far, row(b_down), row(ln2_gain), w_out, att, att_far],
        scratch=[pltpu.VMEM((tokens, width), BF)], name="outb",
    )
    slots = sum(split(n)) + split(n)[0] - 3 + 1
    bufs = []
    for cols in (hidden, hidden, half_width, half_width, half_width, half_width):
        bufs += scatter_bufs(n, chunk, cols)
    half_chunk = chunk // 2
    sems = pltpu.SemaphoreType.DMA((10, slots))
    sums = call(
        functools.partial(back_body, n),
        [
            ((rows, width), F32), ((chunk, hidden), F32), ((chunk, hidden), F32), ((half_chunk, width), F32),
            ((half_chunk, 3 * width), F32), ((8, 128), F32), ((1, 128), F32), ((1, 128), F32),
        ],
        [
            qkv, table, marks_t, att, den, gatt, h1, w_own, layer_input, row(ln1_gain), gm, d_up, d_down, d_out, vec2, d_bup,
        ],
        scratch=bufs + [
            phi, phi, pltpu.VMEM((tokens, 128), BF), pltpu.VMEM((tokens, 128), F32), pltpu.VMEM((tokens, feats), F32),
            pltpu.VMEM((tokens, 3 * half_width), BF), pltpu.VMEM((3, n, chunk, half_width), BF),
            pltpu.VMEM((rows, width), BF), pltpu.VMEM((rows, width), BF),
            pltpu.VMEM((2, half_chunk, half_width), F32), pltpu.VMEM((half_chunk, half_width), F32),
            pltpu.VMEM((3, 2, half_chunk, half_width), F32), pltpu.VMEM((3, half_chunk, half_width), F32),
            pltpu.VMEM((4 + slots, 8, width), F32), pltpu.VMEM((4 + slots, 1, 3 * width), F32),
            pltpu.VMEM((4 + slots, 1, hidden), F32), sems, sems,
        ],
        name="back", net=1,
    )
    own = width // (2 * n)
    turn = chunk % 8 == 0
    dx, up, down, out, full, d_b, d_bup, *vec = call(
        emit_body,
        [
            ((rows, width), F32), ((chunk, hidden), F32), ((hidden, chunk) if turn else (chunk, hidden), F32),
            ((half_chunk, width), F32), ((half_chunk, 3 * width), F32), ((1, 3 * own), F32), ((1, hidden // n), F32),
        ] + [((1, own), F32)] * 6,
        sums, name="emit",
    )
    vec = [v.reshape(-1) for v in vec]
    return (
        y, dx, vec[0], vec[1], full, d_b.reshape(-1), out, vec[4], vec[2], vec[3], up, d_bup.reshape(-1),
        down if turn else down.T, vec[5],
    )


def solution(mesh):
    both = ("seq", "feat")
    return jax.shard_map(
        body,
        mesh=mesh,
        in_specs=(
            P(both, None), P(), P(), P(), P(), P(), P(), P(), P(), P(None, "feat"), P("feat"), P("feat", None), P(),
            P(None, None, "feat"), P("seq", None, None, None), P("seq", None, None), P(both, None),
        ),
        out_specs=(
            P(both, None), P(both, None), P(both), P(both), P(both, None), P(both), P(both, None), P(both), P(both),
            P(both), P("seq", "feat"), P(("feat", "seq")), P("feat", "seq"), P(both),
        ),
        check_vma=False,
    )
```

```python
import functools
import math

import jax
import jax.numpy as jnp
from jax import lax
from jax.experimental import pallas as pl
from jax.experimental.pallas import tpu as pltpu
from jax.sharding import PartitionSpec as P

HEADS = 12
HEAD_DIM = 64
BLOCK = 64
NB = 16
SEQLEN = NB * BLOCK
BF = jnp.bfloat16
F32 = jnp.float32
EPS = 1e-05
TILE = 256
ATILE = 512
BTILE = 512
GELU_A = math.sqrt(2.0 / math.pi)
GELU_B = 0.044715
MESH = pl.DeviceIdType.MESH
VMEM = pl.BlockSpec(memory_space=pltpu.VMEM)
ANY = pl.BlockSpec(memory_space=pl.ANY)


def nn(a, b):
    return lax.dot_general(a, b, (((1,), (0,)), ((), ())), preferred_element_type=F32)


def nt(a, b):
    return lax.dot_general(a, b, (((1,), (1,)), ((), ())), preferred_element_type=F32)


def tn(a, b):
    return lax.dot_general(a, b, (((0,), (0,)), ((), ())), preferred_element_type=F32)


def ds(i, n):
    return pl.ds(i * n if isinstance(i, int) else pl.multiple_of(i * n, n), n)


def norm(x):
    c = x - jnp.mean(x, axis=-1, keepdims=True)
    inv = lax.rsqrt(jnp.mean(c * c, axis=-1, keepdims=True) + EPS)
    return c * inv, inv


def norm_back(g, normed, inv, gain):
    a = g * gain
    return inv * (
        a
        - jnp.mean(a, axis=-1, keepdims=True)
        - normed * jnp.mean(a * normed, axis=-1, keepdims=True)
    )


def split(n):
    p = 1
    while 2 * (2 * p) ** 3 <= n:
        p *= 2
    assert n % (p * p) == 0
    return p, n // (p * p)


class Net:
    def __init__(self, n):
        p, self.nz = split(n)
        self.p = p
        self.s, self.f = lax.axis_index("seq"), lax.axis_index("feat")
        x, y = lax.rem(self.s, p), lax.rem(self.s // p, p)
        f = self.f
        self.sizes = (p, p, self.nz)
        self.at = (x + f * (y - x), y + f * (x - y), self.s // (p * p))
        self.strides = (1 + f * (p - 1), p + f * (1 - p), p * p)

    def place(self, dest):
        p = self.p
        x, y, z = lax.rem(dest, p), lax.rem(dest // p, p), dest // (p * p)
        f = self.f
        return ((x + f * (y - x)) * p + y + f * (x - y)) * self.nz + z

    def peer(self, phase, d):
        j = lax.rem(self.at[phase] + d, self.sizes[phase])
        return j, self.s + (j - self.at[phase]) * self.strides[phase]

    def barrier(self):
        sem = pltpu.get_barrier_semaphore()
        count = 1
        for phase in range(3):
            for d in range(1, self.sizes[phase]):
                pl.semaphore_signal(sem, inc=1, device_id={"seq": self.peer(phase, d)[1]}, device_id_type=MESH)
                count += 1
        pl.semaphore_signal(sem, inc=1, device_id={"feat": 1 - self.f}, device_id_type=MESH)
        pl.semaphore_wait(sem, count)

    def slot(self, phase, d):
        return sum(size - 1 for size in self.sizes[:phase]) + d - 1

    def slots(self):
        return self.slot(3, 1) + 1


def scatter_bufs(n, rows, cols):
    p, nz = split(n)
    return [
        pltpu.VMEM((p - 1, p * nz, rows, cols), BF),
        pltpu.VMEM((p * nz, rows, cols), BF),
        pltpu.VMEM((p - 1, nz, rows, cols), BF),
        pltpu.VMEM((nz, rows, cols), BF),
        pltpu.VMEM((nz - 1, 1, rows, cols), BF),
    ]


class Scatter:
    def __init__(self, net, src, bufs, send, recv):
        self.net, self.send, self.recv = net, send, recv
        self.hold = (src, bufs[1], bufs[3])
        self.got = (bufs[0], bufs[2], bufs[4])

    def block(self, phase, j):
        size = self.got[phase].shape[1]
        return pl.ds(j * size, size)

    def copies(self, phase):
        net, out = self.net, []
        for d in range(1, net.sizes[phase]):
            j, device = net.peer(phase, d)
            k = net.slot(phase, d)
            out.append(
                pltpu.make_async_remote_copy(
                    src_ref=self.hold[phase].at[self.block(phase, j)],
                    dst_ref=self.got[phase].at[d - 1],
                    send_sem=self.send.at[k],
                    recv_sem=self.recv.at[k],
                    device_id={"seq": device},
                    device_id_type=MESH,
                )
            )
        return out

    def start(self, phase):
        for copy in self.copies(phase):
            copy.start()

    def finish(self, phase, put=None):
        for copy in self.copies(phase):
            copy.wait()
        got, own = self.got[phase], self.hold[phase]
        size = got.shape[1]
        base = self.net.at[phase] * size

        def add(i, _):
            total = own[base + i].astype(F32)
            for d in range(got.shape[0]):
                total = total + got[d, i].astype(F32)
            if put is None:
                self.hold[phase + 1][i] = total.astype(BF)
            else:
                put(total)
            return 0

        lax.fori_loop(0, size, add, 0)


class Vector:
    def __init__(self, net, bufs, send, recv):
        self.net, self.bufs, self.send, self.recv = net, bufs, send, recv

    def copies(self, phase):
        net, out = self.net, []
        peers = [({"feat": 1 - net.f}, net.slots() - 1)]
        if phase < 3:
            peers = [({"seq": net.peer(phase, d)[1]}, net.slot(phase, d)) for d in range(1, net.sizes[phase])]
        for device, k in peers:
            out.append(
                pltpu.make_async_remote_copy(
                    src_ref=self.bufs.at[phase],
                    dst_ref=self.bufs.at[4 + k],
                    send_sem=self.send.at[k],
                    recv_sem=self.recv.at[k],
                    device_id=device,
                    device_id_type=MESH,
                )
            )
        return out

    def start(self, phase):
        for copy in self.copies(phase):
            copy.start()

    def finish(self, phase):
        for copy in self.copies(phase):
            copy.wait()
        first, count = (self.net.slots() - 1, 1) if phase == 3 else (self.net.slot(phase, 1), self.net.sizes[phase] - 1)
        total = self.bufs[phase]
        for k in range(count):
            total = total + self.bufs[4 + first + k]
        if phase < 3:
            self.bufs[phase + 1] = total
        return total


def call(body, outs, ins, specs=None, scratch=(), name=None, net=None):
    return pl.pallas_call(
        body,
        out_shape=[jax.ShapeDtypeStruct(s, d) for s, d in outs],
        in_specs=specs or [VMEM] * len(ins),
        out_specs=[VMEM] * len(outs),
        scratch_shapes=list(scratch),
        compiler_params=pltpu.CompilerParams(
            vmem_limit_bytes=64000 * 1024, collective_id=net, has_side_effects=net is not None
        ),
        name=name,
    )(*ins)


def qkv_body(x_ref, g_ref, s_ref, w_ref, b_ref, h_ref, qkv_ref):
    gain = g_ref[...].astype(F32)
    shift = s_ref[...].astype(F32)
    bias = b_ref[...].astype(F32)

    def step(i, _):
        rows = ds(i, TILE)
        normed, _inv = norm(x_ref[rows, :].astype(F32))
        h = (normed * gain + shift).astype(BF)
        h_ref[rows, :] = h
        qkv_ref[rows, :] = (nn(h, w_ref[...]) + bias).astype(BF)
        return 0

    lax.fori_loop(0, x_ref.shape[0] // TILE, step, 0)


def head_parts(qkv_ref, h):
    own = qkv_ref.shape[1] // 3
    p, e = h // 2, h % 2
    lane = lax.broadcasted_iota(jnp.int32, (1, 128), 1)
    mine = (lane // HEAD_DIM) == e

    def cols(part):
        return pl.ds(pl.multiple_of(part * own + p * 128, 128), 128)

    return p, e, lane, mine, cols


def lift_all(qkv_ref, s_ref, h, pq_ref, pk_ref):
    p, e, lane, mine, cols = head_parts(qkv_ref, h)
    feats = pq_ref.shape[1]
    signs = s_ref[p, :, ds(e, feats)]

    def step(i, _):
        rows = ds(i, TILE)
        for part, out in ((0, pq_ref), (1, pk_ref)):
            t = qkv_ref[rows, cols(part)]
            w = jnp.where(mine, t.astype(F32), 0.0)
            sq = jnp.sum(w * w, axis=-1, keepdims=True) * (0.5 * HEAD_DIM ** (-0.5))
            lifted = nn(t, signs) * HEAD_DIM ** (-0.25)
            out[rows, :] = (jnp.exp(lifted - sq) * feats ** (-0.5)).astype(BF)
        return 0

    lax.fori_loop(0, qkv_ref.shape[0] // TILE, step, 0)


def att_body(qkv_ref, s_ref, m_ref, att_ref, den_ref, pq_ref, pk_ref):
    def head(h, _):
        p, e, lane, mine, cols = head_parts(qkv_ref, h)
        lift_all(qkv_ref, s_ref, h, pq_ref, pk_ref)
        zero = jnp.zeros((), BF)
        v_one = jnp.where(mine, qkv_ref[:, cols(2)], jnp.ones((), BF))

        def step(i, _):
            rows = ds(i, ATILE)
            q = jnp.where(mine, qkv_ref[rows, cols(0)] * BF(HEAD_DIM ** (-0.5)), zero)
            ex = jnp.exp(nt(q, qkv_ref[:, cols(1)]))
            low = nt(pq_ref[rows, :], pk_ref[...])
            per = ATILE // BLOCK
            marks = m_ref[h, i]
            probs = jnp.concatenate(
                [
                    jnp.where(
                        marks[j : j + 1, :] > 0.5,
                        ex[j * BLOCK : (j + 1) * BLOCK],
                        low[j * BLOCK : (j + 1) * BLOCK],
                    )
                    for j in range(per)
                ],
                axis=0,
            ).astype(BF)
            both = nn(probs, v_one)
            den = pltpu.roll(both, HEAD_DIM, 1)
            out_cols = ds(p, 128)
            att = (both / den).astype(BF)
            att_ref[rows, out_cols] = jnp.where(mine, att, att_ref[rows, out_cols])
            den_ref[rows, out_cols] = jnp.where(mine, den, den_ref[rows, out_cols])
            return 0

        lax.fori_loop(0, qkv_ref.shape[0] // ATILE, step, 0)
        return 0

    lax.fori_loop(0, qkv_ref.shape[1] // (3 * HEAD_DIM), head, 0)


def mix_tiles(x_ref, mine_ref, other_ref, w_ref, b_ref, g_ref, s_ref, mixed_ref, h_ref):
    f = lax.axis_index("feat")
    half = mine_ref.shape[1]

    def step(i, _):
        rows = ds(i, TILE)
        mixed = (
            x_ref[rows, :].astype(F32)
            + nn(mine_ref[rows, :], w_ref[ds(f, half), :])
            + nn(other_ref[rows, :], w_ref[ds(1 - f, half), :])
            + b_ref[...].astype(F32)
        )
        mixed_ref[rows, :] = mixed
        normed, _inv = norm(mixed)
        h_ref[rows, :] = (normed * g_ref[...].astype(F32) + s_ref[...].astype(F32)).astype(BF)
        return 0

    lax.fori_loop(0, x_ref.shape[0] // TILE, step, 0)


def ff_tiles(h_ref, og_ref, up_ref, down_ref, b_ref, act_ref, gp_ref, hid_ref, gh_ref, db_ref, send):
    tiles = h_ref.shape[0] // TILE
    db_ref[...] = jnp.zeros_like(db_ref)

    def step(i, _):
        tile = lax.rem(i + tiles // 2, tiles)
        rows = ds(tile, TILE)
        v = nn(h_ref[rows, :], up_ref[...]) + b_ref[...].astype(F32)
        vv = v * v
        th = jnp.tanh(GELU_A * v * (1.0 + GELU_B * vv))
        half = 0.5 + 0.5 * th
        act = (v * half).astype(BF)
        slope = half + (0.5 * GELU_A) * v * (1.0 - th * th) * (1.0 + (3.0 * GELU_B) * vv)
        act_ref[rows, :] = act
        hid_ref[rows, :] = nn(act, down_ref[...]).astype(BF)
        gp = nt(og_ref[rows, :], down_ref[...]) * slope
        gpl = gp.astype(BF)
        gp_ref[rows, :] = gpl
        db_ref[...] += jnp.sum(gpl.astype(F32), axis=0, keepdims=True)
        gh_ref[rows, :] = nt(gpl, up_ref[...]).astype(BF)
        send(i, tile)
        return 0

    lax.fori_loop(0, tiles, step, 0)


def put_chunks(out_ref, first, value, net):
    rows = out_ref.shape[1]
    for i in range(value.shape[0] // rows):
        out_ref[net.place(first + i)] = value[i * rows : (i + 1) * rows].astype(BF)


def ff_weights(n, h_ref, og_ref, act_ref, gp_ref, up_ref, down_ref):
    net = Net(n)
    wide = h_ref.shape[1] // 2
    per = wide // up_ref.shape[1]

    def step(i, _):
        rows = ds(i, wide)
        put_chunks(up_ref, i * per, tn(h_ref[:, rows], gp_ref[...]), net)
        put_chunks(down_ref, i * per, tn(og_ref[:, rows], act_ref[...]), net)
        return 0

    lax.fori_loop(0, 2, step, 0)


def out_back(
    n, gh_ref, gho_ref, mixed_ref, og_ref, hid_ref, hido_ref, bd_ref, g_ref, w_ref, mine_ref, other_ref,
    gm_ref, gatt_ref, dw_ref, y_ref, vec_ref, gb_ref,
):
    f = lax.axis_index("feat")
    half = mine_ref.shape[1]
    tiles = mixed_ref.shape[0] // TILE
    own = tiles // 2
    gain = g_ref[...].astype(F32)
    vec_ref[...] = jnp.zeros_like(vec_ref)

    def step(i, _):
        rows = ds(i, TILE)
        mixed = mixed_ref[rows, :]
        og = og_ref[rows, :].astype(F32)
        normed, inv = norm(mixed)
        g = gh_ref[rows, :].astype(F32) + gho_ref[rows, :].astype(F32)
        gm = og + norm_back(g, normed, inv, gain)
        gb = gm.astype(BF)
        gb_ref[rows, :] = gb
        gatt_ref[rows, :] = nt(gb, w_ref[ds(f, half), :])

        @pl.when(i < own)
        def _():
            gm_ref[rows, :] = gm
            y_ref[rows, :] = (
                mixed + hid_ref[rows, :].astype(F32) + hido_ref[rows, :].astype(F32) + bd_ref[...].astype(F32)
            ).astype(BF)
            for j, term in enumerate((g * normed, g, gb.astype(F32), og)):
                vec_ref[j + 2 : j + 3, :] += jnp.sum(term, axis=0, keepdims=True)

        return 0

    lax.fori_loop(0, tiles, step, 0)
    gb_own = gb_ref[:, ds(f, half)]
    net = Net(n)
    per = half // dw_ref.shape[1]
    put_chunks(dw_ref, f * per, tn(mine_ref[...], gb_own), net)
    put_chunks(dw_ref, (1 - f) * per, tn(other_ref[...], gb_own), net)


def mid_body(
    n, x_ref, att_ref, wout_ref, bout_ref, g_ref, s_ref, og_own_ref, up_ref, down_ref, bup_ref, bdown_ref,
    gm_ref, gatt_ref, dout_ref, y_ref, vec_ref, dup_ref, ddown_ref, dbup_ref,
    far, og, mixed, h, act, gp, hid, gh, hid_got, gh_got, gb, send, recv,
):
    rows = og_own_ref.shape[0]
    tiles = h.shape[0] // TILE
    other = {"feat": 1 - lax.axis_index("feat")}

    def copy(k, src, dst):
        return pltpu.make_async_remote_copy(
            src_ref=src, dst_ref=dst, send_sem=send.at[k], recv_sem=recv.at[k], device_id=other, device_id_type=MESH
        )

    barrier = pltpu.get_barrier_semaphore()
    pl.semaphore_signal(barrier, inc=1, device_id=other, device_id_type=MESH)
    pl.semaphore_wait(barrier, 1)
    low, high = pl.ds(0, rows), pl.ds(rows, rows)
    atts = [copy(0, att_ref.at[low], far.at[high]), copy(1, att_ref.at[high], far.at[low])]
    og_copy = copy(2, og_own_ref, og.at[high])
    for c in atts:
        c.start()
    og_copy.start()
    og[low, :] = og_own_ref[...]
    for c in atts:
        c.wait()
    mix_tiles(x_ref, att_ref, far, wout_ref, bout_ref, g_ref, s_ref, mixed, h)
    og_copy.wait()

    def gh_copy(i, tile):
        return copy(3 + i, gh.at[ds(tile, TILE)], gh_got.at[ds(i, TILE)])

    def hid_copy(i, tile):
        return copy(3 + tiles + i, hid.at[ds(tile, TILE)], hid_got.at[ds(i, TILE)])

    def send_tile(i, tile):
        gh_copy(i, tile).start()

        @pl.when(i < tiles // 2)
        def _():
            hid_copy(i, tile).start()

    ff_tiles(h, og, up_ref, down_ref, bup_ref, act, gp, hid, gh, dbup_ref, send_tile)
    ff_weights(n, h, og, act, gp, dup_ref, ddown_ref)
    for i in range(tiles):
        gh_copy(i, (i + tiles // 2) % tiles).wait()
    for i in range(tiles // 2):
        hid_copy(i, i + tiles // 2).wait()
    out_back(
        n, gh, gh_got, mixed, og, hid, hid_got, bdown_ref, g_ref, wout_ref, att_ref, far,
        gm_ref, gatt_ref, dout_ref, y_ref, vec_ref, gb,
    )


def heads_back(
    qkv_ref, s_ref, m_ref, att_ref, den_ref, gatt_ref, gqkv_ref, pq_ref, pk_ref, gn_ref, gq_ref, gpq_ref, after
):
    rows_all = qkv_ref.shape[0]
    scale = HEAD_DIM ** (-0.5)

    def head(h, _):
        p, e, lane, mine, cols = head_parts(qkv_ref, h)
        feats = pq_ref.shape[1]
        zero = jnp.zeros((), BF)
        lift_all(qkv_ref, s_ref, h, pq_ref, pk_ref)
        first_other = (1 - e) * HEAD_DIM

        def prep(i, _):
            rows = ds(i, TILE)
            inv = 1.0 / den_ref[rows, ds(p, 128)]
            ga = jnp.where(mine, gatt_ref[rows, ds(p, 128)] * inv, 0.0)
            gd = -jnp.sum(ga * att_ref[rows, ds(p, 128)].astype(F32), axis=-1, keepdims=True)
            gn_ref[rows, :] = jnp.where(lane == first_other, gd, ga).astype(BF)
            return 0

        lax.fori_loop(0, rows_all // TILE, prep, 0)
        gq_ref[...] = jnp.zeros_like(gq_ref)
        gpq_ref[...] = jnp.zeros_like(gpq_ref)
        signs = s_ref[p, :, ds(e, feats)]

        def lift_back(t, raw, g_phi):
            gl = g_phi * raw.astype(F32)
            gt = nt(gl.astype(BF), signs) * HEAD_DIM ** (-0.25)
            return gt - jnp.sum(gl, axis=-1, keepdims=True) * (scale * t.astype(F32))

        def put(part, rows, value):
            gqkv_ref[rows, cols(part)] = jnp.where(mine, value.astype(BF), gqkv_ref[rows, cols(part)])

        def step(i, _):
            rows = ds(i, BTILE)
            k = jnp.where(mine, qkv_ref[rows, cols(1)] * BF(scale), zero)
            v_one = jnp.where(mine, qkv_ref[rows, cols(2)], jnp.ones((), BF))
            q_all = qkv_ref[:, cols(0)]
            pk = pk_ref[rows, :]
            ex = jnp.exp(nt(k, q_all))
            low = nt(pk, pq_ref[...])
            da = nt(v_one, gn_ref[...])
            per = BTILE // BLOCK
            marks = m_ref[h, i]
            probs, dl, gs = [], [], []
            for j in range(per):
                part = slice(j * BLOCK, (j + 1) * BLOCK)
                on = marks[j : j + 1, :] > 0.5
                exj, daj = ex[part], da[part]
                probs.append(jnp.where(on, exj, low[part]))
                dl.append(jnp.where(on, 0.0, daj))
                gs.append(jnp.where(on, daj * exj, 0.0))
            probs = jnp.concatenate(probs, axis=0).astype(BF)
            dl = jnp.concatenate(dl, axis=0).astype(BF)
            gs = jnp.concatenate(gs, axis=0).astype(BF)
            put(2, rows, nn(probs, gn_ref[...]))
            g_phi_k = nn(dl, pq_ref[...])
            gk = nn(gs, q_all) * scale + lift_back(qkv_ref[rows, cols(1)], pk, g_phi_k)
            put(1, rows, gk)
            gpq_ref[...] += tn(dl, pk)
            gq_ref[...] += tn(gs, k)
            return 0

        lax.fori_loop(0, rows_all // BTILE, step, 0)

        def last(i, _):
            rows = ds(i, TILE)
            gq = gq_ref[rows, :] + lift_back(qkv_ref[rows, cols(0)], pq_ref[rows, :], gpq_ref[rows, :])
            put(0, rows, gq)
            return 0

        lax.fori_loop(0, rows_all // TILE, last, 0)
        for k, then in after.items():
            pl.when(h == k)(then)
        return 0

    lax.fori_loop(0, qkv_ref.shape[1] // (3 * HEAD_DIM), head, 0)


def back_body(
    n, qkv_ref, s_ref, m_ref, att_ref, den_ref, gatt_ref, h_ref, w_ref, x_ref, g_ref, gm_ref, up_ref, down_ref, out_ref,
    vec_ref, bup_ref, dx_ref, oup_ref, odown_ref, oout_ref, oqkv_ref, orows_ref, obqkv_ref, obup_ref, *scratch,
):
    net = Net(n)
    bufs, tail = scratch[:30], scratch[30:]
    pq, pk, gn, gq, gpq, gqkv, gw, gh_send, gh_got, sout, rout, sqkv, rqkv, vrows, vbqkv, vbup, send, recv = tail
    f = net.f
    other = {"feat": 1 - f}
    parts = [
        Scatter(net, src, bufs[5 * i : 5 * i + 5], send.at[i], recv.at[i])
        for i, src in enumerate((down_ref, up_ref, out_ref, gw.at[0], gw.at[1], gw.at[2]))
    ]
    down, up, out = parts[:3]
    pairs = parts[3:]
    vectors = [Vector(net, ref, send.at[6 + i], recv.at[6 + i]) for i, ref in enumerate((vrows, vbqkv, vbup))]
    last = net.slots() - 1
    half = sout.shape[1]
    rows = x_ref.shape[0]
    width = x_ref.shape[1]
    own = width // 2
    lanes = orows_ref.shape[1]

    def whole(ref):
        def put(total):
            ref[...] = total

        return put

    def halves(ref):
        def put(total):
            ref[0], ref[1] = total[:half], total[half:]

        return put

    def swap(i, src, dst):
        return pltpu.make_async_remote_copy(
            src_ref=src, dst_ref=dst, send_sem=send.at[i, last], recv_sem=recv.at[i, last],
            device_id=other, device_id_type=MESH,
        )

    def move(part, phase):
        part.finish(phase)
        part.start(phase + 1)

    def weight(p):
        g = jnp.concatenate([gqkv[:, i * own + p * 128 : i * own + (p + 1) * 128] for i in range(3)], axis=1)
        per = own // gw.shape[2]
        for i in range(2):
            put_chunks(gw.at[p], i * per, tn(h_ref[:, i * own : (i + 1) * own], g), net)
        pairs[p].start(0)

    net.barrier()
    for part in (down, up, out):
        part.start(0)

    def after1():
        move(down, 0)
        weight(0)

    def after2():
        move(up, 0)
        move(out, 0)

    def after3():
        move(down, 1)
        move(pairs[0], 0)
        weight(1)

    def after4():
        move(up, 1)
        move(out, 1)
        move(pairs[0], 1)

    heads_back(
        qkv_ref, s_ref, m_ref, att_ref, den_ref, gatt_ref, gqkv, pq, pk, gn, gq, gpq,
        {1: after1, 2: after2, 3: after3, 4: after4},
    )
    weight(2)
    tiles = rows // TILE

    def far(i, total):
        g = gqkv[ds(tiles + i, TILE), :]
        gh_send[ds(i, TILE), :] = nt(g, w_ref[...]).astype(BF)
        return total + jnp.sum(g.astype(F32), axis=0, keepdims=True)

    total = lax.fori_loop(0, tiles, far, jnp.zeros((1, 3 * own), F32))
    gh_swap = swap(9, gh_send, gh_got)
    gh_swap.start()
    move(pairs[1], 0)

    def sums(i, total):
        return total + jnp.sum(gqkv[ds(i, TILE), :].astype(F32), axis=0, keepdims=True)

    total = lax.fori_loop(0, tiles, sums, total)
    vbqkv[0] = jnp.zeros_like(vbqkv[0])
    for i in range(3):
        vbqkv[0, :, ds(2 * i + f, own)] = total[:, i * own : (i + 1) * own]
    vbup[0] = bup_ref[...]
    down.finish(2, whole(odown_ref))
    out.finish(2, halves(sout))
    out_swap = swap(2, sout.at[1 - f], rout)
    out_swap.start()
    up.finish(2, whole(oup_ref))
    move(pairs[1], 1)
    move(pairs[2], 0)
    gh_swap.wait()
    gain = g_ref[...].astype(F32)
    vrows[0] = vec_ref[...]

    def norm1(i, _):
        r = ds(i, TILE)
        normed, inv = norm(x_ref[r, :].astype(F32))
        g = nt(gqkv[r, :], w_ref[...]) + gh_got[r, :].astype(F32)
        dx_ref[r, :] = gm_ref[r, :] + norm_back(g, normed, inv, gain)
        vrows[0, 0:1, :] += jnp.sum(g * normed, axis=0, keepdims=True)
        vrows[0, 1:2, :] += jnp.sum(g, axis=0, keepdims=True)
        return 0

    lax.fori_loop(0, tiles, norm1, 0)
    for v in vectors:
        v.start(0)
    move(pairs[2], 1)
    for p in (0, 1):
        pairs[p].finish(2, halves(sqkv.at[p]))
    for v in vectors:
        v.finish(0)
        v.start(1)
    swaps = [swap(3 + p, sqkv.at[p, 1 - f], rqkv.at[p]) for p in range(3)]
    swaps[0].start()
    swaps[1].start()
    for v in vectors:
        v.finish(1)
        v.start(2)
    pairs[2].finish(2, halves(sqkv.at[2]))
    swaps[2].start()
    vecs, bqkv, bup = [v.finish(2) for v in vectors]
    vectors[0].start(3)
    vectors[1].start(3)
    where = 2 * net.s + f

    def cut(value, per, index, size):
        return pltpu.roll(value, lax.rem(size - index * per, size), 1)[:, :lanes]

    obup_ref[...] = cut(bup, bup.shape[1] // n, net.s, bup.shape[1])
    out_swap.wait()
    oout_ref[:, ds(f, own)] = sout[f]
    oout_ref[:, ds(1 - f, own)] = rout[...]

    def cols(i, p, side):
        return pl.ds(pl.multiple_of(i * width + side * own + p * 128, 128), 128)

    for p in range(3):
        swaps[p].wait()
        for i in range(3):
            part = slice(i * 128, (i + 1) * 128)
            oqkv_ref[:, cols(i, p, f)] = sqkv[p, f, :, part]
            oqkv_ref[:, cols(i, p, 1 - f)] = rqkv[p, :, part]
    vecs = vectors[0].finish(3)
    bqkv = vectors[1].finish(3)
    orows_ref[...] = cut(vecs, width // (2 * n), where, width)
    obqkv_ref[...] = cut(bqkv, bqkv.shape[1] // (2 * n), where, bqkv.shape[1])


def emit_body(dx_ref, up_ref, down_ref, out_ref, qkv_ref, rows_ref, bqkv_ref, bup_ref, *outs):
    odx, oup, odown, oout, oqkv, obqkv, obup = outs[:7]
    odx[...], oup[...], oout[...], oqkv[...] = dx_ref[...], up_ref[...], out_ref[...], qkv_ref[...]
    down = down_ref[...]
    odown[...] = down if odown.shape == down.shape else down.T
    obqkv[...] = bqkv_ref[:, : obqkv.shape[1]]
    obup[...] = bup_ref[:, : obup.shape[1]]
    for i, ref in enumerate(outs[7:]):
        ref[...] = rows_ref[i : i + 1, : ref.shape[1]]


def body(
    layer_input, ln1_gain, ln1_bias, w_qkv, b_qkv, w_out, b_out, ln2_gain, ln2_bias,
    w_up, b_up, w_down, b_down, feature_signs, match_blocks, match_count, out_grad,
):
    rows, width = layer_input.shape
    half_width = width // 2
    half_heads = HEADS // 2
    hidden = w_up.shape[1]
    f = lax.axis_index("feat")
    tokens = 2 * rows
    n = lax.axis_size("seq")
    chunk = width // n
    assert lax.axis_size("feat") == 2 and match_blocks.shape[0] == 1 and tokens == SEQLEN

    def swap(a):
        return lax.ppermute(a, "feat", [(0, 1), (1, 0)])

    def row(a):
        return a.reshape(1, -1)

    x = jnp.concatenate([layer_input, swap(layer_input)], axis=0)
    signs = (2 * feature_signs - 1).astype(BF)
    own_signs = lax.dynamic_slice_in_dim(signs, f * half_heads, half_heads, 0)
    far_signs = swap(lax.dynamic_slice_in_dim(signs, (1 - f) * half_heads, half_heads, 0))
    signs = jnp.concatenate([own_signs, far_signs], axis=2)
    feats = signs.shape[2]
    pairs = signs.reshape(half_heads // 2, 2, HEAD_DIM, feats)
    table = jnp.concatenate(
        [
            jnp.pad(pairs[:, 0], ((0, 0), (0, HEAD_DIM), (0, 0))),
            jnp.pad(pairs[:, 1], ((0, 0), (HEAD_DIM, 0), (0, 0))),
        ],
        axis=2,
    )
    lists = lax.dynamic_slice_in_dim(match_blocks[0], f * half_heads, half_heads, 0)
    counts = lax.dynamic_slice_in_dim(match_count[0], f * half_heads, half_heads, 0)
    used = jnp.arange(lists.shape[2], dtype=jnp.int32) < counts[..., None]
    shift = f * (NB // 2)
    block = (jnp.arange(NB, dtype=jnp.int32) + shift) % NB
    matched = jnp.any(used[..., None] & (lists[..., None] == block), axis=2)
    matched = jnp.where(f == 0, matched, jnp.roll(matched, NB // 2, axis=1)).astype(F32)

    def spread(a, tile):
        return jnp.repeat(a, BLOCK, axis=2).reshape(half_heads, tokens // tile, tile // BLOCK, tokens)

    marks, marks_t = spread(matched, ATILE), spread(matched.transpose(0, 2, 1), BTILE)

    def own_cols(a):
        return jnp.concatenate(
            [lax.dynamic_slice_in_dim(a, i * width + f * half_width, half_width, 1) for i in range(3)], axis=1
        )

    w_own, b_own = own_cols(w_qkv), own_cols(row(b_qkv))
    h1, qkv = call(
        qkv_body, [((tokens, width), BF), ((tokens, 3 * half_width), BF)],
        [x, row(ln1_gain), row(ln1_bias), w_own, b_own], name="qkv",
    )
    phi = pltpu.VMEM((tokens, feats), BF)
    att, den = call(
        att_body, [((tokens, half_width), BF), ((tokens, half_width), F32)], [qkv, table, marks],
        scratch=[phi, phi], name="att",
    )
    big, wide = pltpu.VMEM((tokens, width), BF), pltpu.VMEM((tokens, hidden), BF)
    pair_sems = pltpu.SemaphoreType.DMA((3 + tokens // TILE + rows // TILE,))
    gm, gatt, d_out, y, vec2, d_up, d_down, d_bup = call(
        functools.partial(mid_body, n),
        [
            ((rows, width), F32), ((tokens, half_width), F32), ((n, chunk, half_width), BF), ((rows, width), BF),
            ((8, width), F32), ((n, chunk, hidden), BF), ((n, chunk, hidden), BF), ((1, hidden), F32),
        ],
        [
            x, att, w_out, row(b_out), row(ln2_gain), row(ln2_bias), out_grad, w_up, w_down, row(b_up), row(b_down),
        ],
        scratch=[
            pltpu.VMEM((tokens, half_width), BF), big, pltpu.VMEM((tokens, width), F32), big, wide, wide, big, big,
            pltpu.VMEM((rows, width), BF), big, big, pair_sems, pair_sems,
        ],
        name="mid", net=2,
    )
    slots = sum(split(n)) + split(n)[0] - 3 + 1
    bufs = []
    for cols in (hidden, hidden, half_width, half_width, half_width, half_width):
        bufs += scatter_bufs(n, chunk, cols)
    half_chunk = chunk // 2
    sems = pltpu.SemaphoreType.DMA((10, slots))
    sums = call(
        functools.partial(back_body, n),
        [
            ((rows, width), F32), ((chunk, hidden), F32), ((chunk, hidden), F32), ((half_chunk, width), F32),
            ((half_chunk, 3 * width), F32), ((8, 128), F32), ((1, 128), F32), ((1, 128), F32),
        ],
        [
            qkv, table, marks_t, att, den, gatt, h1, w_own, layer_input, row(ln1_gain), gm, d_up, d_down, d_out, vec2, d_bup,
        ],
        scratch=bufs + [
            phi, phi, pltpu.VMEM((tokens, 128), BF), pltpu.VMEM((tokens, 128), F32), pltpu.VMEM((tokens, feats), F32),
            pltpu.VMEM((tokens, 3 * half_width), BF), pltpu.VMEM((3, n, chunk, half_width), BF),
            pltpu.VMEM((rows, width), BF), pltpu.VMEM((rows, width), BF),
            pltpu.VMEM((2, half_chunk, half_width), F32), pltpu.VMEM((half_chunk, half_width), F32),
            pltpu.VMEM((3, 2, half_chunk, half_width), F32), pltpu.VMEM((3, half_chunk, half_width), F32),
            pltpu.VMEM((4 + slots, 8, width), F32), pltpu.VMEM((4 + slots, 1, 3 * width), F32),
            pltpu.VMEM((4 + slots, 1, hidden), F32), sems, sems,
        ],
        name="back", net=1,
    )
    own = width // (2 * n)
    turn = chunk % 8 == 0
    dx, up, down, out, full, d_b, d_bup, *vec = call(
        emit_body,
        [
            ((rows, width), F32), ((chunk, hidden), F32), ((hidden, chunk) if turn else (chunk, hidden), F32),
            ((half_chunk, width), F32), ((half_chunk, 3 * width), F32), ((1, 3 * own), F32), ((1, hidden // n), F32),
        ] + [((1, own), F32)] * 6,
        sums, name="emit",
    )
    vec = [v.reshape(-1) for v in vec]
    return (
        y, dx, vec[0], vec[1], full, d_b.reshape(-1), out, vec[4], vec[2], vec[3], up, d_bup.reshape(-1),
        down if turn else down.T, vec[5],
    )


def solution(mesh):
    both = ("seq", "feat")
    return jax.shard_map(
        body,
        mesh=mesh,
        in_specs=(
            P(both, None), P(), P(), P(), P(), P(), P(), P(), P(), P(None, "feat"), P("feat"), P("feat", None), P(),
            P(None, None, "feat"), P("seq", None, None, None), P("seq", None, None), P(both, None),
        ),
        out_specs=(
            P(both, None), P(both, None), P(both), P(both), P(both, None), P(both), P(both, None), P(both), P(both),
            P(both), P("seq", "feat"), P(("feat", "seq")), P("feat", "seq"), P(both),
        ),
        check_vma=False,
    )
```

```python
import functools
import math

import jax
import jax.numpy as jnp
from jax import lax
from jax.experimental import pallas as pl
from jax.experimental.pallas import tpu as pltpu
from jax.sharding import PartitionSpec as P

HEADS = 12
HEAD_DIM = 64
BLOCK = 64
NB = 16
SEQLEN = NB * BLOCK
BF = jnp.bfloat16
F32 = jnp.float32
EPS = 1e-05
TILE = 256
ATILE = 512
BTILE = 512
GELU_A = math.sqrt(2.0 / math.pi)
GELU_B = 0.044715
GAIN1, BIAS1, BOUT, GAIN2, BIAS2, BDOWN, BQKV, BUP = 0, 1, 2, 3, 4, 5, 6, 9
MESH = pl.DeviceIdType.MESH
VMEM = pl.BlockSpec(memory_space=pltpu.VMEM)
ANY = pl.BlockSpec(memory_space=pl.ANY)


def nn(a, b):
    return lax.dot_general(a, b, (((1,), (0,)), ((), ())), preferred_element_type=F32)


def nt(a, b):
    return lax.dot_general(a, b, (((1,), (1,)), ((), ())), preferred_element_type=F32)


def tn(a, b):
    return lax.dot_general(a, b, (((0,), (0,)), ((), ())), preferred_element_type=F32)


def ds(i, n):
    return pl.ds(i * n if isinstance(i, int) else pl.multiple_of(i * n, n), n)


def norm(x):
    c = x - jnp.mean(x, axis=-1, keepdims=True)
    inv = lax.rsqrt(jnp.mean(c * c, axis=-1, keepdims=True) + EPS)
    return c * inv, inv


def norm_back(g, normed, inv, gain):
    a = g * gain
    return inv * (
        a
        - jnp.mean(a, axis=-1, keepdims=True)
        - normed * jnp.mean(a * normed, axis=-1, keepdims=True)
    )


def split(n):
    p = 1
    while 2 * (2 * p) ** 3 <= n:
        p *= 2
    assert n % (p * p) == 0
    return p, n // (p * p)


class Net:
    def __init__(self, n):
        p, self.nz = split(n)
        self.p = p
        self.s, self.f = lax.axis_index("seq"), lax.axis_index("feat")
        x, y = lax.rem(self.s, p), lax.rem(self.s // p, p)
        f = self.f
        self.sizes = (p, p, self.nz)
        self.at = (x + f * (y - x), y + f * (x - y), self.s // (p * p))
        self.strides = (1 + f * (p - 1), p + f * (1 - p), p * p)

    def place(self, dest):
        p = self.p
        x, y, z = lax.rem(dest, p), lax.rem(dest // p, p), dest // (p * p)
        f = self.f
        return ((x + f * (y - x)) * p + y + f * (x - y)) * self.nz + z

    def peer(self, phase, d):
        j = lax.rem(self.at[phase] + d, self.sizes[phase])
        return j, self.s + (j - self.at[phase]) * self.strides[phase]

    def barrier(self):
        sem = pltpu.get_barrier_semaphore()
        count = 1
        for phase in range(3):
            for d in range(1, self.sizes[phase]):
                pl.semaphore_signal(sem, inc=1, device_id={"seq": self.peer(phase, d)[1]}, device_id_type=MESH)
                count += 1
        pl.semaphore_signal(sem, inc=1, device_id={"feat": 1 - self.f}, device_id_type=MESH)
        pl.semaphore_wait(sem, count)

    def slot(self, phase, d):
        return sum(size - 1 for size in self.sizes[:phase]) + d - 1

    def slots(self):
        return self.slot(3, 1) + 1


def scatter_bufs(n, rows, cols):
    p, nz = split(n)
    return [
        pltpu.VMEM((p - 1, p * nz, rows, cols), BF),
        pltpu.VMEM((p * nz, rows, cols), BF),
        pltpu.VMEM((p - 1, nz, rows, cols), BF),
        pltpu.VMEM((nz, rows, cols), BF),
        pltpu.VMEM((nz - 1, 1, rows, cols), BF),
    ]


class Scatter:
    def __init__(self, net, src, bufs, send, recv):
        self.net, self.send, self.recv = net, send, recv
        self.hold = (src, bufs[1], bufs[3])
        self.got = (bufs[0], bufs[2], bufs[4])

    def block(self, phase, j):
        size = self.got[phase].shape[1]
        return pl.ds(j * size, size)

    def copies(self, phase):
        net, out = self.net, []
        for d in range(1, net.sizes[phase]):
            j, device = net.peer(phase, d)
            k = net.slot(phase, d)
            out.append(
                pltpu.make_async_remote_copy(
                    src_ref=self.hold[phase].at[self.block(phase, j)],
                    dst_ref=self.got[phase].at[d - 1],
                    send_sem=self.send.at[k],
                    recv_sem=self.recv.at[k],
                    device_id={"seq": device},
                    device_id_type=MESH,
                )
            )
        return out

    def start(self, phase):
        for copy in self.copies(phase):
            copy.start()

    def finish(self, phase, put=None):
        for copy in self.copies(phase):
            copy.wait()
        got, own = self.got[phase], self.hold[phase]
        size = got.shape[1]
        base = self.net.at[phase] * size

        def add(i, _):
            total = own[base + i].astype(F32)
            for d in range(got.shape[0]):
                total = total + got[d, i].astype(F32)
            if put is None:
                self.hold[phase + 1][i] = total.astype(BF)
            else:
                put(total)
            return 0

        lax.fori_loop(0, size, add, 0)


class Vector:
    def __init__(self, net, bufs, send, recv):
        self.net, self.bufs, self.send, self.recv = net, bufs, send, recv

    def copies(self, phase):
        net, out = self.net, []
        peers = [({"feat": 1 - net.f}, net.slots() - 1)]
        if phase < 3:
            peers = [({"seq": net.peer(phase, d)[1]}, net.slot(phase, d)) for d in range(1, net.sizes[phase])]
        for device, k in peers:
            out.append(
                pltpu.make_async_remote_copy(
                    src_ref=self.bufs.at[phase],
                    dst_ref=self.bufs.at[4 + k],
                    send_sem=self.send.at[k],
                    recv_sem=self.recv.at[k],
                    device_id=device,
                    device_id_type=MESH,
                )
            )
        return out

    def start(self, phase):
        for copy in self.copies(phase):
            copy.start()

    def finish(self, phase):
        for copy in self.copies(phase):
            copy.wait()
        first, count = (self.net.slots() - 1, 1) if phase == 3 else (self.net.slot(phase, 1), self.net.sizes[phase] - 1)
        total = self.bufs[phase]
        for k in range(count):
            total = total + self.bufs[4 + first + k]
        if phase < 3:
            self.bufs[phase + 1] = total
        return total


def call(body, outs, ins, specs=None, scratch=(), name=None, net=None):
    return pl.pallas_call(
        body,
        out_shape=[jax.ShapeDtypeStruct(s, d) for s, d in outs],
        in_specs=specs or [VMEM] * len(ins),
        out_specs=[VMEM] * len(outs),
        scratch_shapes=list(scratch),
        compiler_params=pltpu.CompilerParams(
            vmem_limit_bytes=64000 * 1024, collective_id=net, has_side_effects=net is not None
        ),
        name=name,
    )(*ins)


def qkv_tiles(first, last, x_ref, p_ref, w_ref, h_ref, qkv_ref):
    width = x_ref.shape[1]
    f = lax.axis_index("feat")
    gain = p_ref[GAIN1 : GAIN1 + 1, :]
    shift = p_ref[BIAS1 : BIAS1 + 1, :]
    bias = jnp.concatenate([p_ref[BQKV + i : BQKV + i + 1, ds(f, width // 2)] for i in range(3)], axis=1)

    def step(i, _):
        rows = ds(i, TILE)
        normed, _inv = norm(x_ref[rows, :].astype(F32))
        h = (normed * gain + shift).astype(BF)
        h_ref[rows, :] = h
        qkv_ref[rows, :] = (nn(h, w_ref[...]) + bias).astype(BF)
        return 0

    lax.fori_loop(first, last, step, 0)


def matches(list_ref, count_ref, h):
    at = lax.axis_index("feat") * (HEADS // 2) + h
    lists, count = list_ref[0, at], count_ref[0, pl.ds(at, 1), :]
    block = lax.broadcasted_iota(jnp.int32, (NB, NB), 0)
    found = jnp.zeros((NB, NB), F32)
    for j in range(lists.shape[0]):
        found = jnp.where((lists[j : j + 1] == block) & (count > j), 1.0, found)
    return found.astype(BF)


def fill_spread(e_ref):
    shift = lax.axis_index("feat") * (NB // 2)
    block = lax.broadcasted_iota(jnp.int32, e_ref.shape, 0)
    token = lax.broadcasted_iota(jnp.int32, e_ref.shape, 1)
    start = lax.rem(block + shift, NB) * BLOCK
    e_ref[...] = jnp.where((token >= start) & (token < start + BLOCK), 1.0, 0.0).astype(BF)


def local_marks(mk_ref, i, tile):
    assert tile * 2 == SEQLEN
    return mk_ref[ds(lax.rem(i + lax.axis_index("feat"), 2), tile // BLOCK), :]


def front_body(
    x_own_ref, w_all_ref, fs_ref, list_ref, count_ref, g1, b1, bo, g2, b2, bd, bqkv, bup,
    p_ref, x_ref, h_ref, qkv_ref, table_ref, w_ref, att_ref, den_ref, s_send, s_got, e_ref, mk_ref, pq_ref, pk_ref, send, recv, local,
):
    rows, width = x_own_ref.shape
    own = width // 2
    f = lax.axis_index("feat")
    other = {"feat": 1 - f}

    def copy(k, src, dst):
        return pltpu.make_async_remote_copy(
            src_ref=src, dst_ref=dst, send_sem=send.at[k], recv_sem=recv.at[k], device_id=other, device_id_type=MESH
        )

    loads = [
        pltpu.make_async_copy(w_all_ref.at[:, ds(2 * i + f, own)], w_ref.at[:, pl.ds(i * own, own)], local.at[i])
        for i in range(3)
    ]
    for c in loads:
        c.start()
    barrier = pltpu.get_barrier_semaphore()
    pl.semaphore_signal(barrier, inc=1, device_id=other, device_id_type=MESH)
    pl.semaphore_wait(barrier, 1)
    x_copy = copy(0, x_own_ref, x_ref.at[pl.ds(rows, rows)])
    x_copy.start()
    heads, dim, feats = s_send.shape
    line = 0
    for vector in (g1, b1, bo, g2, b2, bd, bqkv, bup):
        for i in range(vector.shape[0] // width):
            p_ref[line : line + 1, :] = vector[i * width : (i + 1) * width].astype(F32).reshape(1, width)
            line += 1

    def sign(i):
        return (2.0 * fs_ref[i].astype(F32) - 1.0).astype(BF)

    for i in range(heads):
        s_send[i] = sign((1 - f) * heads + i)
    s_copy = copy(1, s_send, s_got)
    s_copy.start()
    x_ref[0:rows, :] = x_own_ref[...]
    table_ref[...] = jnp.zeros_like(table_ref)
    for i in range(heads):
        e = i % 2
        table_ref[i // 2, e * dim : (e + 1) * dim, 2 * e * feats : (2 * e + 1) * feats] = sign(f * heads + i)
    fill_spread(e_ref)
    for c in loads:
        c.wait()
    tiles = rows // TILE
    qkv_tiles(0, tiles, x_ref, p_ref, w_ref, h_ref, qkv_ref)
    s_copy.wait()
    for i in range(heads):
        e = i % 2
        table_ref[i // 2, e * dim : (e + 1) * dim, (2 * e + 1) * feats : (2 * e + 2) * feats] = s_got[i]
    x_copy.wait()
    qkv_tiles(tiles, 2 * tiles, x_ref, p_ref, w_ref, h_ref, qkv_ref)
    att_heads(qkv_ref, table_ref, list_ref, count_ref, e_ref, mk_ref, att_ref, den_ref, pq_ref, pk_ref)


def head_parts(qkv_ref, h):
    own = qkv_ref.shape[1] // 3
    p, e = h // 2, h % 2
    lane = lax.broadcasted_iota(jnp.int32, (1, 128), 1)
    mine = (lane // HEAD_DIM) == e

    def cols(part):
        return pl.ds(pl.multiple_of(part * own + p * 128, 128), 128)

    return p, e, lane, mine, cols


def lift_all(qkv_ref, s_ref, h, pq_ref, pk_ref):
    p, e, lane, mine, cols = head_parts(qkv_ref, h)
    feats = pq_ref.shape[1]
    signs = s_ref[p, :, ds(e, feats)]

    def step(i, _):
        rows = ds(i, TILE)
        for part, out in ((0, pq_ref), (1, pk_ref)):
            t = qkv_ref[rows, cols(part)]
            w = jnp.where(mine, t.astype(F32), 0.0)
            sq = jnp.sum(w * w, axis=-1, keepdims=True) * (0.5 * HEAD_DIM ** (-0.5))
            lifted = nn(t, signs) * HEAD_DIM ** (-0.25)
            out[rows, :] = (jnp.exp(lifted - sq) * feats ** (-0.5)).astype(BF)
        return 0

    lax.fori_loop(0, qkv_ref.shape[0] // TILE, step, 0)


def att_heads(qkv_ref, s_ref, list_ref, count_ref, e_ref, mk_ref, att_ref, den_ref, pq_ref, pk_ref):
    def head(h, _):
        p, e, lane, mine, cols = head_parts(qkv_ref, h)
        mk_ref[...] = tn(matches(list_ref, count_ref, h), e_ref[...])
        lift_all(qkv_ref, s_ref, h, pq_ref, pk_ref)
        zero = jnp.zeros((), BF)
        v_one = jnp.where(mine, qkv_ref[:, cols(2)], jnp.ones((), BF))

        def step(i, _):
            rows = ds(i, ATILE)
            q = jnp.where(mine, qkv_ref[rows, cols(0)] * BF(HEAD_DIM ** (-0.5)), zero)
            ex = jnp.exp(nt(q, qkv_ref[:, cols(1)]))
            low = nt(pq_ref[rows, :], pk_ref[...])
            per = ATILE // BLOCK
            marks = local_marks(mk_ref, i, ATILE)
            probs = jnp.concatenate(
                [
                    jnp.where(
                        marks[j : j + 1, :] > 0.5,
                        ex[j * BLOCK : (j + 1) * BLOCK],
                        low[j * BLOCK : (j + 1) * BLOCK],
                    )
                    for j in range(per)
                ],
                axis=0,
            ).astype(BF)
            both = nn(probs, v_one)
            den = pltpu.roll(both, HEAD_DIM, 1)
            out_cols = ds(p, 128)
            att = (both / den).astype(BF)
            att_ref[rows, out_cols] = jnp.where(mine, att, att_ref[rows, out_cols])
            den_ref[rows, out_cols] = jnp.where(mine, den, den_ref[rows, out_cols])
            return 0

        lax.fori_loop(0, qkv_ref.shape[0] // ATILE, step, 0)
        return 0

    lax.fori_loop(0, qkv_ref.shape[1] // (3 * HEAD_DIM), head, 0)


def mix_tiles(x_ref, mine_ref, other_ref, w_ref, b_ref, g_ref, s_ref, mixed_ref, h_ref):
    f = lax.axis_index("feat")
    half = mine_ref.shape[1]

    def step(i, _):
        rows = ds(i, TILE)
        mixed = (
            x_ref[rows, :].astype(F32)
            + nn(mine_ref[rows, :], w_ref[ds(f, half), :])
            + nn(other_ref[rows, :], w_ref[ds(1 - f, half), :])
            + b_ref[...].astype(F32)
        )
        mixed_ref[rows, :] = mixed
        normed, _inv = norm(mixed)
        h_ref[rows, :] = (normed * g_ref[...].astype(F32) + s_ref[...].astype(F32)).astype(BF)
        return 0

    lax.fori_loop(0, x_ref.shape[0] // TILE, step, 0)


def ff_tiles(h_ref, og_ref, up_ref, down_ref, bias, act_ref, gp_ref, hid_ref, gh_ref, db_ref, send):
    tiles = h_ref.shape[0] // TILE
    db_ref[...] = jnp.zeros_like(db_ref)

    def step(i, _):
        tile = lax.rem(i + tiles // 2, tiles)
        rows = ds(tile, TILE)
        v = nn(h_ref[rows, :], up_ref[...]) + bias
        vv = v * v
        th = jnp.tanh(GELU_A * v * (1.0 + GELU_B * vv))
        half = 0.5 + 0.5 * th
        act = (v * half).astype(BF)
        slope = half + (0.5 * GELU_A) * v * (1.0 - th * th) * (1.0 + (3.0 * GELU_B) * vv)
        act_ref[rows, :] = act
        hid_ref[rows, :] = nn(act, down_ref[...]).astype(BF)
        gp = nt(og_ref[rows, :], down_ref[...]) * slope
        gpl = gp.astype(BF)
        gp_ref[rows, :] = gpl
        db_ref[...] += jnp.sum(gpl.astype(F32), axis=0, keepdims=True)
        gh_ref[rows, :] = nt(gpl, up_ref[...]).astype(BF)
        send(i, tile)
        return 0

    lax.fori_loop(0, tiles, step, 0)


def put_chunks(out_ref, first, value, net):
    rows = out_ref.shape[1]
    for i in range(value.shape[0] // rows):
        out_ref[net.place(first + i)] = value[i * rows : (i + 1) * rows].astype(BF)


def ff_weight(net, lhs_ref, rhs_ref, out_ref):
    wide = lhs_ref.shape[1] // 2
    per = wide // out_ref.shape[1]

    def step(i, _):
        put_chunks(out_ref, i * per, tn(lhs_ref[:, ds(i, wide)], rhs_ref[...]), net)
        return 0

    lax.fori_loop(0, 2, step, 0)


def out_back(
    n, gh_ref, gho_ref, mixed_ref, og_ref, hid_ref, hido_ref, bd_ref, g_ref, w_ref, mine_ref, other_ref,
    gm_ref, gatt_ref, dw_ref, y_ref, vec_ref, gb_ref,
):
    f = lax.axis_index("feat")
    half = mine_ref.shape[1]
    tiles = mixed_ref.shape[0] // TILE
    own = tiles // 2
    gain = g_ref[...].astype(F32)
    vec_ref[...] = jnp.zeros_like(vec_ref)

    def step(i, _):
        rows = ds(i, TILE)
        mixed = mixed_ref[rows, :]
        og = og_ref[rows, :].astype(F32)
        normed, inv = norm(mixed)
        g = gh_ref[rows, :].astype(F32) + gho_ref[rows, :].astype(F32)
        gm = og + norm_back(g, normed, inv, gain)
        gb = gm.astype(BF)
        gb_ref[rows, :] = gb
        gatt_ref[rows, :] = nt(gb, w_ref[ds(f, half), :])

        @pl.when(i < own)
        def _():
            gm_ref[rows, :] = gm
            y_ref[rows, :] = (
                mixed + hid_ref[rows, :].astype(F32) + hido_ref[rows, :].astype(F32) + bd_ref[...].astype(F32)
            ).astype(BF)
            for j, term in enumerate((g * normed, g, gb.astype(F32), og)):
                vec_ref[j + 2 : j + 3, :] += jnp.sum(term, axis=0, keepdims=True)

        return 0

    lax.fori_loop(0, tiles, step, 0)
    gb_own = gb_ref[:, ds(f, half)]
    net = Net(n)
    per = half // dw_ref.shape[1]
    put_chunks(dw_ref, f * per, tn(mine_ref[...], gb_own), net)
    put_chunks(dw_ref, (1 - f) * per, tn(other_ref[...], gb_own), net)


def mid_body(
    n, x_ref, att_ref, wout_ref, p_ref, og_own_ref, up_ref, down_ref,
    gm_ref, gatt_ref, dout_ref, y_ref, vec_ref, dup_ref, ddown_ref, dbup_ref,
    far, og, mixed, h, act, gp, hid, gh, hid_got, gh_got, gb, ddown, ddown_got, send, recv, down_send, down_recv,
):
    net = Net(n)
    down = Scatter(net, ddown, [ddown_got, ddown_ref, None, None, None], down_send, down_recv)
    bout_ref, g_ref, s_ref, bdown_ref = [p_ref.at[i : i + 1] for i in (BOUT, GAIN2, BIAS2, BDOWN)]
    bup = jnp.concatenate([p_ref[i : i + 1, :] for i in range(BUP, p_ref.shape[0])], axis=1)
    rows = og_own_ref.shape[0]
    tiles = h.shape[0] // TILE
    other = {"feat": 1 - lax.axis_index("feat")}

    def copy(k, src, dst):
        return pltpu.make_async_remote_copy(
            src_ref=src, dst_ref=dst, send_sem=send.at[k], recv_sem=recv.at[k], device_id=other, device_id_type=MESH
        )

    net.barrier()
    low, high = pl.ds(0, rows), pl.ds(rows, rows)
    atts = [copy(0, att_ref.at[low], far.at[high]), copy(1, att_ref.at[high], far.at[low])]
    og_copy = copy(2, og_own_ref, og.at[high])
    for c in atts:
        c.start()
    og_copy.start()
    og[low, :] = og_own_ref[...]
    for c in atts:
        c.wait()
    mix_tiles(x_ref, att_ref, far, wout_ref, bout_ref, g_ref, s_ref, mixed, h)
    og_copy.wait()

    def gh_copy(i, tile):
        return copy(3 + i, gh.at[ds(tile, TILE)], gh_got.at[ds(i, TILE)])

    def hid_copy(i, tile):
        return copy(3 + tiles + i, hid.at[ds(tile, TILE)], hid_got.at[ds(i, TILE)])

    def send_tile(i, tile):
        gh_copy(i, tile).start()

        @pl.when(i < tiles // 2)
        def _():
            hid_copy(i, tile).start()

    ff_tiles(h, og, up_ref, down_ref, bup, act, gp, hid, gh, dbup_ref, send_tile)
    ff_weight(net, og, act, ddown)
    down.start(0)
    ff_weight(net, h, gp, dup_ref)
    for i in range(tiles):
        gh_copy(i, (i + tiles // 2) % tiles).wait()
    for i in range(tiles // 2):
        hid_copy(i, i + tiles // 2).wait()
    out_back(
        n, gh, gh_got, mixed, og, hid, hid_got, bdown_ref, g_ref, wout_ref, att_ref, far,
        gm_ref, gatt_ref, dout_ref, y_ref, vec_ref, gb,
    )
    down.finish(0)


def heads_back(
    qkv_ref, s_ref, list_ref, count_ref, e_ref, mk_ref, att_ref, den_ref, gatt_ref, gqkv_ref, pq_ref, pk_ref, gn_ref, gq_ref, gpq_ref, after
):
    rows_all = qkv_ref.shape[0]
    scale = HEAD_DIM ** (-0.5)

    def head(h, _):
        p, e, lane, mine, cols = head_parts(qkv_ref, h)
        feats = pq_ref.shape[1]
        zero = jnp.zeros((), BF)
        mk_ref[...] = nn(matches(list_ref, count_ref, h), e_ref[...])
        lift_all(qkv_ref, s_ref, h, pq_ref, pk_ref)
        first_other = (1 - e) * HEAD_DIM

        def prep(i, _):
            rows = ds(i, TILE)
            inv = 1.0 / den_ref[rows, ds(p, 128)]
            ga = jnp.where(mine, gatt_ref[rows, ds(p, 128)] * inv, 0.0)
            gd = -jnp.sum(ga * att_ref[rows, ds(p, 128)].astype(F32), axis=-1, keepdims=True)
            gn_ref[rows, :] = jnp.where(lane == first_other, gd, ga).astype(BF)
            return 0

        lax.fori_loop(0, rows_all // TILE, prep, 0)
        gq_ref[...] = jnp.zeros_like(gq_ref)
        gpq_ref[...] = jnp.zeros_like(gpq_ref)
        signs = s_ref[p, :, ds(e, feats)]

        def lift_back(t, raw, g_phi):
            gl = g_phi * raw.astype(F32)
            gt = nt(gl.astype(BF), signs) * HEAD_DIM ** (-0.25)
            return gt - jnp.sum(gl, axis=-1, keepdims=True) * (scale * t.astype(F32))

        def put(part, rows, value):
            gqkv_ref[rows, cols(part)] = jnp.where(mine, value.astype(BF), gqkv_ref[rows, cols(part)])

        def step(i, _):
            rows = ds(i, BTILE)
            k = jnp.where(mine, qkv_ref[rows, cols(1)] * BF(scale), zero)
            v_one = jnp.where(mine, qkv_ref[rows, cols(2)], jnp.ones((), BF))
            q_all = qkv_ref[:, cols(0)]
            pk = pk_ref[rows, :]
            ex = jnp.exp(nt(k, q_all))
            low = nt(pk, pq_ref[...])
            da = nt(v_one, gn_ref[...])
            per = BTILE // BLOCK
            marks = local_marks(mk_ref, i, BTILE)
            probs, dl, gs = [], [], []
            for j in range(per):
                part = slice(j * BLOCK, (j + 1) * BLOCK)
                on = marks[j : j + 1, :] > 0.5
                exj, daj = ex[part], da[part]
                probs.append(jnp.where(on, exj, low[part]))
                dl.append(jnp.where(on, 0.0, daj))
                gs.append(jnp.where(on, daj * exj, 0.0))
            probs = jnp.concatenate(probs, axis=0).astype(BF)
            dl = jnp.concatenate(dl, axis=0).astype(BF)
            gs = jnp.concatenate(gs, axis=0).astype(BF)
            put(2, rows, nn(probs, gn_ref[...]))
            g_phi_k = nn(dl, pq_ref[...])
            gk = nn(gs, q_all) * scale + lift_back(qkv_ref[rows, cols(1)], pk, g_phi_k)
            put(1, rows, gk)
            gpq_ref[...] += tn(dl, pk)
            gq_ref[...] += tn(gs, k)
            return 0

        lax.fori_loop(0, rows_all // BTILE, step, 0)

        def last(i, _):
            rows = ds(i, TILE)
            gq = gq_ref[rows, :] + lift_back(qkv_ref[rows, cols(0)], pq_ref[rows, :], gpq_ref[rows, :])
            put(0, rows, gq)
            return 0

        lax.fori_loop(0, rows_all // TILE, last, 0)
        for k, then in after.items():
            pl.when(h == k)(then)
        return 0

    lax.fori_loop(0, qkv_ref.shape[1] // (3 * HEAD_DIM), head, 0)


def back_body(
    n, qkv_ref, s_ref, list_ref, count_ref, att_ref, den_ref, gatt_ref, h_ref, w_ref, x_ref, p_ref, gm_ref, up_ref, down_ref, out_ref,
    vec_ref, bup_ref, dx_ref, oup_ref, odown_ref, oout_ref, oqkv_ref, orows_ref, obqkv_ref, obup_ref, *scratch,
):
    net = Net(n)
    bufs, tail = (None, down_ref) + scratch[:28], scratch[28:]
    e_ref, mk_ref, pq, pk, gn, gq, gpq, gqkv, gw, gh_send, gh_got, sout, rout, sqkv, rqkv, vrows, vbqkv, vbup, send, recv = tail
    f = net.f
    other = {"feat": 1 - f}
    parts = [
        Scatter(net, src, bufs[5 * i : 5 * i + 5], send.at[i], recv.at[i])
        for i, src in enumerate((None, up_ref, out_ref, gw.at[0], gw.at[1], gw.at[2]))
    ]
    down, up, out = parts[:3]
    pairs = parts[3:]
    vectors = [Vector(net, ref, send.at[6 + i], recv.at[6 + i]) for i, ref in enumerate((vrows, vbqkv, vbup))]
    last = net.slots() - 1
    half = sout.shape[1]
    rows = x_ref.shape[0]
    width = x_ref.shape[1]
    own = width // 2
    lanes = orows_ref.shape[1]

    def whole(ref):
        def put(total):
            ref[...] = total

        return put

    def halves(ref):
        def put(total):
            ref[0], ref[1] = total[:half], total[half:]

        return put

    def swap(i, src, dst):
        return pltpu.make_async_remote_copy(
            src_ref=src, dst_ref=dst, send_sem=send.at[i, last], recv_sem=recv.at[i, last],
            device_id=other, device_id_type=MESH,
        )

    def move(part, phase):
        part.finish(phase)
        part.start(phase + 1)

    def weight(p):
        g = jnp.concatenate([gqkv[:, i * own + p * 128 : i * own + (p + 1) * 128] for i in range(3)], axis=1)
        per = own // gw.shape[2]
        for i in range(2):
            put_chunks(gw.at[p], i * per, tn(h_ref[:, i * own : (i + 1) * own], g), net)
        pairs[p].start(0)

    fill_spread(e_ref)
    net.barrier()
    down.start(1)
    up.start(0)
    out.start(0)

    def after1():
        move(down, 1)
        weight(0)

    def after2():
        move(up, 0)
        move(out, 0)
        move(pairs[0], 0)

    def after3():
        move(up, 1)
        move(out, 1)
        weight(1)

    def after4():
        down.finish(2, whole(odown_ref))
        move(pairs[0], 1)

    heads_back(
        qkv_ref, s_ref, list_ref, count_ref, e_ref, mk_ref, att_ref, den_ref, gatt_ref, gqkv, pq, pk, gn, gq, gpq,
        {1: after1, 2: after2, 3: after3, 4: after4},
    )
    weight(2)
    tiles = rows // TILE

    def far(i, total):
        g = gqkv[ds(tiles + i, TILE), :]
        gh_send[ds(i, TILE), :] = nt(g, w_ref[...]).astype(BF)
        return total + jnp.sum(g.astype(F32), axis=0, keepdims=True)

    total = lax.fori_loop(0, tiles, far, jnp.zeros((1, 3 * own), F32))
    gh_swap = swap(9, gh_send, gh_got)
    gh_swap.start()
    move(pairs[1], 0)

    def sums(i, total):
        return total + jnp.sum(gqkv[ds(i, TILE), :].astype(F32), axis=0, keepdims=True)

    total = lax.fori_loop(0, tiles, sums, total)
    vbqkv[0] = jnp.zeros_like(vbqkv[0])
    for i in range(3):
        vbqkv[0, :, ds(2 * i + f, own)] = total[:, i * own : (i + 1) * own]
    vbup[0] = bup_ref[...]
    out.finish(2, halves(sout))
    out_swap = swap(2, sout.at[1 - f], rout)
    out_swap.start()
    up.finish(2, whole(oup_ref))
    move(pairs[1], 1)
    move(pairs[2], 0)
    gh_swap.wait()
    gain = p_ref[GAIN1 : GAIN1 + 1, :]
    vrows[0] = vec_ref[...]

    def norm1(i, _):
        r = ds(i, TILE)
        normed, inv = norm(x_ref[r, :].astype(F32))
        g = nt(gqkv[r, :], w_ref[...]) + gh_got[r, :].astype(F32)
        dx_ref[r, :] = gm_ref[r, :] + norm_back(g, normed, inv, gain)
        vrows[0, 0:1, :] += jnp.sum(g * normed, axis=0, keepdims=True)
        vrows[0, 1:2, :] += jnp.sum(g, axis=0, keepdims=True)
        return 0

    lax.fori_loop(0, tiles, norm1, 0)
    for v in vectors:
        v.start(0)
    move(pairs[2], 1)
    for p in (0, 1):
        pairs[p].finish(2, halves(sqkv.at[p]))
    for v in vectors:
        v.finish(0)
        v.start(1)
    swaps = [swap(3 + p, sqkv.at[p, 1 - f], rqkv.at[p]) for p in range(3)]
    swaps[0].start()
    swaps[1].start()
    for v in vectors:
        v.finish(1)
        v.start(2)
    pairs[2].finish(2, halves(sqkv.at[2]))
    swaps[2].start()
    vecs, bqkv, bup = [v.finish(2) for v in vectors]
    vectors[0].start(3)
    vectors[1].start(3)
    where = 2 * net.s + f

    def cut(value, per, index, size):
        return pltpu.roll(value, lax.rem(size - index * per, size), 1)[:, :lanes]

    obup_ref[...] = cut(bup, bup.shape[1] // n, net.s, bup.shape[1])
    out_swap.wait()
    oout_ref[:, ds(f, own)] = sout[f]
    oout_ref[:, ds(1 - f, own)] = rout[...]

    def cols(i, p, side):
        return pl.ds(pl.multiple_of(i * width + side * own + p * 128, 128), 128)

    for p in range(3):
        swaps[p].wait()
        for i in range(3):
            part = slice(i * 128, (i + 1) * 128)
            oqkv_ref[:, cols(i, p, f)] = sqkv[p, f, :, part]
            oqkv_ref[:, cols(i, p, 1 - f)] = rqkv[p, :, part]
    vecs = vectors[0].finish(3)
    bqkv = vectors[1].finish(3)
    orows_ref[...] = cut(vecs, width // (2 * n), where, width)
    obqkv_ref[...] = cut(bqkv, bqkv.shape[1] // (2 * n), where, bqkv.shape[1])


def emit_body(y_ref, dx_ref, up_ref, down_ref, out_ref, qkv_ref, rows_ref, bqkv_ref, bup_ref, *outs):
    oy, odx, oup, odown, oout, oqkv, obqkv, obup = outs[:8]
    oy[...] = y_ref[...]
    odx[...], oup[...], oout[...], oqkv[...] = dx_ref[...], up_ref[...], out_ref[...], qkv_ref[...]
    down = down_ref[...]
    odown[...] = down if odown.shape == down.shape else down.T
    obqkv[...] = bqkv_ref[:, : obqkv.shape[1]]
    obup[...] = bup_ref[:, : obup.shape[1]]
    for i, ref in enumerate(outs[8:]):
        ref[...] = rows_ref[i : i + 1, : ref.shape[1]]


def body(
    layer_input, ln1_gain, ln1_bias, w_qkv, b_qkv, w_out, b_out, ln2_gain, ln2_bias,
    w_up, b_up, w_down, b_down, feature_signs, match_blocks, match_count, out_grad,
):
    rows, width = layer_input.shape
    half_width = width // 2
    half_heads = HEADS // 2
    hidden = w_up.shape[1]
    f = lax.axis_index("feat")
    tokens = 2 * rows
    n = lax.axis_size("seq")
    chunk = width // n
    assert lax.axis_size("feat") == 2 and match_blocks.shape[0] == 1 and tokens == SEQLEN

    lists = match_blocks.transpose(0, 1, 3, 2)
    vectors = [ln1_gain, ln1_bias, b_out, ln2_gain, ln2_bias, b_down, b_qkv, b_up]
    lines = sum(a.shape[0] for a in vectors) // width
    feats = 2 * feature_signs.shape[2]
    phi = pltpu.VMEM((tokens, feats), BF)
    masks = [pltpu.VMEM((NB, tokens), BF), pltpu.VMEM((NB, tokens), F32)]
    sign_half = pltpu.VMEM((half_heads, HEAD_DIM, feats // 2), BF)
    two = pltpu.SemaphoreType.DMA((2,))
    params, x, h1, qkv, table, w_own, att, den = call(
        front_body,
        [
            ((lines, width), F32),
            ((tokens, width), BF), ((tokens, width), BF), ((tokens, 3 * half_width), BF),
            ((half_heads // 2, 2 * HEAD_DIM, 2 * feats), BF), ((width, 3 * half_width), BF),
            ((tokens, half_width), BF), ((tokens, half_width), F32),
        ],
        [layer_input, w_qkv, feature_signs, lists, match_count] + vectors,
        specs=[VMEM, ANY] + [VMEM] * (3 + len(vectors)),
        scratch=[sign_half, sign_half] + masks + [phi, phi, two, two, pltpu.SemaphoreType.DMA((3,))],
        name="front", net=3,
    )
    big, wide = pltpu.VMEM((tokens, width), BF), pltpu.VMEM((tokens, hidden), BF)
    down_bufs = scatter_bufs(n, chunk, hidden)
    down_sems = pltpu.SemaphoreType.DMA((split(n)[0] - 1,))
    pair_sems = pltpu.SemaphoreType.DMA((3 + tokens // TILE + rows // TILE,))
    gm, gatt, d_out, y, vec2, d_up, d_down, d_bup = call(
        functools.partial(mid_body, n),
        [
            ((rows, width), F32), ((tokens, half_width), F32), ((n, chunk, half_width), BF), ((rows, width), BF),
            ((8, width), F32), ((n, chunk, hidden), BF), (down_bufs[1].shape, BF), ((1, hidden), F32),
        ],
        [
            x, att, w_out, params, out_grad, w_up, w_down,
        ],
        scratch=[
            pltpu.VMEM((tokens, half_width), BF), big, pltpu.VMEM((tokens, width), F32), big, wide, wide, big, big,
            pltpu.VMEM((rows, width), BF), big, big, pltpu.VMEM((n, chunk, hidden), BF), down_bufs[0],
            pair_sems, pair_sems, down_sems, down_sems,
        ],
        name="mid", net=2,
    )
    slots = sum(split(n)) + split(n)[0] - 3 + 1
    bufs = down_bufs[2:]
    for cols in (hidden, half_width, half_width, half_width, half_width):
        bufs += scatter_bufs(n, chunk, cols)
    half_chunk = chunk // 2
    sems = pltpu.SemaphoreType.DMA((10, slots))
    sums = call(
        functools.partial(back_body, n),
        [
            ((rows, width), F32), ((chunk, hidden), F32), ((chunk, hidden), F32), ((half_chunk, width), F32),
            ((half_chunk, 3 * width), F32), ((8, 128), F32), ((1, 128), F32), ((1, 128), F32),
        ],
        [
            qkv, table, lists, match_count, att, den, gatt, h1, w_own, layer_input, params, gm, d_up, d_down, d_out, vec2, d_bup,
        ],
        scratch=bufs + masks + [
            phi, phi, pltpu.VMEM((tokens, 128), BF), pltpu.VMEM((tokens, 128), F32), pltpu.VMEM((tokens, feats), F32),
            pltpu.VMEM((tokens, 3 * half_width), BF), pltpu.VMEM((3, n, chunk, half_width), BF),
            pltpu.VMEM((rows, width), BF), pltpu.VMEM((rows, width), BF),
            pltpu.VMEM((2, half_chunk, half_width), F32), pltpu.VMEM((half_chunk, half_width), F32),
            pltpu.VMEM((3, 2, half_chunk, half_width), F32), pltpu.VMEM((3, half_chunk, half_width), F32),
            pltpu.VMEM((4 + slots, 8, width), F32), pltpu.VMEM((4 + slots, 1, 3 * width), F32),
            pltpu.VMEM((4 + slots, 1, hidden), F32), sems, sems,
        ],
        name="back", net=1,
    )
    own = width // (2 * n)
    turn = False
    y, dx, up, down, out, full, d_b, d_bup, *vec = call(
        emit_body,
        [
            ((rows, width), BF),
            ((rows, width), F32), ((chunk, hidden), F32), ((hidden, chunk) if turn else (chunk, hidden), F32),
            ((half_chunk, width), F32), ((half_chunk, 3 * width), F32), ((1, 3 * own), F32), ((1, hidden // n), F32),
        ] + [((1, own), F32)] * 6,
        [y] + list(sums), name="emit",
    )
    vec = [v.reshape(-1) for v in vec]
    return (
        y, dx, vec[0], vec[1], full, d_b.reshape(-1), out, vec[4], vec[2], vec[3], up, d_bup.reshape(-1),
        down if turn else down.T, vec[5],
    )


def solution(mesh):
    both = ("seq", "feat")
    return jax.shard_map(
        body,
        mesh=mesh,
        in_specs=(
            P(both, None), P(), P(), P(), P(), P(), P(), P(), P(), P(None, "feat"), P("feat"), P("feat", None), P(),
            P(None, None, "feat"), P("seq", None, None, None), P("seq", None, None), P(both, None),
        ),
        out_specs=(
            P(both, None), P(both, None), P(both), P(both), P(both, None), P(both), P(both, None), P(both), P(both),
            P(both), P("seq", "feat"), P(("feat", "seq")), P("feat", "seq"), P(both),
        ),
        check_vma=False,
    )
```

```python
import functools
import math

import jax
import jax.numpy as jnp
from jax import lax
from jax.experimental import pallas as pl
from jax.experimental.pallas import tpu as pltpu
from jax.sharding import PartitionSpec as P

HEADS = 12
HEAD_DIM = 64
BLOCK = 64
NB = 16
SEQLEN = NB * BLOCK
BF = jnp.bfloat16
F32 = jnp.float32
EPS = 1e-05
TILE = 256
ATILE = 512
BTILE = 512
GELU_A = math.sqrt(2.0 / math.pi)
GELU_B = 0.044715
LOG2E = math.log2(math.e)
GAIN1, BIAS1, BOUT, GAIN2, BIAS2, BDOWN, BQKV, BUP = 0, 1, 2, 3, 4, 5, 6, 9
MESH = pl.DeviceIdType.MESH
VMEM = pl.BlockSpec(memory_space=pltpu.VMEM)
ANY = pl.BlockSpec(memory_space=pl.ANY)


def nn(a, b):
    return lax.dot_general(a, b, (((1,), (0,)), ((), ())), preferred_element_type=F32)


def nt(a, b):
    return lax.dot_general(a, b, (((1,), (1,)), ((), ())), preferred_element_type=F32)


def tn(a, b):
    return lax.dot_general(a, b, (((0,), (0,)), ((), ())), preferred_element_type=F32)


def ds(i, n):
    return pl.ds(i * n if isinstance(i, int) else pl.multiple_of(i * n, n), n)


def norm(x):
    c = x - jnp.mean(x, axis=-1, keepdims=True)
    inv = lax.rsqrt(jnp.mean(c * c, axis=-1, keepdims=True) + EPS)
    return c * inv, inv


def norm_back(g, normed, inv, gain):
    a = g * gain
    return inv * (
        a
        - jnp.mean(a, axis=-1, keepdims=True)
        - normed * jnp.mean(a * normed, axis=-1, keepdims=True)
    )


def split(n):
    p = 1
    while 2 * (2 * p) ** 3 <= n:
        p *= 2
    assert n % (p * p) == 0
    return p, n // (p * p)


class Net:
    def __init__(self, n):
        p, self.nz = split(n)
        self.p = p
        self.s, self.f = lax.axis_index("seq"), lax.axis_index("feat")
        x, y = lax.rem(self.s, p), lax.rem(self.s // p, p)
        f = self.f
        self.sizes = (p, p, self.nz)
        self.at = (x + f * (y - x), y + f * (x - y), self.s // (p * p))
        self.strides = (1 + f * (p - 1), p + f * (1 - p), p * p)

    def place(self, dest):
        p = self.p
        x, y, z = lax.rem(dest, p), lax.rem(dest // p, p), dest // (p * p)
        f = self.f
        return ((x + f * (y - x)) * p + y + f * (x - y)) * self.nz + z

    def peer(self, phase, d):
        j = lax.rem(self.at[phase] + d, self.sizes[phase])
        return j, self.s + (j - self.at[phase]) * self.strides[phase]

    def barrier(self):
        sem = pltpu.get_barrier_semaphore()
        count = 1
        for phase in range(3):
            for d in range(1, self.sizes[phase]):
                pl.semaphore_signal(sem, inc=1, device_id={"seq": self.peer(phase, d)[1]}, device_id_type=MESH)
                count += 1
        pl.semaphore_signal(sem, inc=1, device_id={"feat": 1 - self.f}, device_id_type=MESH)
        pl.semaphore_wait(sem, count)

    def slot(self, phase, d):
        return sum(size - 1 for size in self.sizes[:phase]) + d - 1

    def slots(self):
        return self.slot(3, 1) + 1


def scatter_bufs(n, rows, cols):
    p, nz = split(n)
    return [
        pltpu.VMEM((p - 1, p * nz, rows, cols), BF),
        pltpu.VMEM((p * nz, rows, cols), BF),
        pltpu.VMEM((p - 1, nz, rows, cols), BF),
        pltpu.VMEM((nz, rows, cols), BF),
        pltpu.VMEM((nz - 1, 1, rows, cols), BF),
    ]


class Scatter:
    def __init__(self, net, src, bufs, send, recv):
        self.net, self.send, self.recv = net, send, recv
        self.hold = (src, bufs[1], bufs[3])
        self.got = (bufs[0], bufs[2], bufs[4])

    def block(self, phase, j):
        size = self.got[phase].shape[1]
        return pl.ds(j * size, size)

    def copies(self, phase):
        net, out = self.net, []
        for d in range(1, net.sizes[phase]):
            j, device = net.peer(phase, d)
            k = net.slot(phase, d)
            out.append(
                pltpu.make_async_remote_copy(
                    src_ref=self.hold[phase].at[self.block(phase, j)],
                    dst_ref=self.got[phase].at[d - 1],
                    send_sem=self.send.at[k],
                    recv_sem=self.recv.at[k],
                    device_id={"seq": device},
                    device_id_type=MESH,
                )
            )
        return out

    def start(self, phase):
        for copy in self.copies(phase):
            copy.start()

    def finish(self, phase, put=None):
        for copy in self.copies(phase):
            copy.wait()
        got, own = self.got[phase], self.hold[phase]
        size = got.shape[1]
        base = self.net.at[phase] * size

        def add(i, _):
            total = own[base + i].astype(F32)
            for d in range(got.shape[0]):
                total = total + got[d, i].astype(F32)
            if put is None:
                self.hold[phase + 1][i] = total.astype(BF)
            else:
                put(total)
            return 0

        lax.fori_loop(0, size, add, 0)


class Vector:
    def __init__(self, net, bufs, send, recv):
        self.net, self.bufs, self.send, self.recv = net, bufs, send, recv

    def copies(self, phase):
        net, out = self.net, []
        peers = [({"feat": 1 - net.f}, net.slots() - 1)]
        if phase < 3:
            peers = [({"seq": net.peer(phase, d)[1]}, net.slot(phase, d)) for d in range(1, net.sizes[phase])]
        for device, k in peers:
            out.append(
                pltpu.make_async_remote_copy(
                    src_ref=self.bufs.at[phase],
                    dst_ref=self.bufs.at[4 + k],
                    send_sem=self.send.at[k],
                    recv_sem=self.recv.at[k],
                    device_id=device,
                    device_id_type=MESH,
                )
            )
        return out

    def start(self, phase):
        for copy in self.copies(phase):
            copy.start()

    def finish(self, phase):
        for copy in self.copies(phase):
            copy.wait()
        first, count = (self.net.slots() - 1, 1) if phase == 3 else (self.net.slot(phase, 1), self.net.sizes[phase] - 1)
        total = self.bufs[phase]
        for k in range(count):
            total = total + self.bufs[4 + first + k]
        if phase < 3:
            self.bufs[phase + 1] = total
        return total


def call(body, outs, ins, specs=None, out_specs=None, scratch=(), name=None, net=None):
    return pl.pallas_call(
        body,
        out_shape=[jax.ShapeDtypeStruct(s, d) for s, d in outs],
        in_specs=specs or [VMEM] * len(ins),
        out_specs=out_specs or [VMEM] * len(outs),
        scratch_shapes=list(scratch),
        compiler_params=pltpu.CompilerParams(
            vmem_limit_bytes=64000 * 1024, collective_id=net, has_side_effects=net is not None
        ),
        name=name,
    )(*ins)


def qkv_tiles(first, last, x_ref, p_ref, w_ref, h_ref, qkv_ref):
    width = x_ref.shape[1]
    f = lax.axis_index("feat")
    gain = p_ref[GAIN1 : GAIN1 + 1, :]
    shift = p_ref[BIAS1 : BIAS1 + 1, :]
    bias = jnp.concatenate([p_ref[BQKV + i : BQKV + i + 1, ds(f, width // 2)] for i in range(3)], axis=1)

    def step(i, _):
        rows = ds(i, TILE)
        normed, _inv = norm(x_ref[rows, :].astype(F32))
        h = (normed * gain + shift).astype(BF)
        h_ref[rows, :] = h
        qkv_ref[rows, :] = (nn(h, w_ref[...]) + bias).astype(BF)
        return 0

    lax.fori_loop(first, last, step, 0)


def matches(list_ref, count_ref, h):
    at = lax.axis_index("feat") * (HEADS // 2) + h
    lists, count = list_ref[0, at], count_ref[0, pl.ds(at, 1), :]
    block = lax.broadcasted_iota(jnp.int32, (NB, NB), 0)
    found = jnp.zeros((NB, NB), F32)
    for j in range(lists.shape[0]):
        found = jnp.where((lists[j : j + 1] == block) & (count > j), 1.0, found)
    return found.astype(BF)


def fill_spread(e_ref):
    shift = lax.axis_index("feat") * (NB // 2)
    block = lax.broadcasted_iota(jnp.int32, e_ref.shape, 0)
    token = lax.broadcasted_iota(jnp.int32, e_ref.shape, 1)
    start = lax.rem(block + shift, NB) * BLOCK
    e_ref[...] = jnp.where((token >= start) & (token < start + BLOCK), 1.0, 0.0).astype(BF)


def local_marks(mk_ref, i, tile):
    assert tile * 2 == SEQLEN
    return mk_ref[ds(lax.rem(i + lax.axis_index("feat"), 2), tile // BLOCK), :]


def front_body(
    x_own_ref, w_all_ref, fs_ref, list_ref, count_ref, g1, b1, bo, g2, b2, bd, bqkv, bup,
    p_ref, x_ref, h_ref, qkv_ref, table_ref, w_ref, att_ref, den_ref, kept_ref, s_send, s_got, e_ref, mk_ref, pq_ref, pk_ref, keep_ref, acc_ref, send, recv, local, keep_sems,
):
    rows, width = x_own_ref.shape
    own = width // 2
    f = lax.axis_index("feat")
    other = {"feat": 1 - f}

    def copy(k, src, dst):
        return pltpu.make_async_remote_copy(
            src_ref=src, dst_ref=dst, send_sem=send.at[k], recv_sem=recv.at[k], device_id=other, device_id_type=MESH
        )

    loads = [
        pltpu.make_async_copy(w_all_ref.at[:, ds(2 * i + f, own)], w_ref.at[:, pl.ds(i * own, own)], local.at[i])
        for i in range(3)
    ]
    for c in loads:
        c.start()
    barrier = pltpu.get_barrier_semaphore()
    pl.semaphore_signal(barrier, inc=1, device_id=other, device_id_type=MESH)
    pl.semaphore_wait(barrier, 1)
    x_copy = copy(0, x_own_ref, x_ref.at[pl.ds(rows, rows)])
    x_copy.start()
    heads, dim, feats = s_send.shape
    line = 0
    for vector in (g1, b1, bo, g2, b2, bd, bqkv, bup):
        for i in range(vector.shape[0] // width):
            p_ref[line : line + 1, :] = vector[i * width : (i + 1) * width].astype(F32).reshape(1, width)
            line += 1

    def sign(i):
        return (2.0 * fs_ref[i].astype(F32) - 1.0).astype(BF)

    for i in range(heads):
        s_send[i] = sign((1 - f) * heads + i)
    s_copy = copy(1, s_send, s_got)
    s_copy.start()
    x_ref[0:rows, :] = x_own_ref[...]
    table_ref[...] = jnp.zeros_like(table_ref)
    for i in range(heads):
        e = i % 2
        table_ref[i // 2, e * dim : (e + 1) * dim, 2 * e * feats : (2 * e + 1) * feats] = sign(f * heads + i)
    fill_spread(e_ref)
    for c in loads:
        c.wait()
    tiles = rows // TILE
    qkv_tiles(0, tiles, x_ref, p_ref, w_ref, h_ref, qkv_ref)
    s_copy.wait()
    for i in range(heads):
        e = i % 2
        table_ref[i // 2, e * dim : (e + 1) * dim, (2 * e + 1) * feats : (2 * e + 2) * feats] = s_got[i]
    x_copy.wait()
    qkv_tiles(tiles, 2 * tiles, x_ref, p_ref, w_ref, h_ref, qkv_ref)
    att_heads(
        qkv_ref, table_ref, list_ref, count_ref, e_ref, mk_ref, att_ref, den_ref, kept_ref, pq_ref, pk_ref, keep_ref,
        acc_ref, keep_sems,
    )


def head_parts(qkv_ref, h):
    own = qkv_ref.shape[1] // 3
    p, e = h // 2, h % 2
    lane = lax.broadcasted_iota(jnp.int32, (1, 128), 1)
    mine = (lane // HEAD_DIM) == e

    def cols(part):
        return pl.ds(pl.multiple_of(part * own + p * 128, 128), 128)

    return p, e, lane, mine, cols


def lift_all(qkv_ref, s_ref, h, pq_ref, pk_ref):
    p, e, lane, mine, cols = head_parts(qkv_ref, h)
    feats = pq_ref.shape[1]
    signs = s_ref[p, :, ds(e, feats)]

    def step(i, _):
        rows = ds(i, TILE)
        for part, out in ((0, pq_ref), (1, pk_ref)):
            t = qkv_ref[rows, cols(part)]
            w = jnp.where(mine, t.astype(F32), 0.0)
            sq = jnp.sum(w * w, axis=-1, keepdims=True) * (LOG2E * 0.5 * HEAD_DIM ** (-0.5)) + 0.5 * math.log2(feats)
            out[rows, :] = jnp.exp2(nn(t, signs) * (LOG2E * HEAD_DIM ** (-0.25)) - sq).astype(BF)
        return 0

    lax.fori_loop(0, qkv_ref.shape[0] // TILE, step, 0)


def att_heads(
    qkv_ref, s_ref, list_ref, count_ref, e_ref, mk_ref, att_ref, den_ref, kept_ref, pq_ref, pk_ref, p_ref, acc_ref, sems
):
    heads = qkv_ref.shape[1] // (3 * HEAD_DIM)

    def keep(h):
        slot = lax.rem(h, 2)
        return pltpu.make_async_copy(p_ref.at[slot], kept_ref.at[h], sems.at[slot])

    def head(h, _):
        p, e, lane, mine, cols = head_parts(qkv_ref, h)
        slot = lax.rem(h, 2)
        mk_ref[...] = nn(matches(list_ref, count_ref, h), e_ref[...])
        lift_all(qkv_ref, s_ref, h, pq_ref, pk_ref)
        zero = jnp.zeros((), BF)

        @pl.when(h >= 2)
        def _():
            keep(h - 2).wait()

        acc_ref[...] = jnp.zeros_like(acc_ref)

        def step(i, _):
            rows = ds(i, ATILE)
            k = jnp.where(mine, qkv_ref[rows, cols(1)] * BF(HEAD_DIM ** (-0.5)), zero)
            v_one = jnp.where(mine, qkv_ref[rows, cols(2)], jnp.ones((), BF))
            ex = jnp.exp(nt(k, qkv_ref[:, cols(0)]))
            low = nt(pk_ref[rows, :], pq_ref[...])
            marks = local_marks(mk_ref, i, ATILE)
            probs = jnp.concatenate(
                [
                    jnp.where(
                        marks[j : j + 1, :] > 0.5,
                        ex[j * BLOCK : (j + 1) * BLOCK],
                        low[j * BLOCK : (j + 1) * BLOCK],
                    )
                    for j in range(ATILE // BLOCK)
                ],
                axis=0,
            ).astype(BF)
            p_ref[slot, rows, :] = probs
            acc_ref[...] += tn(probs, v_one)
            return 0

        lax.fori_loop(0, qkv_ref.shape[0] // ATILE, step, 0)
        keep(h).start()

        def last(i, _):
            rows = ds(i, TILE)
            both = acc_ref[rows, :]
            den = pltpu.roll(both, HEAD_DIM, 1)
            out_cols = ds(p, 128)
            att = (both / den).astype(BF)
            att_ref[rows, out_cols] = jnp.where(mine, att, att_ref[rows, out_cols])
            den_ref[rows, out_cols] = jnp.where(mine, den, den_ref[rows, out_cols])
            return 0

        lax.fori_loop(0, qkv_ref.shape[0] // TILE, last, 0)
        return 0

    lax.fori_loop(0, heads, head, 0)
    keep(heads - 2).wait()
    keep(heads - 1).wait()


def mix_tiles(x_ref, mine_ref, other_ref, w_ref, b_ref, g_ref, s_ref, mixed_ref, h_ref):
    f = lax.axis_index("feat")
    half = mine_ref.shape[1]

    def step(i, _):
        rows = ds(i, TILE)
        mixed = (
            x_ref[rows, :].astype(F32)
            + nn(mine_ref[rows, :], w_ref[ds(f, half), :])
            + nn(other_ref[rows, :], w_ref[ds(1 - f, half), :])
            + b_ref[...].astype(F32)
        )
        mixed_ref[rows, :] = mixed
        normed, _inv = norm(mixed)
        h_ref[rows, :] = (normed * g_ref[...].astype(F32) + s_ref[...].astype(F32)).astype(BF)
        return 0

    lax.fori_loop(0, x_ref.shape[0] // TILE, step, 0)


def ff_forward(h_ref, up_ref, down_ref, bias, act_ref, slope_ref, hid_ref, send):
    tiles = h_ref.shape[0] // TILE

    def step(i, _):
        tile = lax.rem(i + tiles // 2, tiles)
        rows = ds(tile, TILE)
        v = nn(h_ref[rows, :], up_ref[...]) + bias
        vv = v * v
        th = jnp.tanh(GELU_A * v * (1.0 + GELU_B * vv))
        half = 0.5 + 0.5 * th
        act = (v * half).astype(BF)
        slope_ref[rows, :] = half + (0.5 * GELU_A) * v * (1.0 - th * th) * (1.0 + (3.0 * GELU_B) * vv)
        act_ref[rows, :] = act
        hid_ref[rows, :] = nn(act, down_ref[...]).astype(BF)
        send(i, tile)
        return 0

    lax.fori_loop(0, tiles, step, 0)


def ff_backward(og_ref, up_ref, down_ref, slope_ref, gp_ref, gh_ref, db_ref, send):
    tiles = og_ref.shape[0] // TILE
    db_ref[...] = jnp.zeros_like(db_ref)

    def step(i, _):
        tile = lax.rem(i + tiles // 2, tiles)
        rows = ds(tile, TILE)
        gp = (nt(og_ref[rows, :], down_ref[...]) * slope_ref[rows, :]).astype(BF)
        gp_ref[rows, :] = gp
        db_ref[...] += jnp.sum(gp.astype(F32), axis=0, keepdims=True)
        gh_ref[rows, :] = nt(gp, up_ref[...]).astype(BF)
        send(i, tile)
        return 0

    lax.fori_loop(0, tiles, step, 0)


def put_chunks(out_ref, first, value, net):
    rows = out_ref.shape[1]
    for i in range(value.shape[0] // rows):
        out_ref[net.place(first + i)] = value[i * rows : (i + 1) * rows].astype(BF)


def ff_weight(net, lhs_ref, rhs_ref, outs):
    wide = lhs_ref.shape[1] // 2
    per = wide // outs[0].shape[1]

    def step(i, _):
        value = tn(lhs_ref[:, ds(i, wide)], rhs_ref[...])
        for j, out in enumerate(outs):
            put_chunks(out, i * per, value[:, j * out.shape[2] : (j + 1) * out.shape[2]], net)
        return 0

    lax.fori_loop(0, 2, step, 0)


def out_back(
    n, gh_ref, gho_ref, mixed_ref, og_ref, hid_ref, hido_ref, bd_ref, g_ref, w_ref, mine_ref, other_ref,
    gm_ref, gatt_ref, dw_ref, y_ref, vec_ref, gb_ref,
):
    f = lax.axis_index("feat")
    half = mine_ref.shape[1]
    tiles = mixed_ref.shape[0] // TILE
    own = tiles // 2
    gain = g_ref[...].astype(F32)
    vec_ref[...] = jnp.zeros_like(vec_ref)

    def step(i, _):
        rows = ds(i, TILE)
        mixed = mixed_ref[rows, :]
        og = og_ref[rows, :].astype(F32)
        normed, inv = norm(mixed)
        g = gh_ref[rows, :].astype(F32) + gho_ref[rows, :].astype(F32)
        gm = og + norm_back(g, normed, inv, gain)
        gb = gm.astype(BF)
        gb_ref[rows, :] = gb
        gatt_ref[rows, :] = nt(gb, w_ref[ds(f, half), :])

        @pl.when(i < own)
        def _():
            gm_ref[rows, :] = gm
            y_ref[rows, :] = (
                mixed + hid_ref[rows, :].astype(F32) + hido_ref[rows, :].astype(F32) + bd_ref[...].astype(F32)
            ).astype(BF)
            for j, term in enumerate((g * normed, g, gb.astype(F32), og)):
                vec_ref[j + 2 : j + 3, :] += jnp.sum(term, axis=0, keepdims=True)

        return 0

    lax.fori_loop(0, tiles, step, 0)
    gb_own = gb_ref[:, ds(f, half)]
    net = Net(n)
    per = half // dw_ref.shape[1]
    put_chunks(dw_ref, f * per, tn(mine_ref[...], gb_own), net)
    put_chunks(dw_ref, (1 - f) * per, tn(other_ref[...], gb_own), net)


def mid_body(
    n, x_ref, att_ref, wout_ref, p_ref, og_own_ref, up_ref, down_ref,
    gm_ref, gatt_ref, dout_ref, y_ref, vec_ref, dup_ref, ddown_ref, dbup_ref,
    far, og, mixed, h, act, gp, hid, gh, hid_got, gh_got, gb, ddown, ddown_got, slope, send, recv, down_send, down_recv,
):
    net = Net(n)
    down = Scatter(net, ddown, [ddown_got, ddown_ref, None, None, None], down_send, down_recv)
    bout_ref, g_ref, s_ref, bdown_ref = [p_ref.at[i : i + 1] for i in (BOUT, GAIN2, BIAS2, BDOWN)]
    bup = jnp.concatenate([p_ref[i : i + 1, :] for i in range(BUP, p_ref.shape[0])], axis=1)
    rows = og_own_ref.shape[0]
    tiles = h.shape[0] // TILE
    other = {"feat": 1 - lax.axis_index("feat")}

    def copy(k, src, dst):
        return pltpu.make_async_remote_copy(
            src_ref=src, dst_ref=dst, send_sem=send.at[k], recv_sem=recv.at[k], device_id=other, device_id_type=MESH
        )

    net.barrier()
    low, high = pl.ds(0, rows), pl.ds(rows, rows)
    atts = [copy(0, att_ref.at[low], far.at[high]), copy(1, att_ref.at[high], far.at[low])]
    og_copy = copy(2, og_own_ref, og.at[high])
    for c in atts:
        c.start()
    og_copy.start()
    og[low, :] = og_own_ref[...]
    for c in atts:
        c.wait()
    mix_tiles(x_ref, att_ref, far, wout_ref, bout_ref, g_ref, s_ref, mixed, h)

    def gh_copy(i, tile):
        return copy(3 + i, gh.at[ds(tile, TILE)], gh_got.at[ds(i, TILE)])

    def hid_copy(i, tile):
        return copy(3 + tiles + i, hid.at[ds(tile, TILE)], hid_got.at[ds(i, TILE)])

    def send_gh(i, tile):
        gh_copy(i, tile).start()

    def send_hid(i, tile):
        @pl.when(i < tiles // 2)
        def _():
            hid_copy(i, tile).start()

    ff_forward(h, up_ref, down_ref, bup, act, slope, hid, send_hid)
    og_copy.wait()
    ff_weight(net, og, act, [ddown])
    down.start(0)
    ff_backward(og, up_ref, down_ref, slope, gp, gh, dbup_ref, send_gh)
    ff_weight(net, h, gp, [dup_ref.at[0], dup_ref.at[1]])
    for i in range(tiles):
        gh_copy(i, (i + tiles // 2) % tiles).wait()
    for i in range(tiles // 2):
        hid_copy(i, i + tiles // 2).wait()
    out_back(
        n, gh, gh_got, mixed, og, hid, hid_got, bdown_ref, g_ref, wout_ref, att_ref, far,
        gm_ref, gatt_ref, dout_ref, y_ref, vec_ref, gb,
    )
    down.finish(0)


def heads_back(
    qkv_ref, s_ref, list_ref, count_ref, kept_ref, p_ref, sems, e_ref, mk_ref, att_ref, den_ref, gatt_ref, gqkv_ref, pq_ref, pk_ref, gn_ref, gq_ref, gpq_ref, after
):
    rows_all = qkv_ref.shape[0]
    scale = HEAD_DIM ** (-0.5)

    heads = qkv_ref.shape[1] // (3 * HEAD_DIM)

    def fetch(h):
        slot = lax.rem(h, 2)
        return pltpu.make_async_copy(kept_ref.at[h], p_ref.at[slot], sems.at[slot])

    fetch(0).start()

    def head(h, _):
        slot = lax.rem(h, 2)

        @pl.when(h + 1 < heads)
        def _():
            fetch(h + 1).start()

        p, e, lane, mine, cols = head_parts(qkv_ref, h)
        feats = pq_ref.shape[1]
        zero = jnp.zeros((), BF)
        mk_ref[...] = nn(matches(list_ref, count_ref, h), e_ref[...])
        lift_all(qkv_ref, s_ref, h, pq_ref, pk_ref)
        first_other = (1 - e) * HEAD_DIM

        def prep(i, _):
            rows = ds(i, TILE)
            inv = 1.0 / den_ref[rows, ds(p, 128)]
            ga = jnp.where(mine, gatt_ref[rows, ds(p, 128)] * inv, 0.0)
            gd = -jnp.sum(ga * att_ref[rows, ds(p, 128)].astype(F32), axis=-1, keepdims=True)
            gn_ref[rows, :] = jnp.where(lane == first_other, gd, ga).astype(BF)
            return 0

        lax.fori_loop(0, rows_all // TILE, prep, 0)
        gq_ref[...] = jnp.zeros_like(gq_ref)
        gpq_ref[...] = jnp.zeros_like(gpq_ref)
        signs = s_ref[p, :, ds(e, feats)]

        def lift_back(t, raw, g_phi):
            gl = g_phi * raw.astype(F32)
            gt = nt(gl.astype(BF), signs) * HEAD_DIM ** (-0.25)
            return gt - jnp.sum(gl, axis=-1, keepdims=True) * (scale * t.astype(F32))

        def put(part, rows, value):
            gqkv_ref[rows, cols(part)] = jnp.where(mine, value.astype(BF), gqkv_ref[rows, cols(part)])

        fetch(h).wait()

        def step(i, _):
            rows = ds(i, BTILE)
            k = jnp.where(mine, qkv_ref[rows, cols(1)] * BF(scale), zero)
            v_one = jnp.where(mine, qkv_ref[rows, cols(2)], jnp.ones((), BF))
            q_all = qkv_ref[:, cols(0)]
            pk = pk_ref[rows, :]
            probs = p_ref[slot, rows, :]
            da = nt(v_one, gn_ref[...])
            marks = local_marks(mk_ref, i, BTILE)
            dl, gs = [], []
            for j in range(BTILE // BLOCK):
                part = slice(j * BLOCK, (j + 1) * BLOCK)
                on = marks[j : j + 1, :] > 0.5
                daj = da[part]
                dl.append(jnp.where(on, 0.0, daj))
                gs.append(jnp.where(on, daj * probs[part].astype(F32), 0.0))
            dl = jnp.concatenate(dl, axis=0).astype(BF)
            gs = jnp.concatenate(gs, axis=0).astype(BF)
            put(2, rows, nn(probs, gn_ref[...]))
            g_phi_k = nn(dl, pq_ref[...])
            gk = nn(gs, q_all) * scale + lift_back(qkv_ref[rows, cols(1)], pk, g_phi_k)
            put(1, rows, gk)
            gpq_ref[...] += tn(dl, pk)
            gq_ref[...] += tn(gs, k)
            return 0

        lax.fori_loop(0, rows_all // BTILE, step, 0)

        def last(i, _):
            rows = ds(i, TILE)
            gq = gq_ref[rows, :] + lift_back(qkv_ref[rows, cols(0)], pq_ref[rows, :], gpq_ref[rows, :])
            put(0, rows, gq)
            return 0

        lax.fori_loop(0, rows_all // TILE, last, 0)
        for k, then in after.items():
            pl.when(h == k)(then)
        return 0

    lax.fori_loop(0, qkv_ref.shape[1] // (3 * HEAD_DIM), head, 0)


def back_body(
    n, qkv_ref, s_ref, list_ref, count_ref, kept_ref, att_ref, den_ref, gatt_ref, h_ref, w_ref, x_ref, p_ref, gm_ref, up_ref, down_ref, out_ref,
    vec_ref, bup_ref, dx_ref, oup_ref, odown_ref, oout_ref, oqkv_ref, orows_ref, obqkv_ref, obup_ref, *scratch,
):
    net = Net(n)
    bufs, tail = (None, down_ref) + scratch[:33], scratch[33:]
    kept_buf, keep_sems, e_ref, mk_ref, pq, pk, gn, gq, gpq, gqkv, gw, gh_send, gh_got, sout, rout, sqkv, rqkv, vrows, vbqkv, vbup, send, recv = tail
    f = net.f
    other = {"feat": 1 - f}
    sources = (None, up_ref.at[0], out_ref, gw.at[0], gw.at[1], gw.at[2], up_ref.at[1])
    lanes_of = (0, 1, 2, 3, 4, 5, 10)
    down, up_low, out, *pairs, up_high = [
        Scatter(net, src, bufs[5 * i : 5 * i + 5], send.at[k], recv.at[k])
        for i, (src, k) in enumerate(zip(sources, lanes_of))
    ]
    vectors = [Vector(net, ref, send.at[6 + i], recv.at[6 + i]) for i, ref in enumerate((vrows, vbqkv, vbup))]
    last = net.slots() - 1
    half = sout.shape[1]
    rows = x_ref.shape[0]
    width = x_ref.shape[1]
    own = width // 2
    lanes = orows_ref.shape[1]

    def whole(ref):
        def put(total):
            ref[...] = total

        return put

    def halves(ref):
        def put(total):
            ref[0], ref[1] = total[:half], total[half:]

        return put

    def swap(i, src, dst):
        return pltpu.make_async_remote_copy(
            src_ref=src, dst_ref=dst, send_sem=send.at[i, last], recv_sem=recv.at[i, last],
            device_id=other, device_id_type=MESH,
        )

    def move(part, phase):
        part.finish(phase)
        part.start(phase + 1)

    def weight(p):
        g = jnp.concatenate([gqkv[:, i * own + p * 128 : i * own + (p + 1) * 128] for i in range(3)], axis=1)
        per = own // gw.shape[2]
        for i in range(2):
            put_chunks(gw.at[p], i * per, tn(h_ref[:, i * own : (i + 1) * own], g), net)
        pairs[p].start(0)

    fill_spread(e_ref)
    net.barrier()
    down.start(1)
    up_low.start(0)
    up_high.start(0)
    out.start(0)

    def after1():
        move(down, 1)
        move(up_low, 0)
        weight(0)

    def after2():
        move(up_high, 0)
        move(up_low, 1)

    def after3():
        move(out, 0)
        move(pairs[0], 0)
        move(up_high, 1)
        weight(1)

    def after4():
        down.finish(2, whole(odown_ref))
        move(out, 1)
        move(pairs[0], 1)
        move(pairs[1], 0)

    heads_back(
        qkv_ref, s_ref, list_ref, count_ref, kept_ref, kept_buf, keep_sems, e_ref, mk_ref, att_ref, den_ref, gatt_ref, gqkv, pq, pk, gn, gq, gpq,
        {1: after1, 2: after2, 3: after3, 4: after4},
    )
    weight(2)
    tiles = rows // TILE

    def far(i, total):
        g = gqkv[ds(tiles + i, TILE), :]
        gh_send[ds(i, TILE), :] = nt(g, w_ref[...]).astype(BF)
        return total + jnp.sum(g.astype(F32), axis=0, keepdims=True)

    total = lax.fori_loop(0, tiles, far, jnp.zeros((1, 3 * own), F32))
    gh_swap = swap(9, gh_send, gh_got)
    gh_swap.start()
    move(pairs[1], 1)

    def sums(i, total):
        return total + jnp.sum(gqkv[ds(i, TILE), :].astype(F32), axis=0, keepdims=True)

    total = lax.fori_loop(0, tiles, sums, total)
    vbqkv[0] = jnp.zeros_like(vbqkv[0])
    for i in range(3):
        vbqkv[0, :, ds(2 * i + f, own)] = total[:, i * own : (i + 1) * own]
    vbup[0] = bup_ref[...]
    up_low.finish(2, whole(oup_ref.at[:, 0 : oup_ref.shape[1] // 2]))
    out.finish(2, halves(sout))
    out_swap = swap(2, sout.at[1 - f], rout)
    out_swap.start()
    move(pairs[2], 0)
    up_high.finish(2, whole(oup_ref.at[:, oup_ref.shape[1] // 2 :]))
    gh_swap.wait()
    gain = p_ref[GAIN1 : GAIN1 + 1, :]
    vrows[0] = vec_ref[...]

    def norm1(i, _):
        r = ds(i, TILE)
        normed, inv = norm(x_ref[r, :].astype(F32))
        g = nt(gqkv[r, :], w_ref[...]) + gh_got[r, :].astype(F32)
        dx_ref[r, :] = gm_ref[r, :] + norm_back(g, normed, inv, gain)
        vrows[0, 0:1, :] += jnp.sum(g * normed, axis=0, keepdims=True)
        vrows[0, 1:2, :] += jnp.sum(g, axis=0, keepdims=True)
        return 0

    lax.fori_loop(0, tiles, norm1, 0)
    for v in vectors:
        v.start(0)
    move(pairs[2], 1)
    for p in (0, 1):
        pairs[p].finish(2, halves(sqkv.at[p]))
    for v in vectors:
        v.finish(0)
        v.start(1)
    swaps = [swap(3 + p, sqkv.at[p, 1 - f], rqkv.at[p]) for p in range(3)]
    swaps[0].start()
    swaps[1].start()
    for v in vectors:
        v.finish(1)
        v.start(2)
    pairs[2].finish(2, halves(sqkv.at[2]))
    swaps[2].start()
    vecs, bqkv, bup = [v.finish(2) for v in vectors]
    vectors[0].start(3)
    vectors[1].start(3)
    where = 2 * net.s + f

    def cut(value, per, index, size):
        return pltpu.roll(value, lax.rem(size - index * per, size), 1)[:, :lanes]

    obup_ref[...] = cut(bup, bup.shape[1] // n, net.s, bup.shape[1])
    out_swap.wait()
    oout_ref[:, ds(f, own)] = sout[f]
    oout_ref[:, ds(1 - f, own)] = rout[...]

    def cols(i, p, side):
        return pl.ds(pl.multiple_of(i * width + side * own + p * 128, 128), 128)

    for p in range(3):
        swaps[p].wait()
        for i in range(3):
            part = slice(i * 128, (i + 1) * 128)
            oqkv_ref[:, cols(i, p, f)] = sqkv[p, f, :, part]
            oqkv_ref[:, cols(i, p, 1 - f)] = rqkv[p, :, part]
    vecs = vectors[0].finish(3)
    bqkv = vectors[1].finish(3)
    orows_ref[...] = cut(vecs, width // (2 * n), where, width)
    obqkv_ref[...] = cut(bqkv, bqkv.shape[1] // (2 * n), where, bqkv.shape[1])


def emit_body(y_ref, dx_ref, up_ref, down_ref, out_ref, qkv_ref, rows_ref, bqkv_ref, bup_ref, *outs):
    oy, odx, oup, odown, oout, oqkv, obqkv, obup = outs[:8]
    oy[...] = y_ref[...]
    odx[...], oup[...], oout[...], oqkv[...] = dx_ref[...], up_ref[...], out_ref[...], qkv_ref[...]
    down = down_ref[...]
    odown[...] = down if odown.shape == down.shape else down.T
    obqkv[...] = bqkv_ref[:, : obqkv.shape[1]]
    obup[...] = bup_ref[:, : obup.shape[1]]
    for i, ref in enumerate(outs[8:]):
        ref[...] = rows_ref[i : i + 1, : ref.shape[1]]


def body(
    layer_input, ln1_gain, ln1_bias, w_qkv, b_qkv, w_out, b_out, ln2_gain, ln2_bias,
    w_up, b_up, w_down, b_down, feature_signs, match_blocks, match_count, out_grad,
):
    rows, width = layer_input.shape
    half_width = width // 2
    half_heads = HEADS // 2
    hidden = w_up.shape[1]
    f = lax.axis_index("feat")
    tokens = 2 * rows
    n = lax.axis_size("seq")
    chunk = width // n
    assert lax.axis_size("feat") == 2 and match_blocks.shape[0] == 1 and tokens == SEQLEN

    lists = match_blocks.transpose(0, 1, 3, 2)
    vectors = [ln1_gain, ln1_bias, b_out, ln2_gain, ln2_bias, b_down, b_qkv, b_up]
    lines = sum(a.shape[0] for a in vectors) // width
    feats = 2 * feature_signs.shape[2]
    phi = pltpu.VMEM((tokens, feats), BF)
    masks = [pltpu.VMEM((NB, tokens), BF), pltpu.VMEM((NB, tokens), F32)]
    sign_half = pltpu.VMEM((half_heads, HEAD_DIM, feats // 2), BF)
    two = pltpu.SemaphoreType.DMA((2,))
    params, x, h1, qkv, table, w_own, att, den, kept = call(
        front_body,
        [
            ((lines, width), F32),
            ((tokens, width), BF), ((tokens, width), BF), ((tokens, 3 * half_width), BF),
            ((half_heads // 2, 2 * HEAD_DIM, 2 * feats), BF), ((width, 3 * half_width), BF),
            ((tokens, half_width), BF), ((tokens, half_width), F32), ((half_heads, tokens, tokens), BF),
        ],
        [layer_input, w_qkv, feature_signs, lists, match_count] + vectors,
        specs=[VMEM, ANY] + [VMEM] * (3 + len(vectors)),
        scratch=[sign_half, sign_half] + masks + [
            phi, phi, pltpu.VMEM((2, tokens, tokens), BF), pltpu.VMEM((tokens, 128), F32), two, two,
            pltpu.SemaphoreType.DMA((3,)), two,
        ],
        out_specs=[VMEM] * 8 + [ANY],
        name="front", net=3,
    )
    big, wide = pltpu.VMEM((tokens, width), BF), pltpu.VMEM((tokens, hidden), BF)
    down_bufs = scatter_bufs(n, chunk, hidden)
    down_sems = pltpu.SemaphoreType.DMA((split(n)[0] - 1,))
    pair_sems = pltpu.SemaphoreType.DMA((3 + tokens // TILE + rows // TILE,))
    gm, gatt, d_out, y, vec2, d_up, d_down, d_bup = call(
        functools.partial(mid_body, n),
        [
            ((rows, width), F32), ((tokens, half_width), F32), ((n, chunk, half_width), BF), ((rows, width), BF),
            ((8, width), F32), ((2, n, chunk, hidden // 2), BF), (down_bufs[1].shape, BF), ((1, hidden), F32),
        ],
        [
            x, att, w_out, params, out_grad, w_up, w_down,
        ],
        scratch=[
            pltpu.VMEM((tokens, half_width), BF), big, pltpu.VMEM((tokens, width), F32), big, wide, wide, big, big,
            pltpu.VMEM((rows, width), BF), big, big, pltpu.VMEM((n, chunk, hidden), BF), down_bufs[0],
            pltpu.VMEM((tokens, hidden), F32), pair_sems, pair_sems, down_sems, down_sems,
        ],
        name="mid", net=2,
    )
    slots = sum(split(n)) + split(n)[0] - 3 + 1
    bufs = down_bufs[2:]
    for cols in (hidden // 2, half_width, half_width, half_width, half_width, hidden // 2):
        bufs += scatter_bufs(n, chunk, cols)
    half_chunk = chunk // 2
    sems = pltpu.SemaphoreType.DMA((11, slots))
    sums = call(
        functools.partial(back_body, n),
        [
            ((rows, width), F32), ((chunk, hidden), F32), ((chunk, hidden), F32), ((half_chunk, width), F32),
            ((half_chunk, 3 * width), F32), ((8, 128), F32), ((1, 128), F32), ((1, 128), F32),
        ],
        [
            qkv, table, lists, match_count, kept, att, den, gatt, h1, w_own, layer_input, params, gm, d_up, d_down, d_out, vec2, d_bup,
        ],
        specs=[VMEM] * 4 + [ANY] + [VMEM] * 13,
        scratch=bufs + [pltpu.VMEM((2, tokens, tokens), BF), two] + masks + [
            phi, phi, pltpu.VMEM((tokens, 128), BF), pltpu.VMEM((tokens, 128), F32), pltpu.VMEM((tokens, feats), F32),
            pltpu.VMEM((tokens, 3 * half_width), BF), pltpu.VMEM((3, n, chunk, half_width), BF),
            pltpu.VMEM((rows, width), BF), pltpu.VMEM((rows, width), BF),
            pltpu.VMEM((2, half_chunk, half_width), F32), pltpu.VMEM((half_chunk, half_width), F32),
            pltpu.VMEM((3, 2, half_chunk, half_width), F32), pltpu.VMEM((3, half_chunk, half_width), F32),
            pltpu.VMEM((4 + slots, 8, width), F32), pltpu.VMEM((4 + slots, 1, 3 * width), F32),
            pltpu.VMEM((4 + slots, 1, hidden), F32), sems, sems,
        ],
        name="back", net=1,
    )
    own = width // (2 * n)
    turn = False
    y, dx, up, down, out, full, d_b, d_bup, *vec = call(
        emit_body,
        [
            ((rows, width), BF),
            ((rows, width), F32), ((chunk, hidden), F32), ((hidden, chunk) if turn else (chunk, hidden), F32),
            ((half_chunk, width), F32), ((half_chunk, 3 * width), F32), ((1, 3 * own), F32), ((1, hidden // n), F32),
        ] + [((1, own), F32)] * 6,
        [y] + list(sums), name="emit",
    )
    vec = [v.reshape(-1) for v in vec]
    return (
        y, dx, vec[0], vec[1], full, d_b.reshape(-1), out, vec[4], vec[2], vec[3], up, d_bup.reshape(-1),
        down if turn else down.T, vec[5],
    )


def solution(mesh):
    both = ("seq", "feat")
    return jax.shard_map(
        body,
        mesh=mesh,
        in_specs=(
            P(both, None), P(), P(), P(), P(), P(), P(), P(), P(), P(None, "feat"), P("feat"), P("feat", None), P(),
            P(None, None, "feat"), P("seq", None, None, None), P("seq", None, None), P(both, None),
        ),
        out_specs=(
            P(both, None), P(both, None), P(both), P(both), P(both, None), P(both), P(both, None), P(both), P(both),
            P(both), P("seq", "feat"), P(("feat", "seq")), P("feat", "seq"), P(both),
        ),
        check_vma=False,
    )
```

```python
import functools
import math

import jax
import jax.numpy as jnp
from jax import lax
from jax.experimental import pallas as pl
from jax.experimental.pallas import tpu as pltpu
from jax.sharding import PartitionSpec as P

HEADS = 12
HEAD_DIM = 64
BLOCK = 64
NB = 16
SEQLEN = NB * BLOCK
BF = jnp.bfloat16
F32 = jnp.float32
EPS = 1e-05
TILE = 256
ATILE = 512
BTILE = 512
GELU_A = math.sqrt(2.0 / math.pi)
GELU_B = 0.044715
LOG2E = math.log2(math.e)
GAIN1, BIAS1, BOUT, GAIN2, BIAS2, BDOWN, BQKV, BUP = 0, 1, 2, 3, 4, 5, 6, 9
MESH = pl.DeviceIdType.MESH
VMEM = pl.BlockSpec(memory_space=pltpu.VMEM)
ANY = pl.BlockSpec(memory_space=pl.ANY)


def nn(a, b):
    return lax.dot_general(a, b, (((1,), (0,)), ((), ())), preferred_element_type=F32)


def nt(a, b):
    return lax.dot_general(a, b, (((1,), (1,)), ((), ())), preferred_element_type=F32)


def tn(a, b):
    return lax.dot_general(a, b, (((0,), (0,)), ((), ())), preferred_element_type=F32)


def ds(i, n):
    return pl.ds(i * n if isinstance(i, int) else pl.multiple_of(i * n, n), n)


def norm(x):
    c = x - jnp.mean(x, axis=-1, keepdims=True)
    inv = lax.rsqrt(jnp.mean(c * c, axis=-1, keepdims=True) + EPS)
    return c * inv, inv


def norm_back(g, normed, inv, gain):
    a = g * gain
    return inv * (
        a
        - jnp.mean(a, axis=-1, keepdims=True)
        - normed * jnp.mean(a * normed, axis=-1, keepdims=True)
    )


def split(n):
    p = 1
    while 2 * (2 * p) ** 3 <= n:
        p *= 2
    assert n % (p * p) == 0
    return p, n // (p * p)


class Net:
    def __init__(self, n):
        p, self.nz = split(n)
        self.p = p
        self.s, self.f = lax.axis_index("seq"), lax.axis_index("feat")
        x, y = lax.rem(self.s, p), lax.rem(self.s // p, p)
        f = self.f
        self.sizes = (p, p, self.nz)
        self.at = (x + f * (y - x), y + f * (x - y), self.s // (p * p))
        self.strides = (1 + f * (p - 1), p + f * (1 - p), p * p)

    def place(self, dest):
        p = self.p
        x, y, z = lax.rem(dest, p), lax.rem(dest // p, p), dest // (p * p)
        f = self.f
        return ((x + f * (y - x)) * p + y + f * (x - y)) * self.nz + z

    def peer(self, phase, d):
        j = lax.rem(self.at[phase] + d, self.sizes[phase])
        return j, self.s + (j - self.at[phase]) * self.strides[phase]

    def barrier(self):
        sem = pltpu.get_barrier_semaphore()
        count = 1
        for phase in range(3):
            for d in range(1, self.sizes[phase]):
                pl.semaphore_signal(sem, inc=1, device_id={"seq": self.peer(phase, d)[1]}, device_id_type=MESH)
                count += 1
        pl.semaphore_signal(sem, inc=1, device_id={"feat": 1 - self.f}, device_id_type=MESH)
        pl.semaphore_wait(sem, count)

    def slot(self, phase, d):
        return sum(size - 1 for size in self.sizes[:phase]) + d - 1

    def slots(self):
        return self.slot(3, 1) + 1


def scatter_bufs(n, rows, cols):
    p, nz = split(n)
    return [
        pltpu.VMEM((p - 1, p * nz, rows, cols), BF),
        pltpu.VMEM((p * nz, rows, cols), BF),
        pltpu.VMEM((p - 1, nz, rows, cols), BF),
        pltpu.VMEM((nz, rows, cols), BF),
        pltpu.VMEM((nz - 1, 1, rows, cols), BF),
    ]


class Scatter:
    def __init__(self, net, src, bufs, send, recv):
        self.net, self.send, self.recv = net, send, recv
        self.hold = (src, bufs[1], bufs[3])
        self.got = (bufs[0], bufs[2], bufs[4])

    def block(self, phase, j):
        size = self.got[phase].shape[1]
        return pl.ds(j * size, size)

    def copies(self, phase):
        net, out = self.net, []
        for d in range(1, net.sizes[phase]):
            j, device = net.peer(phase, d)
            k = net.slot(phase, d)
            out.append(
                pltpu.make_async_remote_copy(
                    src_ref=self.hold[phase].at[self.block(phase, j)],
                    dst_ref=self.got[phase].at[d - 1],
                    send_sem=self.send.at[k],
                    recv_sem=self.recv.at[k],
                    device_id={"seq": device},
                    device_id_type=MESH,
                )
            )
        return out

    def start(self, phase):
        for copy in self.copies(phase):
            copy.start()

    def finish(self, phase, put=None):
        for copy in self.copies(phase):
            copy.wait()
        got, own = self.got[phase], self.hold[phase]
        size = got.shape[1]
        base = self.net.at[phase] * size

        def add(i, _):
            total = own[base + i].astype(F32)
            for d in range(got.shape[0]):
                total = total + got[d, i].astype(F32)
            if put is None:
                self.hold[phase + 1][i] = total.astype(BF)
            else:
                put(total)
            return 0

        lax.fori_loop(0, size, add, 0)


class Vector:
    def __init__(self, net, bufs, send, recv):
        self.net, self.bufs, self.send, self.recv = net, bufs, send, recv

    def copies(self, phase):
        net, out = self.net, []
        peers = [({"feat": 1 - net.f}, net.slots() - 1)]
        if phase < 3:
            peers = [({"seq": net.peer(phase, d)[1]}, net.slot(phase, d)) for d in range(1, net.sizes[phase])]
        for device, k in peers:
            out.append(
                pltpu.make_async_remote_copy(
                    src_ref=self.bufs.at[phase],
                    dst_ref=self.bufs.at[4 + k],
                    send_sem=self.send.at[k],
                    recv_sem=self.recv.at[k],
                    device_id=device,
                    device_id_type=MESH,
                )
            )
        return out

    def start(self, phase):
        for copy in self.copies(phase):
            copy.start()

    def finish(self, phase):
        for copy in self.copies(phase):
            copy.wait()
        first, count = (self.net.slots() - 1, 1) if phase == 3 else (self.net.slot(phase, 1), self.net.sizes[phase] - 1)
        total = self.bufs[phase]
        for k in range(count):
            total = total + self.bufs[4 + first + k]
        if phase < 3:
            self.bufs[phase + 1] = total
        return total


def call(body, outs, ins, specs=None, out_specs=None, scratch=(), name=None, net=None):
    return pl.pallas_call(
        body,
        out_shape=[jax.ShapeDtypeStruct(s, d) for s, d in outs],
        in_specs=specs or [VMEM] * len(ins),
        out_specs=out_specs or [VMEM] * len(outs),
        scratch_shapes=list(scratch),
        compiler_params=pltpu.CompilerParams(
            vmem_limit_bytes=64000 * 1024, collective_id=net, has_side_effects=net is not None
        ),
        name=name,
    )(*ins)


def qkv_tiles(first, last, x_ref, p_ref, w_ref, h_ref, qkv_ref):
    width = x_ref.shape[1]
    f = lax.axis_index("feat")
    gain = p_ref[GAIN1 : GAIN1 + 1, :]
    shift = p_ref[BIAS1 : BIAS1 + 1, :]
    bias = jnp.concatenate([p_ref[BQKV + i : BQKV + i + 1, ds(f, width // 2)] for i in range(3)], axis=1)

    def step(i, _):
        rows = ds(i, TILE)
        normed, _inv = norm(x_ref[rows, :].astype(F32))
        h = (normed * gain + shift).astype(BF)
        h_ref[rows, :] = h
        qkv_ref[rows, :] = (nn(h, w_ref[...]) + bias).astype(BF)
        return 0

    lax.fori_loop(first, last, step, 0)


def matches(list_ref, count_ref, h):
    at = lax.axis_index("feat") * (HEADS // 2) + h
    lists, count = list_ref[0, at], count_ref[0, pl.ds(at, 1), :]
    block = lax.broadcasted_iota(jnp.int32, (NB, NB), 0)
    found = jnp.zeros((NB, NB), F32)
    for j in range(lists.shape[0]):
        found = jnp.where((lists[j : j + 1] == block) & (count > j), 1.0, found)
    return found.astype(BF)


def fill_spread(e_ref):
    shift = lax.axis_index("feat") * (NB // 2)
    block = lax.broadcasted_iota(jnp.int32, e_ref.shape, 0)
    token = lax.broadcasted_iota(jnp.int32, e_ref.shape, 1)
    start = lax.rem(block + shift, NB) * BLOCK
    e_ref[...] = jnp.where((token >= start) & (token < start + BLOCK), 1.0, 0.0).astype(BF)


def local_marks(mk_ref, i, tile):
    assert tile * 2 == SEQLEN
    return mk_ref[ds(lax.rem(i + lax.axis_index("feat"), 2), tile // BLOCK), :]


def front_body(
    x_own_ref, w_all_ref, fs_ref, list_ref, count_ref, g1, b1, bo, g2, b2, bd, bqkv, bup,
    p_ref, x_out, h_out, qkv_out, table_ref, att_ref, den_ref, kept_ref,
    x_ref, h_ref, qkv_ref, w_ref, s_send, s_got, e_ref, mk_ref, pq_ref, pk_ref, keep_ref, acc_ref,
    send, recv, local, keep_sems, store,
):
    rows, width = x_own_ref.shape
    own = width // 2
    f = lax.axis_index("feat")
    other = {"feat": 1 - f}

    def copy(k, src, dst):
        return pltpu.make_async_remote_copy(
            src_ref=src, dst_ref=dst, send_sem=send.at[k], recv_sem=recv.at[k], device_id=other, device_id_type=MESH
        )

    loads = [
        pltpu.make_async_copy(w_all_ref.at[:, ds(2 * i + f, own)], w_ref.at[:, pl.ds(i * own, own)], local.at[i])
        for i in range(3)
    ]
    for c in loads:
        c.start()
    barrier = pltpu.get_barrier_semaphore()
    pl.semaphore_signal(barrier, inc=1, device_id=other, device_id_type=MESH)
    pl.semaphore_wait(barrier, 1)
    x_copy = copy(0, x_own_ref, x_ref.at[pl.ds(rows, rows)])
    x_copy.start()
    heads, dim, feats = s_send.shape
    line = 0
    for vector in (g1, b1, bo, g2, b2, bd, bqkv, bup):
        for i in range(vector.shape[0] // width):
            p_ref[line : line + 1, :] = vector[i * width : (i + 1) * width].astype(F32).reshape(1, width)
            line += 1

    def sign(i):
        return (2.0 * fs_ref[i].astype(F32) - 1.0).astype(BF)

    for i in range(heads):
        s_send[i] = sign((1 - f) * heads + i)
    s_copy = copy(1, s_send, s_got)
    s_copy.start()
    x_ref[0:rows, :] = x_own_ref[...]
    table_ref[...] = jnp.zeros_like(table_ref)
    for i in range(heads):
        e = i % 2
        table_ref[i // 2, e * dim : (e + 1) * dim, 2 * e * feats : (2 * e + 1) * feats] = sign(f * heads + i)
    fill_spread(e_ref)
    for c in loads:
        c.wait()
    tiles = rows // TILE
    qkv_tiles(0, tiles, x_ref, p_ref, w_ref, h_ref, qkv_ref)
    s_copy.wait()
    for i in range(heads):
        e = i % 2
        table_ref[i // 2, e * dim : (e + 1) * dim, (2 * e + 1) * feats : (2 * e + 2) * feats] = s_got[i]
    x_copy.wait()
    qkv_tiles(tiles, 2 * tiles, x_ref, p_ref, w_ref, h_ref, qkv_ref)
    pairs = ((x_ref, x_out), (h_ref, h_out), (qkv_ref, qkv_out))
    stores = [pltpu.make_async_copy(src, dst, store.at[i]) for i, (src, dst) in enumerate(pairs)]
    for c in stores:
        c.start()
    att_heads(
        qkv_ref, table_ref, list_ref, count_ref, e_ref, mk_ref, att_ref, den_ref, kept_ref, pq_ref, pk_ref, keep_ref,
        acc_ref, keep_sems,
    )
    for c in stores:
        c.wait()


def head_parts(qkv_ref, h):
    own = qkv_ref.shape[1] // 3
    p, e = h // 2, h % 2
    lane = lax.broadcasted_iota(jnp.int32, (1, 128), 1)
    mine = (lane // HEAD_DIM) == e

    def cols(part):
        return pl.ds(pl.multiple_of(part * own + p * 128, 128), 128)

    return p, e, lane, mine, cols


def lift_all(qkv_ref, s_ref, h, pq_ref, pk_ref):
    p, e, lane, mine, cols = head_parts(qkv_ref, h)
    feats = pq_ref.shape[1]
    signs = s_ref[p, :, ds(e, feats)]

    def step(i, _):
        rows = ds(i, TILE)
        for part, out in ((0, pq_ref), (1, pk_ref)):
            t = qkv_ref[rows, cols(part)]
            w = jnp.where(mine, t.astype(F32), 0.0)
            sq = jnp.sum(w * w, axis=-1, keepdims=True) * (LOG2E * 0.5 * HEAD_DIM ** (-0.5)) + 0.5 * math.log2(feats)
            out[rows, :] = jnp.exp2(nn(t, signs) * (LOG2E * HEAD_DIM ** (-0.25)) - sq).astype(BF)
        return 0

    lax.fori_loop(0, qkv_ref.shape[0] // TILE, step, 0)


def att_heads(
    qkv_ref, s_ref, list_ref, count_ref, e_ref, mk_ref, att_ref, den_ref, kept_ref, pq_ref, pk_ref, p_ref, acc_ref, sems
):
    heads = qkv_ref.shape[1] // (3 * HEAD_DIM)

    def keep(h):
        slot = lax.rem(h, 2)
        return pltpu.make_async_copy(p_ref.at[slot], kept_ref.at[h], sems.at[slot])

    def head(h, _):
        p, e, lane, mine, cols = head_parts(qkv_ref, h)
        slot = lax.rem(h, 2)
        mk_ref[...] = nn(matches(list_ref, count_ref, h), e_ref[...])
        lift_all(qkv_ref, s_ref, h, pq_ref, pk_ref)
        zero = jnp.zeros((), BF)

        @pl.when(h >= 2)
        def _():
            keep(h - 2).wait()

        acc_ref[...] = jnp.zeros_like(acc_ref)

        def step(i, _):
            rows = ds(i, ATILE)
            k = jnp.where(mine, qkv_ref[rows, cols(1)] * BF(HEAD_DIM ** (-0.5)), zero)
            v_one = jnp.where(mine, qkv_ref[rows, cols(2)], jnp.ones((), BF))
            ex = jnp.exp(nt(k, qkv_ref[:, cols(0)]))
            low = nt(pk_ref[rows, :], pq_ref[...])
            marks = local_marks(mk_ref, i, ATILE)
            probs = jnp.concatenate(
                [
                    jnp.where(
                        marks[j : j + 1, :] > 0.5,
                        ex[j * BLOCK : (j + 1) * BLOCK],
                        low[j * BLOCK : (j + 1) * BLOCK],
                    )
                    for j in range(ATILE // BLOCK)
                ],
                axis=0,
            ).astype(BF)
            p_ref[slot, rows, :] = probs
            acc_ref[...] += tn(probs, v_one)
            return 0

        lax.fori_loop(0, qkv_ref.shape[0] // ATILE, step, 0)
        keep(h).start()

        def last(i, _):
            rows = ds(i, TILE)
            both = acc_ref[rows, :]
            den = pltpu.roll(both, HEAD_DIM, 1)
            out_cols = ds(p, 128)
            att = (both / den).astype(BF)
            att_ref[rows, out_cols] = jnp.where(mine, att, att_ref[rows, out_cols])
            den_ref[rows, out_cols] = jnp.where(mine, den, den_ref[rows, out_cols])
            return 0

        lax.fori_loop(0, qkv_ref.shape[0] // TILE, last, 0)
        return 0

    lax.fori_loop(0, heads, head, 0)
    keep(heads - 2).wait()
    keep(heads - 1).wait()


def mix_tiles(x_ref, mine_ref, other_ref, w_ref, b_ref, g_ref, s_ref, mixed_ref, h_ref):
    f = lax.axis_index("feat")
    half = mine_ref.shape[1]

    def step(i, _):
        rows = ds(i, TILE)
        mixed = (
            x_ref[rows, :].astype(F32)
            + nn(mine_ref[rows, :], w_ref[ds(f, half), :])
            + nn(other_ref[rows, :], w_ref[ds(1 - f, half), :])
            + b_ref[...].astype(F32)
        )
        mixed_ref[rows, :] = mixed
        normed, _inv = norm(mixed)
        h_ref[rows, :] = (normed * g_ref[...].astype(F32) + s_ref[...].astype(F32)).astype(BF)
        return 0

    lax.fori_loop(0, x_ref.shape[0] // TILE, step, 0)


def ff_forward(h_ref, up_ref, down_ref, bias, act_ref, slope_ref, hid_ref, send):
    tiles = h_ref.shape[0] // TILE

    def step(i, _):
        tile = lax.rem(i + tiles // 2, tiles)
        rows = ds(tile, TILE)
        v = nn(h_ref[rows, :], up_ref[...]) + bias
        vv = v * v
        th = jnp.tanh(GELU_A * v * (1.0 + GELU_B * vv))
        half = 0.5 + 0.5 * th
        act = (v * half).astype(BF)
        slope_ref[rows, :] = half + (0.5 * GELU_A) * v * (1.0 - th * th) * (1.0 + (3.0 * GELU_B) * vv)
        act_ref[rows, :] = act
        hid_ref[rows, :] = nn(act, down_ref[...]).astype(BF)
        send(i, tile)
        return 0

    lax.fori_loop(0, tiles, step, 0)


def ff_backward(og_ref, up_ref, down_ref, slope_ref, gp_ref, gh_ref, db_ref, send):
    tiles = og_ref.shape[0] // TILE
    db_ref[...] = jnp.zeros_like(db_ref)

    def step(i, _):
        tile = lax.rem(i + tiles // 2, tiles)
        rows = ds(tile, TILE)
        gp = (nt(og_ref[rows, :], down_ref[...]) * slope_ref[rows, :]).astype(BF)
        gp_ref[rows, :] = gp
        db_ref[...] += jnp.sum(gp.astype(F32), axis=0, keepdims=True)
        gh_ref[rows, :] = nt(gp, up_ref[...]).astype(BF)
        send(i, tile)
        return 0

    lax.fori_loop(0, tiles, step, 0)


def put_chunks(out_ref, first, value, net):
    rows = out_ref.shape[1]
    for i in range(value.shape[0] // rows):
        out_ref[net.place(first + i)] = value[i * rows : (i + 1) * rows].astype(BF)


def ff_weight(net, lhs_ref, rhs_ref, outs):
    wide = lhs_ref.shape[1] // 2
    per = wide // outs[0].shape[1]

    def step(i, _):
        value = tn(lhs_ref[:, ds(i, wide)], rhs_ref[...])
        for j, out in enumerate(outs):
            put_chunks(out, i * per, value[:, j * out.shape[2] : (j + 1) * out.shape[2]], net)
        return 0

    lax.fori_loop(0, 2, step, 0)


def out_back(
    n, gh_ref, gho_ref, mixed_ref, og_ref, hid_ref, hido_ref, bd_ref, g_ref, w_ref, mine_ref, other_ref,
    gm_ref, gatt_ref, dw_ref, y_ref, vec_ref, gb_ref,
):
    f = lax.axis_index("feat")
    half = mine_ref.shape[1]
    tiles = mixed_ref.shape[0] // TILE
    own = tiles // 2
    gain = g_ref[...].astype(F32)
    vec_ref[...] = jnp.zeros_like(vec_ref)

    def step(i, _):
        rows = ds(i, TILE)
        mixed = mixed_ref[rows, :]
        og = og_ref[rows, :].astype(F32)
        normed, inv = norm(mixed)
        g = gh_ref[rows, :].astype(F32) + gho_ref[rows, :].astype(F32)
        gm = og + norm_back(g, normed, inv, gain)
        gb = gm.astype(BF)
        gb_ref[rows, :] = gb
        gatt_ref[rows, :] = nt(gb, w_ref[ds(f, half), :])

        @pl.when(i < own)
        def _():
            gm_ref[rows, :] = gm
            y_ref[rows, :] = (
                mixed + hid_ref[rows, :].astype(F32) + hido_ref[rows, :].astype(F32) + bd_ref[...].astype(F32)
            ).astype(BF)
            for j, term in enumerate((g * normed, g, gb.astype(F32), og)):
                vec_ref[j + 2 : j + 3, :] += jnp.sum(term, axis=0, keepdims=True)

        return 0

    lax.fori_loop(0, tiles, step, 0)
    gb_own = gb_ref[:, ds(f, half)]
    net = Net(n)
    per = half // dw_ref.shape[1]
    put_chunks(dw_ref, f * per, tn(mine_ref[...], gb_own), net)
    put_chunks(dw_ref, (1 - f) * per, tn(other_ref[...], gb_own), net)


def mid_body(
    n, x_ref, att_ref, wout_ref, p_ref, og_own_ref, up_all, down_all,
    gm_ref, gatt_ref, dout_ref, y_ref, vec_ref, dup_ref, ddown_ref, dbup_ref,
    far, og, mixed, h, act, gp, hid, gh, hid_got, gh_got, gb, ddown, ddown_got, slope, up_ref, down_ref, send, recv, down_send, down_recv, local,
):
    net = Net(n)
    down = Scatter(net, ddown, [ddown_got, ddown_ref, None, None, None], down_send, down_recv)
    bout_ref, g_ref, s_ref, bdown_ref = [p_ref.at[i : i + 1] for i in (BOUT, GAIN2, BIAS2, BDOWN)]
    bup = jnp.concatenate([p_ref[i : i + 1, :] for i in range(BUP, p_ref.shape[0])], axis=1)
    rows = og_own_ref.shape[0]
    tiles = h.shape[0] // TILE
    other = {"feat": 1 - lax.axis_index("feat")}

    def copy(k, src, dst):
        return pltpu.make_async_remote_copy(
            src_ref=src, dst_ref=dst, send_sem=send.at[k], recv_sem=recv.at[k], device_id=other, device_id_type=MESH
        )

    loads = [pltpu.make_async_copy(a, b, local.at[i]) for i, (a, b) in enumerate(((up_all, up_ref), (down_all, down_ref)))]
    for c in loads:
        c.start()
    net.barrier()
    low, high = pl.ds(0, rows), pl.ds(rows, rows)
    atts = [copy(0, att_ref.at[low], far.at[high]), copy(1, att_ref.at[high], far.at[low])]
    og_copy = copy(2, og_own_ref, og.at[high])
    for c in atts:
        c.start()
    og_copy.start()
    og[low, :] = og_own_ref[...]
    for c in atts:
        c.wait()
    mix_tiles(x_ref, att_ref, far, wout_ref, bout_ref, g_ref, s_ref, mixed, h)

    def gh_copy(i, tile):
        return copy(3 + i, gh.at[ds(tile, TILE)], gh_got.at[ds(i, TILE)])

    def hid_copy(i, tile):
        return copy(3 + tiles + i, hid.at[ds(tile, TILE)], hid_got.at[ds(i, TILE)])

    def send_gh(i, tile):
        gh_copy(i, tile).start()

    def send_hid(i, tile):
        @pl.when(i < tiles // 2)
        def _():
            hid_copy(i, tile).start()

    for c in loads:
        c.wait()
    ff_forward(h, up_ref, down_ref, bup, act, slope, hid, send_hid)
    og_copy.wait()
    ff_weight(net, og, act, [ddown])
    down.start(0)
    ff_backward(og, up_ref, down_ref, slope, gp, gh, dbup_ref, send_gh)
    ff_weight(net, h, gp, [dup_ref.at[0], dup_ref.at[1]])
    for i in range(tiles):
        gh_copy(i, (i + tiles // 2) % tiles).wait()
    for i in range(tiles // 2):
        hid_copy(i, i + tiles // 2).wait()
    out_back(
        n, gh, gh_got, mixed, og, hid, hid_got, bdown_ref, g_ref, wout_ref, att_ref, far,
        gm_ref, gatt_ref, dout_ref, y_ref, vec_ref, gb,
    )
    down.finish(0)


def heads_back(
    qkv_ref, s_ref, list_ref, count_ref, kept_ref, p_ref, sems, e_ref, mk_ref, att_ref, den_ref, gatt_ref, gqkv_ref, pq_ref, pk_ref, gn_ref, gq_ref, gpq_ref, after
):
    rows_all = qkv_ref.shape[0]
    scale = HEAD_DIM ** (-0.5)

    heads = qkv_ref.shape[1] // (3 * HEAD_DIM)

    def fetch(h):
        slot = lax.rem(h, 2)
        return pltpu.make_async_copy(kept_ref.at[h], p_ref.at[slot], sems.at[slot])

    fetch(0).start()

    def head(h, _):
        slot = lax.rem(h, 2)

        @pl.when(h + 1 < heads)
        def _():
            fetch(h + 1).start()

        p, e, lane, mine, cols = head_parts(qkv_ref, h)
        feats = pq_ref.shape[1]
        zero = jnp.zeros((), BF)
        mk_ref[...] = nn(matches(list_ref, count_ref, h), e_ref[...])
        lift_all(qkv_ref, s_ref, h, pq_ref, pk_ref)
        first_other = (1 - e) * HEAD_DIM

        def prep(i, _):
            rows = ds(i, TILE)
            inv = 1.0 / den_ref[rows, ds(p, 128)]
            ga = jnp.where(mine, gatt_ref[rows, ds(p, 128)] * inv, 0.0)
            gd = -jnp.sum(ga * att_ref[rows, ds(p, 128)].astype(F32), axis=-1, keepdims=True)
            gn_ref[rows, :] = jnp.where(lane == first_other, gd, ga).astype(BF)
            return 0

        lax.fori_loop(0, rows_all // TILE, prep, 0)
        gq_ref[...] = jnp.zeros_like(gq_ref)
        gpq_ref[...] = jnp.zeros_like(gpq_ref)
        signs = s_ref[p, :, ds(e, feats)]

        def lift_back(t, raw, g_phi):
            gl = g_phi * raw.astype(F32)
            gt = nt(gl.astype(BF), signs) * HEAD_DIM ** (-0.25)
            return gt - jnp.sum(gl, axis=-1, keepdims=True) * (scale * t.astype(F32))

        def put(part, rows, value):
            gqkv_ref[rows, cols(part)] = jnp.where(mine, value.astype(BF), gqkv_ref[rows, cols(part)])

        fetch(h).wait()

        def step(i, _):
            rows = ds(i, BTILE)
            k = jnp.where(mine, qkv_ref[rows, cols(1)] * BF(scale), zero)
            v_one = jnp.where(mine, qkv_ref[rows, cols(2)], jnp.ones((), BF))
            q_all = qkv_ref[:, cols(0)]
            pk = pk_ref[rows, :]
            probs = p_ref[slot, rows, :]
            da = nt(v_one, gn_ref[...])
            marks = local_marks(mk_ref, i, BTILE)
            dl, gs = [], []
            for j in range(BTILE // BLOCK):
                part = slice(j * BLOCK, (j + 1) * BLOCK)
                on = marks[j : j + 1, :] > 0.5
                daj = da[part]
                dl.append(jnp.where(on, 0.0, daj))
                gs.append(jnp.where(on, daj * probs[part].astype(F32), 0.0))
            dl = jnp.concatenate(dl, axis=0).astype(BF)
            gs = jnp.concatenate(gs, axis=0).astype(BF)
            put(2, rows, nn(probs, gn_ref[...]))
            g_phi_k = nn(dl, pq_ref[...])
            gk = nn(gs, q_all) * scale + lift_back(qkv_ref[rows, cols(1)], pk, g_phi_k)
            put(1, rows, gk)
            gpq_ref[...] += tn(dl, pk)
            gq_ref[...] += tn(gs, k)
            return 0

        lax.fori_loop(0, rows_all // BTILE, step, 0)

        def last(i, _):
            rows = ds(i, TILE)
            gq = gq_ref[rows, :] + lift_back(qkv_ref[rows, cols(0)], pq_ref[rows, :], gpq_ref[rows, :])
            put(0, rows, gq)
            return 0

        lax.fori_loop(0, rows_all // TILE, last, 0)
        for k, then in after.items():
            pl.when(h == k)(then)
        return 0

    lax.fori_loop(0, qkv_ref.shape[1] // (3 * HEAD_DIM), head, 0)


def back_body(
    n, qkv_ref, s_ref, list_ref, count_ref, kept_ref, att_ref, den_ref, gatt_ref, h_all, w_all, x_all, p_ref, gm_all, up_ref, down_ref, out_ref,
    vec_ref, bup_ref, dx_ref, oup_ref, odown_ref, oout_ref, oqkv_ref, orows_ref, obqkv_ref, obup_ref, *scratch,
):
    net = Net(n)
    bufs, tail = (None, down_ref) + scratch[:33], scratch[33:]
    kept_buf, keep_sems, h_ref, w_ref, x_ref, gm_ref, local, e_ref, mk_ref, pq, pk, gn, gq, gpq, gqkv, gw, gh_send, gh_got, sout, rout, sqkv, rqkv, vrows, vbqkv, vbup, send, recv = tail
    f = net.f
    other = {"feat": 1 - f}
    sources = (None, up_ref.at[0], out_ref, gw.at[0], gw.at[1], gw.at[2], up_ref.at[1])
    lanes_of = (0, 1, 2, 3, 4, 5, 10)
    down, up_low, out, *pairs, up_high = [
        Scatter(net, src, bufs[5 * i : 5 * i + 5], send.at[k], recv.at[k])
        for i, (src, k) in enumerate(zip(sources, lanes_of))
    ]
    vectors = [Vector(net, ref, send.at[6 + i], recv.at[6 + i]) for i, ref in enumerate((vrows, vbqkv, vbup))]
    last = net.slots() - 1
    half = sout.shape[1]
    rows = x_ref.shape[0]
    width = x_ref.shape[1]
    own = width // 2
    lanes = orows_ref.shape[1]

    def whole(ref):
        def put(total):
            ref[...] = total

        return put

    def halves(ref):
        def put(total):
            ref[0], ref[1] = total[:half], total[half:]

        return put

    def swap(i, src, dst):
        return pltpu.make_async_remote_copy(
            src_ref=src, dst_ref=dst, send_sem=send.at[i, last], recv_sem=recv.at[i, last],
            device_id=other, device_id_type=MESH,
        )

    def move(part, phase):
        part.finish(phase)
        part.start(phase + 1)

    def weight(p):
        g = jnp.concatenate([gqkv[:, i * own + p * 128 : i * own + (p + 1) * 128] for i in range(3)], axis=1)
        per = own // gw.shape[2]
        for i in range(2):
            put_chunks(gw.at[p], i * per, tn(h_ref[:, i * own : (i + 1) * own], g), net)
        pairs[p].start(0)

    loads = [
        pltpu.make_async_copy(a, b, local.at[i])
        for i, (a, b) in enumerate(((h_all, h_ref), (x_all, x_ref), (gm_all, gm_ref)))
    ] + [
        pltpu.make_async_copy(w_all.at[:, ds(2 * i + f, own)], w_ref.at[:, pl.ds(i * own, own)], local.at[3 + i])
        for i in range(3)
    ]
    for c in loads:
        c.start()
    fill_spread(e_ref)
    net.barrier()
    down.start(1)
    up_low.start(0)
    up_high.start(0)
    out.start(0)

    def after1():
        move(down, 1)
        move(up_low, 0)
        loads[0].wait()
        weight(0)

    def after2():
        move(up_high, 0)
        move(up_low, 1)

    def after3():
        move(out, 0)
        move(pairs[0], 0)
        move(up_high, 1)
        weight(1)

    def after4():
        down.finish(2, whole(odown_ref))
        move(out, 1)
        move(pairs[0], 1)
        move(pairs[1], 0)

    heads_back(
        qkv_ref, s_ref, list_ref, count_ref, kept_ref, kept_buf, keep_sems, e_ref, mk_ref, att_ref, den_ref, gatt_ref, gqkv, pq, pk, gn, gq, gpq,
        {1: after1, 2: after2, 3: after3, 4: after4},
    )
    weight(2)
    for c in loads[1:]:
        c.wait()
    tiles = rows // TILE

    def far(i, total):
        g = gqkv[ds(tiles + i, TILE), :]
        gh_send[ds(i, TILE), :] = nt(g, w_ref[...]).astype(BF)
        return total + jnp.sum(g.astype(F32), axis=0, keepdims=True)

    total = lax.fori_loop(0, tiles, far, jnp.zeros((1, 3 * own), F32))
    gh_swap = swap(9, gh_send, gh_got)
    gh_swap.start()
    move(pairs[1], 1)

    def sums(i, total):
        return total + jnp.sum(gqkv[ds(i, TILE), :].astype(F32), axis=0, keepdims=True)

    total = lax.fori_loop(0, tiles, sums, total)
    vbqkv[0] = jnp.zeros_like(vbqkv[0])
    for i in range(3):
        vbqkv[0, :, ds(2 * i + f, own)] = total[:, i * own : (i + 1) * own]
    vbup[0] = bup_ref[...]
    up_low.finish(2, whole(oup_ref.at[:, 0 : oup_ref.shape[1] // 2]))
    out.finish(2, halves(sout))
    out_swap = swap(2, sout.at[1 - f], rout)
    out_swap.start()
    move(pairs[2], 0)
    up_high.finish(2, whole(oup_ref.at[:, oup_ref.shape[1] // 2 :]))
    gh_swap.wait()
    gain = p_ref[GAIN1 : GAIN1 + 1, :]
    vrows[0] = vec_ref[...]

    def norm1(i, _):
        r = ds(i, TILE)
        normed, inv = norm(x_ref[r, :].astype(F32))
        g = nt(gqkv[r, :], w_ref[...]) + gh_got[r, :].astype(F32)
        dx_ref[r, :] = gm_ref[r, :] + norm_back(g, normed, inv, gain)
        vrows[0, 0:1, :] += jnp.sum(g * normed, axis=0, keepdims=True)
        vrows[0, 1:2, :] += jnp.sum(g, axis=0, keepdims=True)
        return 0

    lax.fori_loop(0, tiles, norm1, 0)
    for v in vectors:
        v.start(0)
    move(pairs[2], 1)
    for p in (0, 1):
        pairs[p].finish(2, halves(sqkv.at[p]))
    for v in vectors:
        v.finish(0)
        v.start(1)
    swaps = [swap(3 + p, sqkv.at[p, 1 - f], rqkv.at[p]) for p in range(3)]
    swaps[0].start()
    swaps[1].start()
    for v in vectors:
        v.finish(1)
        v.start(2)
    pairs[2].finish(2, halves(sqkv.at[2]))
    swaps[2].start()
    vecs, bqkv, bup = [v.finish(2) for v in vectors]
    vectors[0].start(3)
    vectors[1].start(3)
    where = 2 * net.s + f

    def cut(value, per, index, size):
        return pltpu.roll(value, lax.rem(size - index * per, size), 1)[:, :lanes]

    obup_ref[...] = cut(bup, bup.shape[1] // n, net.s, bup.shape[1])
    out_swap.wait()
    oout_ref[:, ds(f, own)] = sout[f]
    oout_ref[:, ds(1 - f, own)] = rout[...]

    def cols(i, p, side):
        return pl.ds(pl.multiple_of(i * width + side * own + p * 128, 128), 128)

    for p in range(3):
        swaps[p].wait()
        for i in range(3):
            part = slice(i * 128, (i + 1) * 128)
            oqkv_ref[:, cols(i, p, f)] = sqkv[p, f, :, part]
            oqkv_ref[:, cols(i, p, 1 - f)] = rqkv[p, :, part]
    vecs = vectors[0].finish(3)
    bqkv = vectors[1].finish(3)
    orows_ref[...] = cut(vecs, width // (2 * n), where, width)
    obqkv_ref[...] = cut(bqkv, bqkv.shape[1] // (2 * n), where, bqkv.shape[1])


def emit_body(y_ref, dx_ref, up_ref, down_ref, out_ref, qkv_ref, rows_ref, bqkv_ref, bup_ref, *outs):
    oy, odx, oup, odown, oout, oqkv, obqkv, obup = outs[:8]
    oy[...] = y_ref[...]
    odx[...], oup[...], oout[...], oqkv[...] = dx_ref[...], up_ref[...], out_ref[...], qkv_ref[...]
    down = down_ref[...]
    odown[...] = down if odown.shape == down.shape else down.T
    obqkv[...] = bqkv_ref[:, : obqkv.shape[1]]
    obup[...] = bup_ref[:, : obup.shape[1]]
    for i, ref in enumerate(outs[8:]):
        ref[...] = rows_ref[i : i + 1, : ref.shape[1]]


def body(
    layer_input, ln1_gain, ln1_bias, w_qkv, b_qkv, w_out, b_out, ln2_gain, ln2_bias,
    w_up, b_up, w_down, b_down, feature_signs, match_blocks, match_count, out_grad,
):
    rows, width = layer_input.shape
    half_width = width // 2
    half_heads = HEADS // 2
    hidden = w_up.shape[1]
    f = lax.axis_index("feat")
    tokens = 2 * rows
    n = lax.axis_size("seq")
    chunk = width // n
    assert lax.axis_size("feat") == 2 and match_blocks.shape[0] == 1 and tokens == SEQLEN

    lists = match_blocks.transpose(0, 1, 3, 2)
    vectors = [ln1_gain, ln1_bias, b_out, ln2_gain, ln2_bias, b_down, b_qkv, b_up]
    lines = sum(a.shape[0] for a in vectors) // width
    feats = 2 * feature_signs.shape[2]
    phi = pltpu.VMEM((tokens, feats), BF)
    masks = [pltpu.VMEM((NB, tokens), BF), pltpu.VMEM((NB, tokens), F32)]
    sign_half = pltpu.VMEM((half_heads, HEAD_DIM, feats // 2), BF)
    two, three = pltpu.SemaphoreType.DMA((2,)), pltpu.SemaphoreType.DMA((3,))
    full, qkv_buf = pltpu.VMEM((tokens, width), BF), pltpu.VMEM((tokens, 3 * half_width), BF)
    w_buf = pltpu.VMEM((width, 3 * half_width), BF)
    params, x, h1, qkv, table, att, den, kept = call(
        front_body,
        [
            ((lines, width), F32),
            ((tokens, width), BF), ((tokens, width), BF), ((tokens, 3 * half_width), BF),
            ((half_heads // 2, 2 * HEAD_DIM, 2 * feats), BF),
            ((tokens, half_width), BF), ((tokens, half_width), F32), ((half_heads, tokens, tokens), BF),
        ],
        [layer_input, w_qkv, feature_signs, lists, match_count] + vectors,
        specs=[VMEM, ANY] + [VMEM] * (3 + len(vectors)),
        scratch=[full, full, qkv_buf, w_buf, sign_half, sign_half] + masks + [
            phi, phi, pltpu.VMEM((2, tokens, tokens), BF), pltpu.VMEM((tokens, 128), F32), two, two,
            three, two, three,
        ],
        out_specs=[VMEM, ANY, ANY, ANY, VMEM, VMEM, VMEM, ANY],
        name="front", net=3,
    )
    big, wide = pltpu.VMEM((tokens, width), BF), pltpu.VMEM((tokens, hidden), BF)
    down_bufs = scatter_bufs(n, chunk, hidden)
    down_sems = pltpu.SemaphoreType.DMA((split(n)[0] - 1,))
    pair_sems = pltpu.SemaphoreType.DMA((3 + tokens // TILE + rows // TILE,))
    gm, gatt, d_out, y, vec2, d_up, d_down, d_bup = call(
        functools.partial(mid_body, n),
        [
            ((rows, width), F32), ((tokens, half_width), F32), ((n, chunk, half_width), BF), ((rows, width), BF),
            ((8, width), F32), ((2, n, chunk, hidden // 2), BF), (down_bufs[1].shape, BF), ((1, hidden), F32),
        ],
        [
            x, att, w_out, params, out_grad, w_up, w_down,
        ],
        specs=[VMEM] * 5 + [ANY] * 2,
        scratch=[
            pltpu.VMEM((tokens, half_width), BF), big, pltpu.VMEM((tokens, width), F32), big, wide, wide, big, big,
            pltpu.VMEM((rows, width), BF), big, big, pltpu.VMEM((n, chunk, hidden), BF), down_bufs[0],
            pltpu.VMEM((tokens, hidden), F32), pltpu.VMEM((width, hidden), BF), pltpu.VMEM((hidden, width), BF),
            pair_sems, pair_sems, down_sems, down_sems, two,
        ],
        name="mid", net=2,
    )
    slots = sum(split(n)) + split(n)[0] - 3 + 1
    bufs = down_bufs[2:]
    for cols in (hidden // 2, half_width, half_width, half_width, half_width, hidden // 2):
        bufs += scatter_bufs(n, chunk, cols)
    half_chunk = chunk // 2
    sems = pltpu.SemaphoreType.DMA((11, slots))
    sums = call(
        functools.partial(back_body, n),
        [
            ((rows, width), F32), ((chunk, hidden), F32), ((chunk, hidden), F32), ((half_chunk, width), F32),
            ((half_chunk, 3 * width), F32), ((8, 128), F32), ((1, 128), F32), ((1, 128), F32),
        ],
        [
            qkv, table, lists, match_count, kept, att, den, gatt, h1, w_qkv, layer_input, params, gm, d_up, d_down, d_out, vec2, d_bup,
        ],
        specs=[VMEM] * 4 + [ANY] + [VMEM] * 3 + [ANY] * 3 + [VMEM, ANY] + [VMEM] * 5,
        scratch=bufs + [
            pltpu.VMEM((2, tokens, tokens), BF), two, full, w_buf, pltpu.VMEM((rows, width), BF),
            pltpu.VMEM((rows, width), F32), pltpu.SemaphoreType.DMA((6,)),
        ] + masks + [
            phi, phi, pltpu.VMEM((tokens, 128), BF), pltpu.VMEM((tokens, 128), F32), pltpu.VMEM((tokens, feats), F32),
            pltpu.VMEM((tokens, 3 * half_width), BF), pltpu.VMEM((3, n, chunk, half_width), BF),
            pltpu.VMEM((rows, width), BF), pltpu.VMEM((rows, width), BF),
            pltpu.VMEM((2, half_chunk, half_width), F32), pltpu.VMEM((half_chunk, half_width), F32),
            pltpu.VMEM((3, 2, half_chunk, half_width), F32), pltpu.VMEM((3, half_chunk, half_width), F32),
            pltpu.VMEM((4 + slots, 8, width), F32), pltpu.VMEM((4 + slots, 1, 3 * width), F32),
            pltpu.VMEM((4 + slots, 1, hidden), F32), sems, sems,
        ],
        name="back", net=1,
    )
    own = width // (2 * n)
    turn = False
    y, dx, up, down, out, full, d_b, d_bup, *vec = call(
        emit_body,
        [
            ((rows, width), BF),
            ((rows, width), F32), ((chunk, hidden), F32), ((hidden, chunk) if turn else (chunk, hidden), F32),
            ((half_chunk, width), F32), ((half_chunk, 3 * width), F32), ((1, 3 * own), F32), ((1, hidden // n), F32),
        ] + [((1, own), F32)] * 6,
        [y] + list(sums), name="emit",
    )
    vec = [v.reshape(-1) for v in vec]
    return (
        y, dx, vec[0], vec[1], full, d_b.reshape(-1), out, vec[4], vec[2], vec[3], up, d_bup.reshape(-1),
        down if turn else down.T, vec[5],
    )


def solution(mesh):
    both = ("seq", "feat")
    return jax.shard_map(
        body,
        mesh=mesh,
        in_specs=(
            P(both, None), P(), P(), P(), P(), P(), P(), P(), P(), P(None, "feat"), P("feat"), P("feat", None), P(),
            P(None, None, "feat"), P("seq", None, None, None), P("seq", None, None), P(both, None),
        ),
        out_specs=(
            P(both, None), P(both, None), P(both), P(both), P(both, None), P(both), P(both, None), P(both), P(both),
            P(both), P("seq", "feat"), P(("feat", "seq")), P("feat", "seq"), P(both),
        ),
        check_vma=False,
    )
```

```python
import functools
import math

import jax
import jax.numpy as jnp
from jax import lax
from jax.experimental import pallas as pl
from jax.experimental.pallas import tpu as pltpu
from jax.sharding import PartitionSpec as P

HEADS = 12
HEAD_DIM = 64
BLOCK = 64
NB = 16
SEQLEN = NB * BLOCK
BF = jnp.bfloat16
F32 = jnp.float32
EPS = 1e-05
TILE = 256
ATILE = 512
BTILE = 512
WTILE = 512
GELU_A = math.sqrt(2.0 / math.pi)
GELU_B = 0.044715
LOG2E = math.log2(math.e)
GAIN1, BIAS1, BOUT, GAIN2, BIAS2, BDOWN, BQKV, BUP = 0, 1, 2, 3, 4, 5, 6, 9
MESH = pl.DeviceIdType.MESH
VMEM = pl.BlockSpec(memory_space=pltpu.VMEM)
ANY = pl.BlockSpec(memory_space=pl.ANY)


def nn(a, b):
    return lax.dot_general(a, b, (((1,), (0,)), ((), ())), preferred_element_type=F32)


def nt(a, b):
    return lax.dot_general(a, b, (((1,), (1,)), ((), ())), preferred_element_type=F32)


def tn(a, b):
    return lax.dot_general(a, b, (((0,), (0,)), ((), ())), preferred_element_type=F32)


def ds(i, n):
    return pl.ds(i * n if isinstance(i, int) else pl.multiple_of(i * n, n), n)


def norm(x):
    c = x - jnp.mean(x, axis=-1, keepdims=True)
    inv = lax.rsqrt(jnp.mean(c * c, axis=-1, keepdims=True) + EPS)
    return c * inv, inv


def norm_back(g, normed, inv, gain):
    a = g * gain
    return inv * (
        a
        - jnp.mean(a, axis=-1, keepdims=True)
        - normed * jnp.mean(a * normed, axis=-1, keepdims=True)
    )


def split(n):
    p = 1
    while 2 * (2 * p) ** 3 <= n:
        p *= 2
    assert n % (p * p) == 0
    return p, n // (p * p)


class Net:
    def __init__(self, n):
        p, self.nz = split(n)
        self.p = p
        self.s, self.f = lax.axis_index("seq"), lax.axis_index("feat")
        x, y = lax.rem(self.s, p), lax.rem(self.s // p, p)
        f = self.f
        self.sizes = (p, p, self.nz)
        self.at = (x + f * (y - x), y + f * (x - y), self.s // (p * p))
        self.strides = (1 + f * (p - 1), p + f * (1 - p), p * p)

    def place(self, dest):
        p = self.p
        x, y, z = lax.rem(dest, p), lax.rem(dest // p, p), dest // (p * p)
        f = self.f
        return ((x + f * (y - x)) * p + y + f * (x - y)) * self.nz + z

    def peer(self, phase, d):
        j = lax.rem(self.at[phase] + d, self.sizes[phase])
        return j, self.s + (j - self.at[phase]) * self.strides[phase]

    def barrier(self):
        sem = pltpu.get_barrier_semaphore()
        count = 1
        for phase in range(3):
            for d in range(1, self.sizes[phase]):
                pl.semaphore_signal(sem, inc=1, device_id={"seq": self.peer(phase, d)[1]}, device_id_type=MESH)
                count += 1
        pl.semaphore_signal(sem, inc=1, device_id={"feat": 1 - self.f}, device_id_type=MESH)
        pl.semaphore_wait(sem, count)

    def slot(self, phase, d):
        return sum(size - 1 for size in self.sizes[:phase]) + d - 1

    def slots(self):
        return self.slot(3, 1) + 1


def scatter_bufs(n, rows, cols):
    p, nz = split(n)
    return [
        pltpu.VMEM((p - 1, p * nz, rows, cols), BF),
        pltpu.VMEM((p * nz, rows, cols), BF),
        pltpu.VMEM((p - 1, nz, rows, cols), BF),
        pltpu.VMEM((nz, rows, cols), BF),
        pltpu.VMEM((nz - 1, 1, rows, cols), BF),
    ]


class Scatter:
    def __init__(self, net, src, bufs, send, recv):
        self.net, self.send, self.recv = net, send, recv
        self.hold = (src, bufs[1], bufs[3])
        self.got = (bufs[0], bufs[2], bufs[4])

    def block(self, phase, j):
        size = self.got[phase].shape[1]
        return pl.ds(j * size, size)

    def copies(self, phase):
        net, out = self.net, []
        for d in range(1, net.sizes[phase]):
            j, device = net.peer(phase, d)
            k = net.slot(phase, d)
            out.append(
                pltpu.make_async_remote_copy(
                    src_ref=self.hold[phase].at[self.block(phase, j)],
                    dst_ref=self.got[phase].at[d - 1],
                    send_sem=self.send.at[k],
                    recv_sem=self.recv.at[k],
                    device_id={"seq": device},
                    device_id_type=MESH,
                )
            )
        return out

    def start(self, phase):
        for copy in self.copies(phase):
            copy.start()

    def finish(self, phase, put=None):
        for copy in self.copies(phase):
            copy.wait()
        got, own = self.got[phase], self.hold[phase]
        size = got.shape[1]
        base = self.net.at[phase] * size

        def add(i, _):
            total = own[base + i].astype(F32)
            for d in range(got.shape[0]):
                total = total + got[d, i].astype(F32)
            if put is None:
                self.hold[phase + 1][i] = total.astype(BF)
            else:
                put(total)
            return 0

        lax.fori_loop(0, size, add, 0)


class Vector:
    def __init__(self, net, bufs, send, recv):
        self.net, self.bufs, self.send, self.recv = net, bufs, send, recv

    def copies(self, phase):
        net, out = self.net, []
        peers = [({"feat": 1 - net.f}, net.slots() - 1)]
        if phase < 3:
            peers = [({"seq": net.peer(phase, d)[1]}, net.slot(phase, d)) for d in range(1, net.sizes[phase])]
        for device, k in peers:
            out.append(
                pltpu.make_async_remote_copy(
                    src_ref=self.bufs.at[phase],
                    dst_ref=self.bufs.at[4 + k],
                    send_sem=self.send.at[k],
                    recv_sem=self.recv.at[k],
                    device_id=device,
                    device_id_type=MESH,
                )
            )
        return out

    def start(self, phase):
        for copy in self.copies(phase):
            copy.start()

    def finish(self, phase):
        for copy in self.copies(phase):
            copy.wait()
        first, count = (self.net.slots() - 1, 1) if phase == 3 else (self.net.slot(phase, 1), self.net.sizes[phase] - 1)
        total = self.bufs[phase]
        for k in range(count):
            total = total + self.bufs[4 + first + k]
        if phase < 3:
            self.bufs[phase + 1] = total
        return total


def call(body, outs, ins, specs=None, out_specs=None, scratch=(), name=None, net=None):
    return pl.pallas_call(
        body,
        out_shape=[jax.ShapeDtypeStruct(s, d) for s, d in outs],
        in_specs=specs or [VMEM] * len(ins),
        out_specs=out_specs or [VMEM] * len(outs),
        scratch_shapes=list(scratch),
        compiler_params=pltpu.CompilerParams(
            vmem_limit_bytes=64000 * 1024, collective_id=net, has_side_effects=net is not None
        ),
        name=name,
    )(*ins)


def qkv_tiles(first, last, x_ref, p_ref, w_ref, h_ref, qkv_ref):
    width = x_ref.shape[1]
    f = lax.axis_index("feat")
    gain = p_ref[GAIN1 : GAIN1 + 1, :]
    shift = p_ref[BIAS1 : BIAS1 + 1, :]
    bias = jnp.concatenate([p_ref[BQKV + i : BQKV + i + 1, ds(f, width // 2)] for i in range(3)], axis=1)

    def step(i, _):
        rows = ds(i, TILE)
        normed, _inv = norm(x_ref[rows, :].astype(F32))
        h = (normed * gain + shift).astype(BF)
        h_ref[rows, :] = h
        qkv_ref[rows, :] = (nn(h, w_ref[...]) + bias).astype(BF)
        return 0

    lax.fori_loop(first, last, step, 0)


def matches(list_ref, count_ref, h):
    at = lax.axis_index("feat") * (HEADS // 2) + h
    lists, count = list_ref[0, at], count_ref[0, pl.ds(at, 1), :]
    block = lax.broadcasted_iota(jnp.int32, (NB, NB), 0)
    found = jnp.zeros((NB, NB), F32)
    for j in range(lists.shape[0]):
        found = jnp.where((lists[j : j + 1] == block) & (count > j), 1.0, found)
    return found.astype(BF)


def fill_spread(e_ref):
    shift = lax.axis_index("feat") * (NB // 2)
    block = lax.broadcasted_iota(jnp.int32, e_ref.shape, 0)
    token = lax.broadcasted_iota(jnp.int32, e_ref.shape, 1)
    start = lax.rem(block + shift, NB) * BLOCK
    e_ref[...] = jnp.where((token >= start) & (token < start + BLOCK), 1.0, 0.0).astype(BF)


def local_marks(mk_ref, i, tile):
    assert tile * 2 == SEQLEN
    return mk_ref[ds(lax.rem(i + lax.axis_index("feat"), 2), tile // BLOCK), :]


def front_body(
    x_own_ref, w_all_ref, fs_ref, list_ref, count_ref, g1, b1, bo, g2, b2, bd, bqkv, bup,
    p_ref, x_out, h_out, qkv_out, table_ref, att_ref, den_ref, kept_ref,
    x_ref, h_ref, qkv_ref, w_ref, s_send, s_got, e_ref, mk_ref, pq_ref, pk_ref, keep_ref, acc_ref,
    send, recv, local, keep_sems, store,
):
    rows, width = x_own_ref.shape
    own = width // 2
    f = lax.axis_index("feat")
    other = {"feat": 1 - f}

    def copy(k, src, dst):
        return pltpu.make_async_remote_copy(
            src_ref=src, dst_ref=dst, send_sem=send.at[k], recv_sem=recv.at[k], device_id=other, device_id_type=MESH
        )

    loads = [
        pltpu.make_async_copy(w_all_ref.at[:, ds(2 * i + f, own)], w_ref.at[:, pl.ds(i * own, own)], local.at[i])
        for i in range(3)
    ]
    for c in loads:
        c.start()
    barrier = pltpu.get_barrier_semaphore()
    pl.semaphore_signal(barrier, inc=1, device_id=other, device_id_type=MESH)
    pl.semaphore_wait(barrier, 1)
    x_copy = copy(0, x_own_ref, x_ref.at[pl.ds(rows, rows)])
    x_copy.start()
    heads, dim, feats = s_send.shape
    line = 0
    for vector in (g1, b1, bo, g2, b2, bd, bqkv, bup):
        for i in range(vector.shape[0] // width):
            p_ref[line : line + 1, :] = vector[i * width : (i + 1) * width].astype(F32).reshape(1, width)
            line += 1

    def sign(i):
        return (2.0 * fs_ref[i].astype(F32) - 1.0).astype(BF)

    for i in range(heads):
        s_send[i] = sign((1 - f) * heads + i)
    s_copy = copy(1, s_send, s_got)
    s_copy.start()
    x_ref[0:rows, :] = x_own_ref[...]
    table_ref[...] = jnp.zeros_like(table_ref)
    for i in range(heads):
        e = i % 2
        table_ref[i // 2, e * dim : (e + 1) * dim, 2 * e * feats : (2 * e + 1) * feats] = sign(f * heads + i)
    fill_spread(e_ref)
    for c in loads:
        c.wait()
    tiles = rows // TILE
    qkv_tiles(0, tiles, x_ref, p_ref, w_ref, h_ref, qkv_ref)
    s_copy.wait()
    for i in range(heads):
        e = i % 2
        table_ref[i // 2, e * dim : (e + 1) * dim, (2 * e + 1) * feats : (2 * e + 2) * feats] = s_got[i]
    x_copy.wait()
    qkv_tiles(tiles, 2 * tiles, x_ref, p_ref, w_ref, h_ref, qkv_ref)
    pairs = ((x_ref, x_out), (h_ref, h_out), (qkv_ref, qkv_out))
    stores = [pltpu.make_async_copy(src, dst, store.at[i]) for i, (src, dst) in enumerate(pairs)]
    for c in stores:
        c.start()
    att_heads(
        qkv_ref, table_ref, list_ref, count_ref, e_ref, mk_ref, att_ref, den_ref, kept_ref, pq_ref, pk_ref, keep_ref,
        acc_ref, keep_sems,
    )
    for c in stores:
        c.wait()


def head_parts(qkv_ref, h):
    own = qkv_ref.shape[1] // 3
    p, e = h // 2, h % 2
    lane = lax.broadcasted_iota(jnp.int32, (1, 128), 1)
    mine = (lane // HEAD_DIM) == e

    def cols(part):
        return pl.ds(pl.multiple_of(part * own + p * 128, 128), 128)

    return p, e, lane, mine, cols


def lift_all(qkv_ref, s_ref, h, pq_ref, pk_ref):
    p, e, lane, mine, cols = head_parts(qkv_ref, h)
    feats = pq_ref.shape[1]
    signs = s_ref[p, :, ds(e, feats)]

    def step(i, _):
        rows = ds(i, WTILE)
        for part, out in ((0, pq_ref), (1, pk_ref)):
            t = qkv_ref[rows, cols(part)]
            w = jnp.where(mine, t.astype(F32), 0.0)
            sq = jnp.sum(w * w, axis=-1, keepdims=True) * (LOG2E * 0.5 * HEAD_DIM ** (-0.5)) + 0.5 * math.log2(feats)
            out[rows, :] = jnp.exp2(nn(t, signs) * (LOG2E * HEAD_DIM ** (-0.25)) - sq).astype(BF)
        return 0

    lax.fori_loop(0, qkv_ref.shape[0] // WTILE, step, 0)


def att_heads(
    qkv_ref, s_ref, list_ref, count_ref, e_ref, mk_ref, att_ref, den_ref, kept_ref, pq_ref, pk_ref, p_ref, acc_ref, sems
):
    heads = qkv_ref.shape[1] // (3 * HEAD_DIM)

    def keep(h):
        slot = lax.rem(h, 2)
        return pltpu.make_async_copy(p_ref.at[slot], kept_ref.at[h], sems.at[slot])

    def head(h, _):
        p, e, lane, mine, cols = head_parts(qkv_ref, h)
        slot = lax.rem(h, 2)
        mk_ref[...] = nn(matches(list_ref, count_ref, h), e_ref[...])
        lift_all(qkv_ref, s_ref, h, pq_ref, pk_ref)
        zero = jnp.zeros((), BF)

        @pl.when(h >= 2)
        def _():
            keep(h - 2).wait()

        acc_ref[...] = jnp.zeros_like(acc_ref)

        def step(i, _):
            rows = ds(i, ATILE)
            k = jnp.where(mine, qkv_ref[rows, cols(1)] * BF(HEAD_DIM ** (-0.5)), zero)
            v_one = jnp.where(mine, qkv_ref[rows, cols(2)], jnp.ones((), BF))
            ex = jnp.exp(nt(k, qkv_ref[:, cols(0)]))
            low = nt(pk_ref[rows, :], pq_ref[...])
            marks = local_marks(mk_ref, i, ATILE)
            probs = jnp.concatenate(
                [
                    jnp.where(
                        marks[j : j + 1, :] > 0.5,
                        ex[j * BLOCK : (j + 1) * BLOCK],
                        low[j * BLOCK : (j + 1) * BLOCK],
                    )
                    for j in range(ATILE // BLOCK)
                ],
                axis=0,
            ).astype(BF)
            p_ref[slot, rows, :] = probs
            acc_ref[...] += tn(probs, v_one)
            return 0

        lax.fori_loop(0, qkv_ref.shape[0] // ATILE, step, 0)
        keep(h).start()

        def last(i, _):
            rows = ds(i, TILE)
            both = acc_ref[rows, :]
            den = pltpu.roll(both, HEAD_DIM, 1)
            out_cols = ds(p, 128)
            att = (both / den).astype(BF)
            att_ref[rows, out_cols] = jnp.where(mine, att, att_ref[rows, out_cols])
            den_ref[rows, out_cols] = jnp.where(mine, den, den_ref[rows, out_cols])
            return 0

        lax.fori_loop(0, qkv_ref.shape[0] // TILE, last, 0)
        return 0

    lax.fori_loop(0, heads, head, 0)
    keep(heads - 2).wait()
    keep(heads - 1).wait()


def mix_tiles(x_ref, mine_ref, other_ref, w_ref, b_ref, g_ref, s_ref, mixed_ref, h_ref):
    f = lax.axis_index("feat")
    half = mine_ref.shape[1]

    def step(i, _):
        rows = ds(i, TILE)
        mixed = (
            x_ref[rows, :].astype(F32)
            + nn(mine_ref[rows, :], w_ref[ds(f, half), :])
            + nn(other_ref[rows, :], w_ref[ds(1 - f, half), :])
            + b_ref[...].astype(F32)
        )
        mixed_ref[rows, :] = mixed
        normed, _inv = norm(mixed)
        h_ref[rows, :] = (normed * g_ref[...].astype(F32) + s_ref[...].astype(F32)).astype(BF)
        return 0

    lax.fori_loop(0, x_ref.shape[0] // TILE, step, 0)


def ff_forward(h_ref, up_ref, down_ref, bias, act_ref, slope_ref, hid_ref, send):
    tiles = h_ref.shape[0] // TILE

    def step(i, _):
        tile = lax.rem(i + tiles // 2, tiles)
        rows = ds(tile, TILE)
        v = nn(h_ref[rows, :], up_ref[...]) + bias
        vv = v * v
        th = jnp.tanh(GELU_A * v * (1.0 + GELU_B * vv))
        half = 0.5 + 0.5 * th
        act = (v * half).astype(BF)
        slope_ref[rows, :] = half + (0.5 * GELU_A) * v * (1.0 - th * th) * (1.0 + (3.0 * GELU_B) * vv)
        act_ref[rows, :] = act
        hid_ref[rows, :] = nn(act, down_ref[...]).astype(BF)
        send(i, tile)
        return 0

    lax.fori_loop(0, tiles, step, 0)


def ff_backward(og_ref, up_ref, down_ref, slope_ref, gp_ref, gh_ref, db_ref, send):
    tiles = og_ref.shape[0] // TILE
    db_ref[...] = jnp.zeros_like(db_ref)

    def step(i, _):
        tile = lax.rem(i + tiles // 2, tiles)
        rows = ds(tile, TILE)
        gp = (nt(og_ref[rows, :], down_ref[...]) * slope_ref[rows, :]).astype(BF)
        gp_ref[rows, :] = gp
        db_ref[...] += jnp.sum(gp.astype(F32), axis=0, keepdims=True)
        gh_ref[rows, :] = nt(gp, up_ref[...]).astype(BF)
        send(i, tile)
        return 0

    lax.fori_loop(0, tiles, step, 0)


def put_chunks(out_ref, first, value, net):
    rows = out_ref.shape[1]
    for i in range(value.shape[0] // rows):
        out_ref[net.place(first + i)] = value[i * rows : (i + 1) * rows].astype(BF)


def ff_weight(net, lhs_ref, rhs_ref, outs):
    wide = lhs_ref.shape[1] // 2
    per = wide // outs[0].shape[1]

    def step(i, _):
        value = tn(lhs_ref[:, ds(i, wide)], rhs_ref[...])
        for j, out in enumerate(outs):
            put_chunks(out, i * per, value[:, j * out.shape[2] : (j + 1) * out.shape[2]], net)
        return 0

    lax.fori_loop(0, 2, step, 0)


def out_back(
    n, gh_ref, gho_ref, mixed_ref, og_ref, hid_ref, hido_ref, bd_ref, g_ref, w_ref, mine_ref, other_ref,
    gm_ref, gatt_ref, dw_ref, y_ref, vec_ref, gb_ref,
):
    f = lax.axis_index("feat")
    half = mine_ref.shape[1]
    tiles = mixed_ref.shape[0] // TILE
    own = tiles // 2
    gain = g_ref[...].astype(F32)
    vec_ref[...] = jnp.zeros_like(vec_ref)

    def step(i, _):
        rows = ds(i, TILE)
        mixed = mixed_ref[rows, :]
        og = og_ref[rows, :].astype(F32)
        normed, inv = norm(mixed)
        g = gh_ref[rows, :].astype(F32) + gho_ref[rows, :].astype(F32)
        gm = og + norm_back(g, normed, inv, gain)
        gb = gm.astype(BF)
        gb_ref[rows, :] = gb
        gatt_ref[rows, :] = nt(gb, w_ref[ds(f, half), :])

        @pl.when(i < own)
        def _():
            gm_ref[rows, :] = gm
            y_ref[rows, :] = (
                mixed + hid_ref[rows, :].astype(F32) + hido_ref[rows, :].astype(F32) + bd_ref[...].astype(F32)
            ).astype(BF)
            for j, term in enumerate((g * normed, g, gb.astype(F32), og)):
                vec_ref[j + 2 : j + 3, :] += jnp.sum(term, axis=0, keepdims=True)

        return 0

    lax.fori_loop(0, tiles, step, 0)
    gb_own = gb_ref[:, ds(f, half)]
    net = Net(n)
    per = half // dw_ref.shape[1]
    put_chunks(dw_ref, f * per, tn(mine_ref[...], gb_own), net)
    put_chunks(dw_ref, (1 - f) * per, tn(other_ref[...], gb_own), net)


def mid_body(
    n, x_ref, att_ref, wout_ref, p_ref, og_own_ref, up_all, down_all,
    gm_ref, gatt_ref, dout_ref, y_ref, vec_ref, dup_ref, ddown_ref, dbup_ref,
    far, og, mixed, h, act, gp, hid, gh, hid_got, gh_got, gb, ddown, ddown_got, slope, up_ref, down_ref, send, recv, down_send, down_recv, local,
):
    net = Net(n)
    down = Scatter(net, ddown, [ddown_got, ddown_ref, None, None, None], down_send, down_recv)
    bout_ref, g_ref, s_ref, bdown_ref = [p_ref.at[i : i + 1] for i in (BOUT, GAIN2, BIAS2, BDOWN)]
    bup = jnp.concatenate([p_ref[i : i + 1, :] for i in range(BUP, p_ref.shape[0])], axis=1)
    rows = og_own_ref.shape[0]
    tiles = h.shape[0] // TILE
    other = {"feat": 1 - lax.axis_index("feat")}

    def copy(k, src, dst):
        return pltpu.make_async_remote_copy(
            src_ref=src, dst_ref=dst, send_sem=send.at[k], recv_sem=recv.at[k], device_id=other, device_id_type=MESH
        )

    loads = [pltpu.make_async_copy(a, b, local.at[i]) for i, (a, b) in enumerate(((up_all, up_ref), (down_all, down_ref)))]
    for c in loads:
        c.start()
    net.barrier()
    low, high = pl.ds(0, rows), pl.ds(rows, rows)
    atts = [copy(0, att_ref.at[low], far.at[high]), copy(1, att_ref.at[high], far.at[low])]
    og_copy = copy(2, og_own_ref, og.at[high])
    for c in atts:
        c.start()
    og_copy.start()
    og[low, :] = og_own_ref[...]
    for c in atts:
        c.wait()
    mix_tiles(x_ref, att_ref, far, wout_ref, bout_ref, g_ref, s_ref, mixed, h)

    def gh_copy(i, tile):
        return copy(3 + i, gh.at[ds(tile, TILE)], gh_got.at[ds(i, TILE)])

    def hid_copy(i, tile):
        return copy(3 + tiles + i, hid.at[ds(tile, TILE)], hid_got.at[ds(i, TILE)])

    def send_gh(i, tile):
        gh_copy(i, tile).start()

    def send_hid(i, tile):
        @pl.when(i < tiles // 2)
        def _():
            hid_copy(i, tile).start()

    for c in loads:
        c.wait()
    ff_forward(h, up_ref, down_ref, bup, act, slope, hid, send_hid)
    og_copy.wait()
    ff_weight(net, og, act, [ddown])
    down.start(0)
    ff_backward(og, up_ref, down_ref, slope, gp, gh, dbup_ref, send_gh)
    ff_weight(net, h, gp, [dup_ref.at[0], dup_ref.at[1]])
    for i in range(tiles):
        gh_copy(i, (i + tiles // 2) % tiles).wait()
    for i in range(tiles // 2):
        hid_copy(i, i + tiles // 2).wait()
    out_back(
        n, gh, gh_got, mixed, og, hid, hid_got, bdown_ref, g_ref, wout_ref, att_ref, far,
        gm_ref, gatt_ref, dout_ref, y_ref, vec_ref, gb,
    )
    down.finish(0)


def heads_back(
    qkv_ref, s_ref, list_ref, count_ref, kept_ref, p_ref, sems, e_ref, mk_ref, att_ref, den_ref, gatt_ref, gqkv_ref, pq_ref, pk_ref, gn_ref, gq_ref, gpq_ref, after
):
    rows_all = qkv_ref.shape[0]
    scale = HEAD_DIM ** (-0.5)

    heads = qkv_ref.shape[1] // (3 * HEAD_DIM)

    def fetch(h):
        slot = lax.rem(h, 2)
        return pltpu.make_async_copy(kept_ref.at[h], p_ref.at[slot], sems.at[slot])

    fetch(0).start()

    def head(h, _):
        slot = lax.rem(h, 2)

        @pl.when(h + 1 < heads)
        def _():
            fetch(h + 1).start()

        p, e, lane, mine, cols = head_parts(qkv_ref, h)
        feats = pq_ref.shape[1]
        zero = jnp.zeros((), BF)
        mk_ref[...] = nn(matches(list_ref, count_ref, h), e_ref[...])
        lift_all(qkv_ref, s_ref, h, pq_ref, pk_ref)
        first_other = (1 - e) * HEAD_DIM

        def prep(i, _):
            rows = ds(i, WTILE)
            inv = 1.0 / den_ref[rows, ds(p, 128)]
            ga = jnp.where(mine, gatt_ref[rows, ds(p, 128)] * inv, 0.0)
            gd = -jnp.sum(ga * att_ref[rows, ds(p, 128)].astype(F32), axis=-1, keepdims=True)
            gn_ref[rows, :] = jnp.where(lane == first_other, gd, ga).astype(BF)
            return 0

        lax.fori_loop(0, rows_all // WTILE, prep, 0)
        gq_ref[...] = jnp.zeros_like(gq_ref)
        gpq_ref[...] = jnp.zeros_like(gpq_ref)
        signs = s_ref[p, :, ds(e, feats)]

        def lift_back(t, raw, g_phi):
            gl = g_phi * raw.astype(F32)
            gt = nt(gl.astype(BF), signs) * HEAD_DIM ** (-0.25)
            return gt - jnp.sum(gl, axis=-1, keepdims=True) * (scale * t.astype(F32))

        def put(part, rows, value):
            gqkv_ref[rows, cols(part)] = jnp.where(mine, value.astype(BF), gqkv_ref[rows, cols(part)])

        fetch(h).wait()

        def step(i, _):
            rows = ds(i, BTILE)
            k = jnp.where(mine, qkv_ref[rows, cols(1)] * BF(scale), zero)
            v_one = jnp.where(mine, qkv_ref[rows, cols(2)], jnp.ones((), BF))
            q_all = qkv_ref[:, cols(0)]
            pk = pk_ref[rows, :]
            probs = p_ref[slot, rows, :]
            da = nt(v_one, gn_ref[...])
            marks = local_marks(mk_ref, i, BTILE)
            dl, gs = [], []
            for j in range(BTILE // BLOCK):
                part = slice(j * BLOCK, (j + 1) * BLOCK)
                on = marks[j : j + 1, :] > 0.5
                daj = da[part]
                dl.append(jnp.where(on, 0.0, daj))
                gs.append(jnp.where(on, daj * probs[part].astype(F32), 0.0))
            dl = jnp.concatenate(dl, axis=0).astype(BF)
            gs = jnp.concatenate(gs, axis=0).astype(BF)
            put(2, rows, nn(probs, gn_ref[...]))
            g_phi_k = nn(dl, pq_ref[...])
            gk = nn(gs, q_all) * scale + lift_back(qkv_ref[rows, cols(1)], pk, g_phi_k)
            put(1, rows, gk)
            gpq_ref[...] += tn(dl, pk)
            gq_ref[...] += tn(gs, k)
            return 0

        lax.fori_loop(0, rows_all // BTILE, step, 0)

        def last(i, _):
            rows = ds(i, WTILE)
            gq = gq_ref[rows, :] + lift_back(qkv_ref[rows, cols(0)], pq_ref[rows, :], gpq_ref[rows, :])
            put(0, rows, gq)
            return 0

        lax.fori_loop(0, rows_all // WTILE, last, 0)
        for k, then in after.items():
            pl.when(h == k)(then)
        return 0

    lax.fori_loop(0, qkv_ref.shape[1] // (3 * HEAD_DIM), head, 0)


def back_body(
    n, qkv_ref, s_ref, list_ref, count_ref, kept_ref, att_ref, den_ref, gatt_ref, h_all, w_all, x_all, p_ref, gm_all, up_ref, down_ref, out_ref,
    vec_ref, bup_ref, dx_ref, oup_ref, odown_ref, oout_ref, oqkv_ref, orows_ref, obqkv_ref, obup_ref, *scratch,
):
    net = Net(n)
    bufs, tail = (None, down_ref) + scratch[:33], scratch[33:]
    kept_buf, keep_sems, h_ref, w_ref, x_ref, gm_ref, local, e_ref, mk_ref, pq, pk, gn, gq, gpq, gqkv, gw, gh_send, gh_got, sout, rout, sqkv, rqkv, vrows, vbqkv, vbup, send, recv = tail
    f = net.f
    other = {"feat": 1 - f}
    sources = (None, up_ref.at[0], out_ref, gw.at[0], gw.at[1], gw.at[2], up_ref.at[1])
    lanes_of = (0, 1, 2, 3, 4, 5, 10)
    down, up_low, out, *pairs, up_high = [
        Scatter(net, src, bufs[5 * i : 5 * i + 5], send.at[k], recv.at[k])
        for i, (src, k) in enumerate(zip(sources, lanes_of))
    ]
    vectors = [Vector(net, ref, send.at[6 + i], recv.at[6 + i]) for i, ref in enumerate((vrows, vbqkv, vbup))]
    last = net.slots() - 1
    half = sout.shape[1]
    rows = x_ref.shape[0]
    width = x_ref.shape[1]
    own = width // 2
    lanes = orows_ref.shape[1]

    def whole(ref):
        def put(total):
            ref[...] = total

        return put

    def halves(ref):
        def put(total):
            ref[0], ref[1] = total[:half], total[half:]

        return put

    def swap(i, src, dst):
        return pltpu.make_async_remote_copy(
            src_ref=src, dst_ref=dst, send_sem=send.at[i, last], recv_sem=recv.at[i, last],
            device_id=other, device_id_type=MESH,
        )

    def move(part, phase):
        part.finish(phase)
        part.start(phase + 1)

    def weight(p):
        g = jnp.concatenate([gqkv[:, i * own + p * 128 : i * own + (p + 1) * 128] for i in range(3)], axis=1)
        per = own // gw.shape[2]
        for i in range(2):
            put_chunks(gw.at[p], i * per, tn(h_ref[:, i * own : (i + 1) * own], g), net)
        pairs[p].start(0)

    loads = [
        pltpu.make_async_copy(a, b, local.at[i])
        for i, (a, b) in enumerate(((h_all, h_ref), (x_all, x_ref), (gm_all, gm_ref)))
    ] + [
        pltpu.make_async_copy(w_all.at[:, ds(2 * i + f, own)], w_ref.at[:, pl.ds(i * own, own)], local.at[3 + i])
        for i in range(3)
    ]
    for c in loads:
        c.start()
    fill_spread(e_ref)
    net.barrier()
    down.start(1)
    up_low.start(0)
    up_high.start(0)
    out.start(0)

    def after1():
        loads[0].wait()
        weight(0)

    def after2():
        move(down, 1)
        move(up_low, 0)

    def after3():
        move(up_high, 0)
        move(up_low, 1)
        move(out, 0)
        move(pairs[0], 0)
        weight(1)

    def after4():
        move(up_high, 1)
        move(out, 1)
        move(pairs[0], 1)
        move(pairs[1], 0)
        down.finish(2, whole(odown_ref))

    heads_back(
        qkv_ref, s_ref, list_ref, count_ref, kept_ref, kept_buf, keep_sems, e_ref, mk_ref, att_ref, den_ref, gatt_ref, gqkv, pq, pk, gn, gq, gpq,
        {1: after1, 2: after2, 3: after3, 4: after4},
    )
    weight(2)
    for c in loads[1:]:
        c.wait()
    tiles = rows // TILE

    def far(i, total):
        g = gqkv[ds(tiles + i, TILE), :]
        gh_send[ds(i, TILE), :] = nt(g, w_ref[...]).astype(BF)
        return total + jnp.sum(g.astype(F32), axis=0, keepdims=True)

    total = lax.fori_loop(0, tiles, far, jnp.zeros((1, 3 * own), F32))
    gh_swap = swap(9, gh_send, gh_got)
    gh_swap.start()
    move(pairs[1], 1)

    def sums(i, total):
        return total + jnp.sum(gqkv[ds(i, TILE), :].astype(F32), axis=0, keepdims=True)

    total = lax.fori_loop(0, tiles, sums, total)
    vbqkv[0] = jnp.zeros_like(vbqkv[0])
    for i in range(3):
        vbqkv[0, :, ds(2 * i + f, own)] = total[:, i * own : (i + 1) * own]
    vbup[0] = bup_ref[...]
    up_low.finish(2, whole(oup_ref.at[:, 0 : oup_ref.shape[1] // 2]))
    out.finish(2, halves(sout))
    out_swap = swap(2, sout.at[1 - f], rout)
    out_swap.start()
    move(pairs[2], 0)
    up_high.finish(2, whole(oup_ref.at[:, oup_ref.shape[1] // 2 :]))
    gh_swap.wait()
    gain = p_ref[GAIN1 : GAIN1 + 1, :]
    vrows[0] = vec_ref[...]

    def norm1(i, _):
        r = ds(i, TILE)
        normed, inv = norm(x_ref[r, :].astype(F32))
        g = nt(gqkv[r, :], w_ref[...]) + gh_got[r, :].astype(F32)
        dx_ref[r, :] = gm_ref[r, :] + norm_back(g, normed, inv, gain)
        vrows[0, 0:1, :] += jnp.sum(g * normed, axis=0, keepdims=True)
        vrows[0, 1:2, :] += jnp.sum(g, axis=0, keepdims=True)
        return 0

    lax.fori_loop(0, tiles, norm1, 0)
    for v in vectors:
        v.start(0)
    move(pairs[2], 1)
    for p in (0, 1):
        pairs[p].finish(2, halves(sqkv.at[p]))
    for v in vectors:
        v.finish(0)
        v.start(1)
    swaps = [swap(3 + p, sqkv.at[p, 1 - f], rqkv.at[p]) for p in range(3)]
    swaps[0].start()
    swaps[1].start()
    for v in vectors:
        v.finish(1)
        v.start(2)
    pairs[2].finish(2, halves(sqkv.at[2]))
    swaps[2].start()
    vecs, bqkv, bup = [v.finish(2) for v in vectors]
    vectors[0].start(3)
    vectors[1].start(3)
    where = 2 * net.s + f

    def cut(value, per, index, size):
        return pltpu.roll(value, lax.rem(size - index * per, size), 1)[:, :lanes]

    obup_ref[...] = cut(bup, bup.shape[1] // n, net.s, bup.shape[1])
    out_swap.wait()
    oout_ref[:, ds(f, own)] = sout[f]
    oout_ref[:, ds(1 - f, own)] = rout[...]

    def cols(i, p, side):
        return pl.ds(pl.multiple_of(i * width + side * own + p * 128, 128), 128)

    for p in range(3):
        swaps[p].wait()
        for i in range(3):
            part = slice(i * 128, (i + 1) * 128)
            oqkv_ref[:, cols(i, p, f)] = sqkv[p, f, :, part]
            oqkv_ref[:, cols(i, p, 1 - f)] = rqkv[p, :, part]
    vecs = vectors[0].finish(3)
    bqkv = vectors[1].finish(3)
    orows_ref[...] = cut(vecs, width // (2 * n), where, width)
    obqkv_ref[...] = cut(bqkv, bqkv.shape[1] // (2 * n), where, bqkv.shape[1])


def emit_body(y_ref, dx_ref, up_ref, down_ref, out_ref, qkv_ref, rows_ref, bqkv_ref, bup_ref, *outs):
    oy, odx, oup, odown, oout, oqkv, obqkv, obup = outs[:8]
    oy[...] = y_ref[...]
    odx[...], oup[...], oout[...], oqkv[...] = dx_ref[...], up_ref[...], out_ref[...], qkv_ref[...]
    down = down_ref[...]
    odown[...] = down if odown.shape == down.shape else down.T
    obqkv[...] = bqkv_ref[:, : obqkv.shape[1]]
    obup[...] = bup_ref[:, : obup.shape[1]]
    for i, ref in enumerate(outs[8:]):
        ref[...] = rows_ref[i : i + 1, : ref.shape[1]]


def body(
    layer_input, ln1_gain, ln1_bias, w_qkv, b_qkv, w_out, b_out, ln2_gain, ln2_bias,
    w_up, b_up, w_down, b_down, feature_signs, match_blocks, match_count, out_grad,
):
    rows, width = layer_input.shape
    half_width = width // 2
    half_heads = HEADS // 2
    hidden = w_up.shape[1]
    f = lax.axis_index("feat")
    tokens = 2 * rows
    n = lax.axis_size("seq")
    chunk = width // n
    assert lax.axis_size("feat") == 2 and match_blocks.shape[0] == 1 and tokens == SEQLEN

    lists = match_blocks.transpose(0, 1, 3, 2)
    vectors = [ln1_gain, ln1_bias, b_out, ln2_gain, ln2_bias, b_down, b_qkv, b_up]
    lines = sum(a.shape[0] for a in vectors) // width
    feats = 2 * feature_signs.shape[2]
    phi = pltpu.VMEM((tokens, feats), BF)
    masks = [pltpu.VMEM((NB, tokens), BF), pltpu.VMEM((NB, tokens), F32)]
    sign_half = pltpu.VMEM((half_heads, HEAD_DIM, feats // 2), BF)
    two, three = pltpu.SemaphoreType.DMA((2,)), pltpu.SemaphoreType.DMA((3,))
    full, qkv_buf = pltpu.VMEM((tokens, width), BF), pltpu.VMEM((tokens, 3 * half_width), BF)
    w_buf = pltpu.VMEM((width, 3 * half_width), BF)
    params, x, h1, qkv, table, att, den, kept = call(
        front_body,
        [
            ((lines, width), F32),
            ((tokens, width), BF), ((tokens, width), BF), ((tokens, 3 * half_width), BF),
            ((half_heads // 2, 2 * HEAD_DIM, 2 * feats), BF),
            ((tokens, half_width), BF), ((tokens, half_width), F32), ((half_heads, tokens, tokens), BF),
        ],
        [layer_input, w_qkv, feature_signs, lists, match_count] + vectors,
        specs=[VMEM, ANY] + [VMEM] * (3 + len(vectors)),
        scratch=[full, full, qkv_buf, w_buf, sign_half, sign_half] + masks + [
            phi, phi, pltpu.VMEM((2, tokens, tokens), BF), pltpu.VMEM((tokens, 128), F32), two, two,
            three, two, three,
        ],
        out_specs=[VMEM, ANY, ANY, ANY, VMEM, VMEM, VMEM, ANY],
        name="front", net=3,
    )
    big, wide = pltpu.VMEM((tokens, width), BF), pltpu.VMEM((tokens, hidden), BF)
    down_bufs = scatter_bufs(n, chunk, hidden)
    down_sems = pltpu.SemaphoreType.DMA((split(n)[0] - 1,))
    pair_sems = pltpu.SemaphoreType.DMA((3 + tokens // TILE + rows // TILE,))
    gm, gatt, d_out, y, vec2, d_up, d_down, d_bup = call(
        functools.partial(mid_body, n),
        [
            ((rows, width), F32), ((tokens, half_width), F32), ((n, chunk, half_width), BF), ((rows, width), BF),
            ((8, width), F32), ((2, n, chunk, hidden // 2), BF), (down_bufs[1].shape, BF), ((1, hidden), F32),
        ],
        [
            x, att, w_out, params, out_grad, w_up, w_down,
        ],
        specs=[VMEM] * 5 + [ANY] * 2,
        scratch=[
            pltpu.VMEM((tokens, half_width), BF), big, pltpu.VMEM((tokens, width), F32), big, wide, wide, big, big,
            pltpu.VMEM((rows, width), BF), big, big, pltpu.VMEM((n, chunk, hidden), BF), down_bufs[0],
            pltpu.VMEM((tokens, hidden), F32), pltpu.VMEM((width, hidden), BF), pltpu.VMEM((hidden, width), BF),
            pair_sems, pair_sems, down_sems, down_sems, two,
        ],
        name="mid", net=2,
    )
    slots = sum(split(n)) + split(n)[0] - 3 + 1
    bufs = down_bufs[2:]
    for cols in (hidden // 2, half_width, half_width, half_width, half_width, hidden // 2):
        bufs += scatter_bufs(n, chunk, cols)
    half_chunk = chunk // 2
    sems = pltpu.SemaphoreType.DMA((11, slots))
    sums = call(
        functools.partial(back_body, n),
        [
            ((rows, width), F32), ((chunk, hidden), F32), ((chunk, hidden), F32), ((half_chunk, width), F32),
            ((half_chunk, 3 * width), F32), ((8, 128), F32), ((1, 128), F32), ((1, 128), F32),
        ],
        [
            qkv, table, lists, match_count, kept, att, den, gatt, h1, w_qkv, layer_input, params, gm, d_up, d_down, d_out, vec2, d_bup,
        ],
        specs=[VMEM] * 4 + [ANY] + [VMEM] * 3 + [ANY] * 3 + [VMEM, ANY] + [VMEM] * 5,
        scratch=bufs + [
            pltpu.VMEM((2, tokens, tokens), BF), two, full, w_buf, pltpu.VMEM((rows, width), BF),
            pltpu.VMEM((rows, width), F32), pltpu.SemaphoreType.DMA((6,)),
        ] + masks + [
            phi, phi, pltpu.VMEM((tokens, 128), BF), pltpu.VMEM((tokens, 128), F32), pltpu.VMEM((tokens, feats), F32),
            pltpu.VMEM((tokens, 3 * half_width), BF), pltpu.VMEM((3, n, chunk, half_width), BF),
            pltpu.VMEM((rows, width), BF), pltpu.VMEM((rows, width), BF),
            pltpu.VMEM((2, half_chunk, half_width), F32), pltpu.VMEM((half_chunk, half_width), F32),
            pltpu.VMEM((3, 2, half_chunk, half_width), F32), pltpu.VMEM((3, half_chunk, half_width), F32),
            pltpu.VMEM((4 + slots, 8, width), F32), pltpu.VMEM((4 + slots, 1, 3 * width), F32),
            pltpu.VMEM((4 + slots, 1, hidden), F32), sems, sems,
        ],
        name="back", net=1,
    )
    own = width // (2 * n)
    turn = False
    y, dx, up, down, out, full, d_b, d_bup, *vec = call(
        emit_body,
        [
            ((rows, width), BF),
            ((rows, width), F32), ((chunk, hidden), F32), ((hidden, chunk) if turn else (chunk, hidden), F32),
            ((half_chunk, width), F32), ((half_chunk, 3 * width), F32), ((1, 3 * own), F32), ((1, hidden // n), F32),
        ] + [((1, own), F32)] * 6,
        [y] + list(sums), name="emit",
    )
    vec = [v.reshape(-1) for v in vec]
    return (
        y, dx, vec[0], vec[1], full, d_b.reshape(-1), out, vec[4], vec[2], vec[3], up, d_bup.reshape(-1),
        down if turn else down.T, vec[5],
    )


def solution(mesh):
    both = ("seq", "feat")
    return jax.shard_map(
        body,
        mesh=mesh,
        in_specs=(
            P(both, None), P(), P(), P(), P(), P(), P(), P(), P(), P(None, "feat"), P("feat"), P("feat", None), P(),
            P(None, None, "feat"), P("seq", None, None, None), P("seq", None, None), P(both, None),
        ),
        out_specs=(
            P(both, None), P(both, None), P(both), P(both), P(both, None), P(both), P(both, None), P(both), P(both),
            P(both), P("seq", "feat"), P(("feat", "seq")), P("feat", "seq"), P(both),
        ),
        check_vma=False,
    )
```

```python
import functools
import math

import jax
import jax.numpy as jnp
from jax import lax
from jax.experimental import pallas as pl
from jax.experimental.pallas import tpu as pltpu
from jax.sharding import PartitionSpec as P

HEADS = 12
HEAD_DIM = 64
BLOCK = 64
NB = 16
SEQLEN = NB * BLOCK
BF = jnp.bfloat16
F32 = jnp.float32
EPS = 1e-05
TILE = 256
ATILE = 512
BTILE = 512
WTILE = 512
GELU_A = math.sqrt(2.0 / math.pi)
GELU_B = 0.044715
LOG2E = math.log2(math.e)
GAIN1, BIAS1, BOUT, GAIN2, BIAS2, BDOWN, BQKV, BUP = 0, 1, 2, 3, 4, 5, 6, 9
MESH = pl.DeviceIdType.MESH
VMEM = pl.BlockSpec(memory_space=pltpu.VMEM)
ANY = pl.BlockSpec(memory_space=pl.ANY)


def nn(a, b):
    return lax.dot_general(a, b, (((1,), (0,)), ((), ())), preferred_element_type=F32)


def nt(a, b):
    return lax.dot_general(a, b, (((1,), (1,)), ((), ())), preferred_element_type=F32)


def tn(a, b):
    return lax.dot_general(a, b, (((0,), (0,)), ((), ())), preferred_element_type=F32)


def ds(i, n):
    return pl.ds(i * n if isinstance(i, int) else pl.multiple_of(i * n, n), n)


def norm(x):
    c = x - jnp.mean(x, axis=-1, keepdims=True)
    inv = lax.rsqrt(jnp.mean(c * c, axis=-1, keepdims=True) + EPS)
    return c * inv, inv


def norm_back(g, normed, inv, gain):
    a = g * gain
    return inv * (
        a
        - jnp.mean(a, axis=-1, keepdims=True)
        - normed * jnp.mean(a * normed, axis=-1, keepdims=True)
    )


def split(n):
    p = 1
    while 2 * (2 * p) ** 3 <= n:
        p *= 2
    assert n % (p * p) == 0
    return p, n // (p * p)


class Net:
    def __init__(self, n):
        p, self.nz = split(n)
        self.p = p
        self.s, self.f = lax.axis_index("seq"), lax.axis_index("feat")
        x, y = lax.rem(self.s, p), lax.rem(self.s // p, p)
        f = self.f
        self.sizes = (p, p, self.nz)
        self.at = (x + f * (y - x), y + f * (x - y), self.s // (p * p))
        self.strides = (1 + f * (p - 1), p + f * (1 - p), p * p)

    def place(self, dest):
        p = self.p
        x, y, z = lax.rem(dest, p), lax.rem(dest // p, p), dest // (p * p)
        f = self.f
        return ((x + f * (y - x)) * p + y + f * (x - y)) * self.nz + z

    def peer(self, phase, d):
        j = lax.rem(self.at[phase] + d, self.sizes[phase])
        return j, self.s + (j - self.at[phase]) * self.strides[phase]

    def barrier(self):
        sem = pltpu.get_barrier_semaphore()
        count = 1
        for phase in range(3):
            for d in range(1, self.sizes[phase]):
                pl.semaphore_signal(sem, inc=1, device_id={"seq": self.peer(phase, d)[1]}, device_id_type=MESH)
                count += 1
        pl.semaphore_signal(sem, inc=1, device_id={"feat": 1 - self.f}, device_id_type=MESH)
        pl.semaphore_wait(sem, count)

    def slot(self, phase, d):
        return sum(size - 1 for size in self.sizes[:phase]) + d - 1

    def slots(self):
        return self.slot(3, 1) + 1


def scatter_bufs(n, rows, cols):
    p, nz = split(n)
    return [
        pltpu.VMEM((p - 1, p * nz, rows, cols), BF),
        pltpu.VMEM((p * nz, rows, cols), BF),
        pltpu.VMEM((p - 1, nz, rows, cols), BF),
        pltpu.VMEM((nz, rows, cols), BF),
        pltpu.VMEM((nz - 1, 1, rows, cols), BF),
    ]


class Scatter:
    def __init__(self, net, src, bufs, send, recv):
        self.net, self.send, self.recv = net, send, recv
        self.hold = (src, bufs[1], bufs[3])
        self.got = (bufs[0], bufs[2], bufs[4])

    def block(self, phase, j):
        size = self.got[phase].shape[1]
        return pl.ds(j * size, size)

    def copies(self, phase):
        net, out = self.net, []
        for d in range(1, net.sizes[phase]):
            j, device = net.peer(phase, d)
            k = net.slot(phase, d)
            out.append(
                pltpu.make_async_remote_copy(
                    src_ref=self.hold[phase].at[self.block(phase, j)],
                    dst_ref=self.got[phase].at[d - 1],
                    send_sem=self.send.at[k],
                    recv_sem=self.recv.at[k],
                    device_id={"seq": device},
                    device_id_type=MESH,
                )
            )
        return out

    def start(self, phase):
        for copy in self.copies(phase):
            copy.start()

    def finish(self, phase, put=None):
        for copy in self.copies(phase):
            copy.wait()
        got, own = self.got[phase], self.hold[phase]
        size = got.shape[1]
        base = self.net.at[phase] * size

        def add(i, _):
            total = own[base + i].astype(F32)
            for d in range(got.shape[0]):
                total = total + got[d, i].astype(F32)
            if put is None:
                self.hold[phase + 1][i] = total.astype(BF)
            else:
                put(total)
            return 0

        lax.fori_loop(0, size, add, 0)


class Vector:
    def __init__(self, net, bufs, send, recv):
        self.net, self.bufs, self.send, self.recv = net, bufs, send, recv

    def copies(self, phase):
        net, out = self.net, []
        peers = [({"feat": 1 - net.f}, net.slots() - 1)]
        if phase < 3:
            peers = [({"seq": net.peer(phase, d)[1]}, net.slot(phase, d)) for d in range(1, net.sizes[phase])]
        for device, k in peers:
            out.append(
                pltpu.make_async_remote_copy(
                    src_ref=self.bufs.at[phase],
                    dst_ref=self.bufs.at[4 + k],
                    send_sem=self.send.at[k],
                    recv_sem=self.recv.at[k],
                    device_id=device,
                    device_id_type=MESH,
                )
            )
        return out

    def start(self, phase):
        for copy in self.copies(phase):
            copy.start()

    def finish(self, phase):
        for copy in self.copies(phase):
            copy.wait()
        first, count = (self.net.slots() - 1, 1) if phase == 3 else (self.net.slot(phase, 1), self.net.sizes[phase] - 1)
        total = self.bufs[phase]
        for k in range(count):
            total = total + self.bufs[4 + first + k]
        if phase < 3:
            self.bufs[phase + 1] = total
        return total


def call(body, outs, ins, specs=None, out_specs=None, scratch=(), name=None, net=None):
    return pl.pallas_call(
        body,
        out_shape=[jax.ShapeDtypeStruct(s, d) for s, d in outs],
        in_specs=specs or [VMEM] * len(ins),
        out_specs=out_specs or [VMEM] * len(outs),
        scratch_shapes=list(scratch),
        compiler_params=pltpu.CompilerParams(
            vmem_limit_bytes=64000 * 1024, collective_id=net, has_side_effects=net is not None
        ),
        name=name,
    )(*ins)


def qkv_tiles(first, last, x_ref, p_ref, w_ref, h_ref, qkv_ref):
    width = x_ref.shape[1]
    f = lax.axis_index("feat")
    gain = p_ref[GAIN1 : GAIN1 + 1, :]
    shift = p_ref[BIAS1 : BIAS1 + 1, :]
    bias = jnp.concatenate([p_ref[BQKV + i : BQKV + i + 1, ds(f, width // 2)] for i in range(3)], axis=1)

    def step(i, _):
        rows = ds(i, TILE)
        normed, _inv = norm(x_ref[rows, :].astype(F32))
        h = (normed * gain + shift).astype(BF)
        h_ref[rows, :] = h
        qkv_ref[rows, :] = (nn(h, w_ref[...]) + bias).astype(BF)
        return 0

    lax.fori_loop(first, last, step, 0)


def matches(list_ref, count_ref, h):
    at = lax.axis_index("feat") * (HEADS // 2) + h
    lists, count = list_ref[0, at], count_ref[0, pl.ds(at, 1), :]
    block = lax.broadcasted_iota(jnp.int32, (NB, NB), 0)
    found = jnp.zeros((NB, NB), F32)
    for j in range(lists.shape[0]):
        found = jnp.where((lists[j : j + 1] == block) & (count > j), 1.0, found)
    return found.astype(BF)


def fill_spread(e_ref):
    shift = lax.axis_index("feat") * (NB // 2)
    block = lax.broadcasted_iota(jnp.int32, e_ref.shape, 0)
    token = lax.broadcasted_iota(jnp.int32, e_ref.shape, 1)
    start = lax.rem(block + shift, NB) * BLOCK
    e_ref[...] = jnp.where((token >= start) & (token < start + BLOCK), 1.0, 0.0).astype(BF)


def local_marks(mk_ref, i, tile):
    assert tile * 2 == SEQLEN
    return mk_ref[ds(lax.rem(i + lax.axis_index("feat"), 2), tile // BLOCK), :]


def front_body(
    x_own_ref, w_all_ref, fs_ref, list_ref, count_ref, g1, b1, bo, g2, b2, bd, bqkv, bup,
    p_ref, x_out, h_out, qkv_out, table_ref, att_ref, den_ref, kept_ref,
    x_ref, h_ref, qkv_ref, w_ref, s_send, s_got, e_ref, mk_ref, pq_ref, pk_ref, keep_ref, acc_ref,
    send, recv, local, keep_sems, store,
):
    rows, width = x_own_ref.shape
    own = width // 2
    f = lax.axis_index("feat")
    other = {"feat": 1 - f}

    def copy(k, src, dst):
        return pltpu.make_async_remote_copy(
            src_ref=src, dst_ref=dst, send_sem=send.at[k], recv_sem=recv.at[k], device_id=other, device_id_type=MESH
        )

    loads = [
        pltpu.make_async_copy(w_all_ref.at[:, ds(2 * i + f, own)], w_ref.at[:, pl.ds(i * own, own)], local.at[i])
        for i in range(3)
    ]
    for c in loads:
        c.start()
    barrier = pltpu.get_barrier_semaphore()
    pl.semaphore_signal(barrier, inc=1, device_id=other, device_id_type=MESH)
    pl.semaphore_wait(barrier, 1)
    x_copy = copy(0, x_own_ref, x_ref.at[pl.ds(rows, rows)])
    x_copy.start()
    heads, dim, feats = s_send.shape
    line = 0
    for vector in (g1, b1, bo, g2, b2, bd, bqkv, bup):
        for i in range(vector.shape[0] // width):
            p_ref[line : line + 1, :] = vector[i * width : (i + 1) * width].astype(F32).reshape(1, width)
            line += 1

    def sign(i):
        return (2.0 * fs_ref[i].astype(F32) - 1.0).astype(BF)

    for i in range(heads):
        s_send[i] = sign((1 - f) * heads + i)
    s_copy = copy(1, s_send, s_got)
    s_copy.start()
    x_ref[0:rows, :] = x_own_ref[...]
    table_ref[...] = jnp.zeros_like(table_ref)
    for i in range(heads):
        e = i % 2
        table_ref[i // 2, e * dim : (e + 1) * dim, 2 * e * feats : (2 * e + 1) * feats] = sign(f * heads + i)
    fill_spread(e_ref)
    for c in loads:
        c.wait()
    tiles = rows // TILE
    qkv_tiles(0, tiles, x_ref, p_ref, w_ref, h_ref, qkv_ref)
    s_copy.wait()
    for i in range(heads):
        e = i % 2
        table_ref[i // 2, e * dim : (e + 1) * dim, (2 * e + 1) * feats : (2 * e + 2) * feats] = s_got[i]
    x_copy.wait()
    qkv_tiles(tiles, 2 * tiles, x_ref, p_ref, w_ref, h_ref, qkv_ref)
    pairs = ((x_ref, x_out), (h_ref, h_out), (qkv_ref, qkv_out))
    stores = [pltpu.make_async_copy(src, dst, store.at[i]) for i, (src, dst) in enumerate(pairs)]
    for c in stores:
        c.start()
    att_heads(
        qkv_ref, table_ref, list_ref, count_ref, e_ref, mk_ref, att_ref, den_ref, kept_ref, pq_ref, pk_ref, keep_ref,
        acc_ref, keep_sems,
    )
    for c in stores:
        c.wait()


def head_parts(qkv_ref, h):
    own = qkv_ref.shape[1] // 3
    p, e = h // 2, h % 2
    lane = lax.broadcasted_iota(jnp.int32, (1, 128), 1)
    mine = (lane // HEAD_DIM) == e

    def cols(part):
        return pl.ds(pl.multiple_of(part * own + p * 128, 128), 128)

    return p, e, lane, mine, cols


def lift_all(qkv_ref, s_ref, h, pq_ref, pk_ref):
    p, e, lane, mine, cols = head_parts(qkv_ref, h)
    feats = pq_ref.shape[1]
    signs = s_ref[p, :, ds(e, feats)]

    def step(i, _):
        rows = ds(i, WTILE)
        for part, out in ((0, pq_ref), (1, pk_ref)):
            t = qkv_ref[rows, cols(part)]
            w = jnp.where(mine, t.astype(F32), 0.0)
            sq = jnp.sum(w * w, axis=-1, keepdims=True) * (LOG2E * 0.5 * HEAD_DIM ** (-0.5)) + 0.5 * math.log2(feats)
            out[rows, :] = jnp.exp2(nn(t, signs) * (LOG2E * HEAD_DIM ** (-0.25)) - sq).astype(BF)
        return 0

    lax.fori_loop(0, qkv_ref.shape[0] // WTILE, step, 0)


def att_heads(
    qkv_ref, s_ref, list_ref, count_ref, e_ref, mk_ref, att_ref, den_ref, kept_ref, pq_ref, pk_ref, p_ref, acc_ref, sems
):
    heads = qkv_ref.shape[1] // (3 * HEAD_DIM)

    def keep(h):
        slot = lax.rem(h, 2)
        return pltpu.make_async_copy(p_ref.at[slot], kept_ref.at[h], sems.at[slot])

    def head(h, _):
        p, e, lane, mine, cols = head_parts(qkv_ref, h)
        slot = lax.rem(h, 2)
        mk_ref[...] = nn(matches(list_ref, count_ref, h), e_ref[...])
        lift_all(qkv_ref, s_ref, h, pq_ref, pk_ref)
        zero = jnp.zeros((), BF)

        @pl.when(h >= 2)
        def _():
            keep(h - 2).wait()

        acc_ref[...] = jnp.zeros_like(acc_ref)

        def step(i, _):
            rows = ds(i, ATILE)
            k = jnp.where(mine, qkv_ref[rows, cols(1)] * BF(HEAD_DIM ** (-0.5)), zero)
            v_one = jnp.where(mine, qkv_ref[rows, cols(2)], jnp.ones((), BF))
            ex = jnp.exp(nt(k, qkv_ref[:, cols(0)]))
            low = nt(pk_ref[rows, :], pq_ref[...])
            marks = local_marks(mk_ref, i, ATILE)
            probs = jnp.concatenate(
                [
                    jnp.where(
                        marks[j : j + 1, :] > 0.5,
                        ex[j * BLOCK : (j + 1) * BLOCK],
                        low[j * BLOCK : (j + 1) * BLOCK],
                    )
                    for j in range(ATILE // BLOCK)
                ],
                axis=0,
            ).astype(BF)
            p_ref[slot, rows, :] = probs
            acc_ref[...] += tn(probs, v_one)
            return 0

        lax.fori_loop(0, qkv_ref.shape[0] // ATILE, step, 0)
        keep(h).start()

        def last(i, _):
            rows = ds(i, TILE)
            both = acc_ref[rows, :]
            den = pltpu.roll(both, HEAD_DIM, 1)
            out_cols = ds(p, 128)
            att = (both / den).astype(BF)
            att_ref[rows, out_cols] = jnp.where(mine, att, att_ref[rows, out_cols])
            den_ref[rows, out_cols] = jnp.where(mine, den, den_ref[rows, out_cols])
            return 0

        lax.fori_loop(0, qkv_ref.shape[0] // TILE, last, 0)
        return 0

    lax.fori_loop(0, heads, head, 0)
    keep(heads - 2).wait()
    keep(heads - 1).wait()


def mix_tiles(x_ref, mine_ref, other_ref, w_ref, b_ref, g_ref, s_ref, mixed_ref, h_ref):
    f = lax.axis_index("feat")
    half = mine_ref.shape[1]

    def step(i, _):
        rows = ds(i, TILE)
        mixed = (
            x_ref[rows, :].astype(F32)
            + nn(mine_ref[rows, :], w_ref[ds(f, half), :])
            + nn(other_ref[rows, :], w_ref[ds(1 - f, half), :])
            + b_ref[...].astype(F32)
        )
        mixed_ref[rows, :] = mixed
        normed, _inv = norm(mixed)
        h_ref[rows, :] = (normed * g_ref[...].astype(F32) + s_ref[...].astype(F32)).astype(BF)
        return 0

    lax.fori_loop(0, x_ref.shape[0] // TILE, step, 0)


def ff_forward(h_ref, up_ref, down_ref, bias, act_ref, slope_ref, hid_ref, send):
    tiles = h_ref.shape[0] // TILE

    def step(i, _):
        tile = lax.rem(i + tiles // 2, tiles)
        rows = ds(tile, TILE)
        v = nn(h_ref[rows, :], up_ref[...]) + bias
        vv = v * v
        th = jnp.tanh(GELU_A * v * (1.0 + GELU_B * vv))
        half = 0.5 + 0.5 * th
        act = (v * half).astype(BF)
        slope_ref[rows, :] = half + (0.5 * GELU_A) * v * (1.0 - th * th) * (1.0 + (3.0 * GELU_B) * vv)
        act_ref[rows, :] = act
        hid_ref[rows, :] = nn(act, down_ref[...]).astype(BF)
        send(i, tile)
        return 0

    lax.fori_loop(0, tiles, step, 0)


def ff_backward(og_ref, up_ref, down_ref, slope_ref, gp_ref, gh_ref, db_ref, send):
    tiles = og_ref.shape[0] // TILE
    db_ref[...] = jnp.zeros_like(db_ref)

    def step(i, _):
        tile = lax.rem(i + tiles // 2, tiles)
        rows = ds(tile, TILE)
        gp = (nt(og_ref[rows, :], down_ref[...]) * slope_ref[rows, :]).astype(BF)
        gp_ref[rows, :] = gp
        db_ref[...] += jnp.sum(gp.astype(F32), axis=0, keepdims=True)
        gh_ref[rows, :] = nt(gp, up_ref[...]).astype(BF)
        send(i, tile)
        return 0

    lax.fori_loop(0, tiles, step, 0)


def put_chunks(out_ref, first, value, net):
    rows = out_ref.shape[1]
    for i in range(value.shape[0] // rows):
        out_ref[net.place(first + i)] = value[i * rows : (i + 1) * rows].astype(BF)


def ff_weight(net, lhs_ref, rhs_ref, outs):
    wide = lhs_ref.shape[1] // 2
    per = wide // outs[0].shape[1]

    def step(i, _):
        value = tn(lhs_ref[:, ds(i, wide)], rhs_ref[...])
        for j, out in enumerate(outs):
            put_chunks(out, i * per, value[:, j * out.shape[2] : (j + 1) * out.shape[2]], net)
        return 0

    lax.fori_loop(0, 2, step, 0)


def out_back(
    n, gh_ref, gho_ref, mixed_ref, og_ref, hid_ref, hido_ref, bd_ref, g_ref, w_ref, mine_ref, other_ref,
    gm_ref, gatt_ref, dw_ref, y_ref, vec_ref, gb_ref,
):
    f = lax.axis_index("feat")
    half = mine_ref.shape[1]
    tiles = mixed_ref.shape[0] // TILE
    own = tiles // 2
    gain = g_ref[...].astype(F32)
    vec_ref[...] = jnp.zeros_like(vec_ref)

    def step(i, _):
        rows = ds(i, TILE)
        mixed = mixed_ref[rows, :]
        og = og_ref[rows, :].astype(F32)
        normed, inv = norm(mixed)
        g = gh_ref[rows, :].astype(F32) + gho_ref[rows, :].astype(F32)
        gm = og + norm_back(g, normed, inv, gain)
        gb = gm.astype(BF)
        gb_ref[rows, :] = gb
        gatt_ref[rows, :] = nt(gb, w_ref[ds(f, half), :])

        @pl.when(i < own)
        def _():
            gm_ref[rows, :] = gm
            y_ref[rows, :] = (
                mixed + hid_ref[rows, :].astype(F32) + hido_ref[rows, :].astype(F32) + bd_ref[...].astype(F32)
            ).astype(BF)
            for j, term in enumerate((g * normed, g, gb.astype(F32), og)):
                vec_ref[j + 2 : j + 3, :] += jnp.sum(term, axis=0, keepdims=True)

        return 0

    lax.fori_loop(0, tiles, step, 0)
    gb_own = gb_ref[:, ds(f, half)]
    net = Net(n)
    per = half // dw_ref.shape[1]
    put_chunks(dw_ref, f * per, tn(mine_ref[...], gb_own), net)
    put_chunks(dw_ref, (1 - f) * per, tn(other_ref[...], gb_own), net)


def mid_body(
    n, x_ref, att_ref, wout_ref, p_ref, og_own_ref, up_all, down_all,
    gm_ref, gatt_ref, dout_ref, y_ref, vec_ref, dup_out, ddown_ref, dbup_ref,
    far, og, mixed, h, act, gp, hid, gh, hid_got, gh_got, gb, ddown, ddown_got, slope, up_ref, down_ref, dup_ref, send, recv, down_send, down_recv, local,
):
    net = Net(n)
    down = Scatter(net, ddown, [ddown_got, ddown_ref, None, None, None], down_send, down_recv)
    bout_ref, g_ref, s_ref, bdown_ref = [p_ref.at[i : i + 1] for i in (BOUT, GAIN2, BIAS2, BDOWN)]
    bup = jnp.concatenate([p_ref[i : i + 1, :] for i in range(BUP, p_ref.shape[0])], axis=1)
    rows = og_own_ref.shape[0]
    tiles = h.shape[0] // TILE
    other = {"feat": 1 - lax.axis_index("feat")}

    def copy(k, src, dst):
        return pltpu.make_async_remote_copy(
            src_ref=src, dst_ref=dst, send_sem=send.at[k], recv_sem=recv.at[k], device_id=other, device_id_type=MESH
        )

    loads = [pltpu.make_async_copy(a, b, local.at[i]) for i, (a, b) in enumerate(((up_all, up_ref), (down_all, down_ref)))]
    for c in loads:
        c.start()
    net.barrier()
    low, high = pl.ds(0, rows), pl.ds(rows, rows)
    atts = [copy(0, att_ref.at[low], far.at[high]), copy(1, att_ref.at[high], far.at[low])]
    og_copy = copy(2, og_own_ref, og.at[high])
    for c in atts:
        c.start()
    og_copy.start()
    og[low, :] = og_own_ref[...]
    for c in atts:
        c.wait()
    mix_tiles(x_ref, att_ref, far, wout_ref, bout_ref, g_ref, s_ref, mixed, h)

    def gh_copy(i, tile):
        return copy(3 + i, gh.at[ds(tile, TILE)], gh_got.at[ds(i, TILE)])

    def hid_copy(i, tile):
        return copy(3 + tiles + i, hid.at[ds(tile, TILE)], hid_got.at[ds(i, TILE)])

    def send_gh(i, tile):
        gh_copy(i, tile).start()

    def send_hid(i, tile):
        @pl.when(i < tiles // 2)
        def _():
            hid_copy(i, tile).start()

    for c in loads:
        c.wait()
    ff_forward(h, up_ref, down_ref, bup, act, slope, hid, send_hid)
    og_copy.wait()
    ff_weight(net, og, act, [ddown])
    down.start(0)
    ff_backward(og, up_ref, down_ref, slope, gp, gh, dbup_ref, send_gh)
    ff_weight(net, h, gp, [dup_ref.at[0], dup_ref.at[1]])
    dup_store = pltpu.make_async_copy(dup_ref, dup_out, local.at[2])
    dup_store.start()
    for i in range(tiles):
        gh_copy(i, (i + tiles // 2) % tiles).wait()
    for i in range(tiles // 2):
        hid_copy(i, i + tiles // 2).wait()
    out_back(
        n, gh, gh_got, mixed, og, hid, hid_got, bdown_ref, g_ref, wout_ref, att_ref, far,
        gm_ref, gatt_ref, dout_ref, y_ref, vec_ref, gb,
    )
    down.finish(0)
    dup_store.wait()


def heads_back(
    qkv_ref, s_ref, list_ref, count_ref, kept_ref, p_ref, sems, e_ref, mk_ref, att_ref, den_ref, gatt_ref, gqkv_ref, pq_ref, pk_ref, gn_ref, gq_ref, gpq_ref, after
):
    rows_all = qkv_ref.shape[0]
    scale = HEAD_DIM ** (-0.5)

    heads = qkv_ref.shape[1] // (3 * HEAD_DIM)

    def fetch(h):
        slot = lax.rem(h, 2)
        return pltpu.make_async_copy(kept_ref.at[h], p_ref.at[slot], sems.at[slot])

    fetch(0).start()

    def head(h, _):
        slot = lax.rem(h, 2)

        @pl.when(h + 1 < heads)
        def _():
            fetch(h + 1).start()

        p, e, lane, mine, cols = head_parts(qkv_ref, h)
        feats = pq_ref.shape[1]
        zero = jnp.zeros((), BF)
        mk_ref[...] = nn(matches(list_ref, count_ref, h), e_ref[...])
        lift_all(qkv_ref, s_ref, h, pq_ref, pk_ref)
        first_other = (1 - e) * HEAD_DIM

        def prep(i, _):
            rows = ds(i, WTILE)
            inv = 1.0 / den_ref[rows, ds(p, 128)]
            ga = jnp.where(mine, gatt_ref[rows, ds(p, 128)] * inv, 0.0)
            gd = -jnp.sum(ga * att_ref[rows, ds(p, 128)].astype(F32), axis=-1, keepdims=True)
            gn_ref[rows, :] = jnp.where(lane == first_other, gd, ga).astype(BF)
            return 0

        lax.fori_loop(0, rows_all // WTILE, prep, 0)
        gq_ref[...] = jnp.zeros_like(gq_ref)
        gpq_ref[...] = jnp.zeros_like(gpq_ref)
        signs = s_ref[p, :, ds(e, feats)]

        def lift_back(t, raw, g_phi):
            gl = g_phi * raw.astype(F32)
            gt = nt(gl.astype(BF), signs) * HEAD_DIM ** (-0.25)
            return gt - jnp.sum(gl, axis=-1, keepdims=True) * (scale * t.astype(F32))

        def put(part, rows, value):
            gqkv_ref[rows, cols(part)] = jnp.where(mine, value.astype(BF), gqkv_ref[rows, cols(part)])

        fetch(h).wait()

        def step(i, _):
            rows = ds(i, BTILE)
            k = jnp.where(mine, qkv_ref[rows, cols(1)] * BF(scale), zero)
            v_one = jnp.where(mine, qkv_ref[rows, cols(2)], jnp.ones((), BF))
            q_all = qkv_ref[:, cols(0)]
            pk = pk_ref[rows, :]
            probs = p_ref[slot, rows, :]
            da = nt(v_one, gn_ref[...])
            marks = local_marks(mk_ref, i, BTILE)
            dl, gs = [], []
            for j in range(BTILE // BLOCK):
                part = slice(j * BLOCK, (j + 1) * BLOCK)
                on = marks[j : j + 1, :] > 0.5
                daj = da[part]
                dl.append(jnp.where(on, 0.0, daj))
                gs.append(jnp.where(on, daj * probs[part].astype(F32), 0.0))
            dl = jnp.concatenate(dl, axis=0).astype(BF)
            gs = jnp.concatenate(gs, axis=0).astype(BF)
            put(2, rows, nn(probs, gn_ref[...]))
            g_phi_k = nn(dl, pq_ref[...])
            gk = nn(gs, q_all) * scale + lift_back(qkv_ref[rows, cols(1)], pk, g_phi_k)
            put(1, rows, gk)
            gpq_ref[...] += tn(dl, pk)
            gq_ref[...] += tn(gs, k)
            return 0

        lax.fori_loop(0, rows_all // BTILE, step, 0)

        def last(i, _):
            rows = ds(i, WTILE)
            gq = gq_ref[rows, :] + lift_back(qkv_ref[rows, cols(0)], pq_ref[rows, :], gpq_ref[rows, :])
            put(0, rows, gq)
            return 0

        lax.fori_loop(0, rows_all // WTILE, last, 0)
        for k, then in after.items():
            pl.when(h == k)(then)
        return 0

    lax.fori_loop(0, qkv_ref.shape[1] // (3 * HEAD_DIM), head, 0)


def back_body(
    n, qkv_ref, s_ref, list_ref, count_ref, kept_ref, att_ref, den_ref, gatt_ref, h_all, w_all, x_all, p_ref, gm_all, up_ref, down_ref, out_ref,
    vec_ref, bup_ref, dx_ref, oup_ref, odown_ref, oout_ref, oqkv_ref, orows_ref, obqkv_ref, obup_ref, *scratch,
):
    net = Net(n)
    bufs, tail = (None, down_ref) + scratch[:33], scratch[33:]
    kept_buf, keep_sems, h_ref, w_ref, x_ref, gm_ref, local, e_ref, mk_ref, pq, pk, gn, gq, gpq, gqkv, gw, gh_send, gh_got, sout, rout, sqkv, rqkv, vrows, vbqkv, vbup, send, recv = tail
    f = net.f
    other = {"feat": 1 - f}
    sources = (None, up_ref.at[0], out_ref, gw.at[0], gw.at[1], gw.at[2], up_ref.at[1])
    lanes_of = (0, 1, 2, 3, 4, 5, 10)
    down, up_low, out, *pairs, up_high = [
        Scatter(net, src, bufs[5 * i : 5 * i + 5], send.at[k], recv.at[k])
        for i, (src, k) in enumerate(zip(sources, lanes_of))
    ]
    vectors = [Vector(net, ref, send.at[6 + i], recv.at[6 + i]) for i, ref in enumerate((vrows, vbqkv, vbup))]
    last = net.slots() - 1
    half = sout.shape[1]
    rows = x_ref.shape[0]
    width = x_ref.shape[1]
    own = width // 2
    lanes = orows_ref.shape[1]

    def whole(ref):
        def put(total):
            ref[...] = total

        return put

    def halves(ref):
        def put(total):
            ref[0], ref[1] = total[:half], total[half:]

        return put

    def swap(i, src, dst):
        return pltpu.make_async_remote_copy(
            src_ref=src, dst_ref=dst, send_sem=send.at[i, last], recv_sem=recv.at[i, last],
            device_id=other, device_id_type=MESH,
        )

    def move(part, phase):
        part.finish(phase)
        part.start(phase + 1)

    def weight(p):
        g = jnp.concatenate([gqkv[:, i * own + p * 128 : i * own + (p + 1) * 128] for i in range(3)], axis=1)
        per = own // gw.shape[2]
        for i in range(2):
            put_chunks(gw.at[p], i * per, tn(h_ref[:, i * own : (i + 1) * own], g), net)
        pairs[p].start(0)

    loads = [
        pltpu.make_async_copy(a, b, local.at[i])
        for i, (a, b) in enumerate(((h_all, h_ref), (x_all, x_ref), (gm_all, gm_ref)))
    ] + [
        pltpu.make_async_copy(w_all.at[:, ds(2 * i + f, own)], w_ref.at[:, pl.ds(i * own, own)], local.at[3 + i])
        for i in range(3)
    ]
    for c in loads:
        c.start()
    fill_spread(e_ref)
    net.barrier()
    down.start(1)
    up_low.start(0)
    up_high.start(0)
    out.start(0)

    def after1():
        loads[0].wait()
        weight(0)

    def after2():
        move(down, 1)
        move(up_low, 0)

    def after3():
        move(up_high, 0)
        move(up_low, 1)
        move(out, 0)
        move(pairs[0], 0)
        weight(1)

    def after4():
        move(up_high, 1)
        move(out, 1)
        move(pairs[0], 1)
        move(pairs[1], 0)
        down.finish(2, whole(odown_ref))

    heads_back(
        qkv_ref, s_ref, list_ref, count_ref, kept_ref, kept_buf, keep_sems, e_ref, mk_ref, att_ref, den_ref, gatt_ref, gqkv, pq, pk, gn, gq, gpq,
        {1: after1, 2: after2, 3: after3, 4: after4},
    )
    weight(2)
    for c in loads[1:]:
        c.wait()
    tiles = rows // TILE

    def far(i, total):
        g = gqkv[ds(tiles + i, TILE), :]
        gh_send[ds(i, TILE), :] = nt(g, w_ref[...]).astype(BF)
        return total + jnp.sum(g.astype(F32), axis=0, keepdims=True)

    total = lax.fori_loop(0, tiles, far, jnp.zeros((1, 3 * own), F32))
    gh_swap = swap(9, gh_send, gh_got)
    gh_swap.start()
    move(pairs[1], 1)

    def sums(i, total):
        return total + jnp.sum(gqkv[ds(i, TILE), :].astype(F32), axis=0, keepdims=True)

    total = lax.fori_loop(0, tiles, sums, total)
    vbqkv[0] = jnp.zeros_like(vbqkv[0])
    for i in range(3):
        vbqkv[0, :, ds(2 * i + f, own)] = total[:, i * own : (i + 1) * own]
    vbup[0] = bup_ref[...]
    up_low.finish(2, whole(oup_ref.at[:, 0 : oup_ref.shape[1] // 2]))
    out.finish(2, halves(sout))
    out_swap = swap(2, sout.at[1 - f], rout)
    out_swap.start()
    move(pairs[2], 0)
    up_high.finish(2, whole(oup_ref.at[:, oup_ref.shape[1] // 2 :]))
    gh_swap.wait()
    gain = p_ref[GAIN1 : GAIN1 + 1, :]
    vrows[0] = vec_ref[...]

    def norm1(i, _):
        r = ds(i, TILE)
        normed, inv = norm(x_ref[r, :].astype(F32))
        g = nt(gqkv[r, :], w_ref[...]) + gh_got[r, :].astype(F32)
        dx_ref[r, :] = gm_ref[r, :] + norm_back(g, normed, inv, gain)
        vrows[0, 0:1, :] += jnp.sum(g * normed, axis=0, keepdims=True)
        vrows[0, 1:2, :] += jnp.sum(g, axis=0, keepdims=True)
        return 0

    lax.fori_loop(0, tiles, norm1, 0)
    for v in vectors:
        v.start(0)
    move(pairs[2], 1)
    for p in (0, 1):
        pairs[p].finish(2, halves(sqkv.at[p]))
    for v in vectors:
        v.finish(0)
        v.start(1)
    swaps = [swap(3 + p, sqkv.at[p, 1 - f], rqkv.at[p]) for p in range(3)]
    swaps[0].start()
    swaps[1].start()
    for v in vectors:
        v.finish(1)
        v.start(2)
    pairs[2].finish(2, halves(sqkv.at[2]))
    swaps[2].start()
    vecs, bqkv, bup = [v.finish(2) for v in vectors]
    vectors[0].start(3)
    vectors[1].start(3)
    where = 2 * net.s + f

    def cut(value, per, index, size):
        return pltpu.roll(value, lax.rem(size - index * per, size), 1)[:, :lanes]

    obup_ref[...] = cut(bup, bup.shape[1] // n, net.s, bup.shape[1])
    out_swap.wait()
    oout_ref[:, ds(f, own)] = sout[f]
    oout_ref[:, ds(1 - f, own)] = rout[...]

    def cols(i, p, side):
        return pl.ds(pl.multiple_of(i * width + side * own + p * 128, 128), 128)

    for p in range(3):
        swaps[p].wait()
        for i in range(3):
            part = slice(i * 128, (i + 1) * 128)
            oqkv_ref[:, cols(i, p, f)] = sqkv[p, f, :, part]
            oqkv_ref[:, cols(i, p, 1 - f)] = rqkv[p, :, part]
    vecs = vectors[0].finish(3)
    bqkv = vectors[1].finish(3)
    orows_ref[...] = cut(vecs, width // (2 * n), where, width)
    obqkv_ref[...] = cut(bqkv, bqkv.shape[1] // (2 * n), where, bqkv.shape[1])


def emit_body(y_ref, dx_ref, up_ref, down_ref, out_ref, qkv_ref, rows_ref, bqkv_ref, bup_ref, *outs):
    oy, odx, oup, odown, oout, oqkv, obqkv, obup = outs[:8]
    oy[...] = y_ref[...]
    odx[...], oup[...], oout[...], oqkv[...] = dx_ref[...], up_ref[...], out_ref[...], qkv_ref[...]
    down = down_ref[...]
    odown[...] = down if odown.shape == down.shape else down.T
    obqkv[...] = bqkv_ref[:, : obqkv.shape[1]]
    obup[...] = bup_ref[:, : obup.shape[1]]
    for i, ref in enumerate(outs[8:]):
        ref[...] = rows_ref[i : i + 1, : ref.shape[1]]


def body(
    layer_input, ln1_gain, ln1_bias, w_qkv, b_qkv, w_out, b_out, ln2_gain, ln2_bias,
    w_up, b_up, w_down, b_down, feature_signs, match_blocks, match_count, out_grad,
):
    rows, width = layer_input.shape
    half_width = width // 2
    half_heads = HEADS // 2
    hidden = w_up.shape[1]
    f = lax.axis_index("feat")
    tokens = 2 * rows
    n = lax.axis_size("seq")
    chunk = width // n
    assert lax.axis_size("feat") == 2 and match_blocks.shape[0] == 1 and tokens == SEQLEN

    lists = match_blocks.transpose(0, 1, 3, 2)
    vectors = [ln1_gain, ln1_bias, b_out, ln2_gain, ln2_bias, b_down, b_qkv, b_up]
    lines = sum(a.shape[0] for a in vectors) // width
    feats = 2 * feature_signs.shape[2]
    phi = pltpu.VMEM((tokens, feats), BF)
    masks = [pltpu.VMEM((NB, tokens), BF), pltpu.VMEM((NB, tokens), F32)]
    sign_half = pltpu.VMEM((half_heads, HEAD_DIM, feats // 2), BF)
    two, three = pltpu.SemaphoreType.DMA((2,)), pltpu.SemaphoreType.DMA((3,))
    full, qkv_buf = pltpu.VMEM((tokens, width), BF), pltpu.VMEM((tokens, 3 * half_width), BF)
    w_buf = pltpu.VMEM((width, 3 * half_width), BF)
    params, x, h1, qkv, table, att, den, kept = call(
        front_body,
        [
            ((lines, width), F32),
            ((tokens, width), BF), ((tokens, width), BF), ((tokens, 3 * half_width), BF),
            ((half_heads // 2, 2 * HEAD_DIM, 2 * feats), BF),
            ((tokens, half_width), BF), ((tokens, half_width), F32), ((half_heads, tokens, tokens), BF),
        ],
        [layer_input, w_qkv, feature_signs, lists, match_count] + vectors,
        specs=[VMEM, ANY] + [VMEM] * (3 + len(vectors)),
        scratch=[full, full, qkv_buf, w_buf, sign_half, sign_half] + masks + [
            phi, phi, pltpu.VMEM((2, tokens, tokens), BF), pltpu.VMEM((tokens, 128), F32), two, two,
            three, two, three,
        ],
        out_specs=[VMEM, ANY, ANY, ANY, VMEM, VMEM, VMEM, ANY],
        name="front", net=3,
    )
    big, wide = pltpu.VMEM((tokens, width), BF), pltpu.VMEM((tokens, hidden), BF)
    down_bufs = scatter_bufs(n, chunk, hidden)
    down_sems = pltpu.SemaphoreType.DMA((split(n)[0] - 1,))
    pair_sems = pltpu.SemaphoreType.DMA((3 + tokens // TILE + rows // TILE,))
    gm, gatt, d_out, y, vec2, d_up, d_down, d_bup = call(
        functools.partial(mid_body, n),
        [
            ((rows, width), F32), ((tokens, half_width), F32), ((n, chunk, half_width), BF), ((rows, width), BF),
            ((8, width), F32), ((2, n, chunk, hidden // 2), BF), (down_bufs[1].shape, BF), ((1, hidden), F32),
        ],
        [
            x, att, w_out, params, out_grad, w_up, w_down,
        ],
        specs=[VMEM] * 5 + [ANY] * 2,
        out_specs=[VMEM] * 5 + [ANY] + [VMEM] * 2,
        scratch=[
            pltpu.VMEM((tokens, half_width), BF), big, pltpu.VMEM((tokens, width), F32), big, wide, wide, big, big,
            pltpu.VMEM((rows, width), BF), big, big, pltpu.VMEM((n, chunk, hidden), BF), down_bufs[0],
            pltpu.VMEM((tokens, hidden), F32), pltpu.VMEM((width, hidden), BF), pltpu.VMEM((hidden, width), BF),
            pltpu.VMEM((2, n, chunk, hidden // 2), BF), pair_sems, pair_sems, down_sems, down_sems, three,
        ],
        name="mid", net=2,
    )
    slots = sum(split(n)) + split(n)[0] - 3 + 1
    bufs = down_bufs[2:]
    for cols in (hidden // 2, half_width, half_width, half_width, half_width, hidden // 2):
        bufs += scatter_bufs(n, chunk, cols)
    half_chunk = chunk // 2
    sems = pltpu.SemaphoreType.DMA((11, slots))
    sums = call(
        functools.partial(back_body, n),
        [
            ((rows, width), F32), ((chunk, hidden), F32), ((chunk, hidden), F32), ((half_chunk, width), F32),
            ((half_chunk, 3 * width), F32), ((8, 128), F32), ((1, 128), F32), ((1, 128), F32),
        ],
        [
            qkv, table, lists, match_count, kept, att, den, gatt, h1, w_qkv, layer_input, params, gm, d_up, d_down, d_out, vec2, d_bup,
        ],
        specs=[VMEM] * 4 + [ANY] + [VMEM] * 3 + [ANY] * 3 + [VMEM, ANY] + [VMEM] * 5,
        scratch=bufs + [
            pltpu.VMEM((2, tokens, tokens), BF), two, full, w_buf, pltpu.VMEM((rows, width), BF),
            pltpu.VMEM((rows, width), F32), pltpu.SemaphoreType.DMA((6,)),
        ] + masks + [
            phi, phi, pltpu.VMEM((tokens, 128), BF), pltpu.VMEM((tokens, 128), F32), pltpu.VMEM((tokens, feats), F32),
            pltpu.VMEM((tokens, 3 * half_width), BF), pltpu.VMEM((3, n, chunk, half_width), BF),
            pltpu.VMEM((rows, width), BF), pltpu.VMEM((rows, width), BF),
            pltpu.VMEM((2, half_chunk, half_width), F32), pltpu.VMEM((half_chunk, half_width), F32),
            pltpu.VMEM((3, 2, half_chunk, half_width), F32), pltpu.VMEM((3, half_chunk, half_width), F32),
            pltpu.VMEM((4 + slots, 8, width), F32), pltpu.VMEM((4 + slots, 1, 3 * width), F32),
            pltpu.VMEM((4 + slots, 1, hidden), F32), sems, sems,
        ],
        name="back", net=1,
    )
    own = width // (2 * n)
    turn = False
    y, dx, up, down, out, full, d_b, d_bup, *vec = call(
        emit_body,
        [
            ((rows, width), BF),
            ((rows, width), F32), ((chunk, hidden), F32), ((hidden, chunk) if turn else (chunk, hidden), F32),
            ((half_chunk, width), F32), ((half_chunk, 3 * width), F32), ((1, 3 * own), F32), ((1, hidden // n), F32),
        ] + [((1, own), F32)] * 6,
        [y] + list(sums), name="emit",
    )
    vec = [v.reshape(-1) for v in vec]
    return (
        y, dx, vec[0], vec[1], full, d_b.reshape(-1), out, vec[4], vec[2], vec[3], up, d_bup.reshape(-1),
        down if turn else down.T, vec[5],
    )


def solution(mesh):
    both = ("seq", "feat")
    return jax.shard_map(
        body,
        mesh=mesh,
        in_specs=(
            P(both, None), P(), P(), P(), P(), P(), P(), P(), P(), P(None, "feat"), P("feat"), P("feat", None), P(),
            P(None, None, "feat"), P("seq", None, None, None), P("seq", None, None), P(both, None),
        ),
        out_specs=(
            P(both, None), P(both, None), P(both), P(both), P(both, None), P(both), P(both, None), P(both), P(both),
            P(both), P("seq", "feat"), P(("feat", "seq")), P("feat", "seq"), P(both),
        ),
        check_vma=False,
    )
```
